32 devices in a mesh: fish: 4 (over y, core), curve: 8 (over z, x).
Axes of the slice: x: 2, y: 2, z: 4, core: 2. Of those that a mesh axis runs over, the one named last changes fastest.
Arguments:
- right_side: float32 [128, 128, 128], P('curve', 'fish'), may hold values from -36 to 36
- block_inverse: float32 [512, 512], replicated, may hold values from -1 to 1
- midline: float32 [7, 16, 256], P(None, 'fish'), may hold values from -2 to 10, as said below
- entry_fish: int32 [2048], P(('fish', 'curve')), may hold values from 0 to 3
- entry_seg: int32 [2048], P(('fish', 'curve')), may hold values from 0 to 240
- entry_dest: int32 [2048, 1], P(('fish', 'curve')), may hold values from 0 to 7; in each aligned block of 64 rows (0 to 63, 64 to 127, ...) at most 16 rows name the same one
- entry_block: int32 [2048], P(('fish', 'curve')), may hold values from 0 to 127
Outputs:
- pressure: float32 [128, 128, 128], P('curve', 'fish')
- residual: float32 [128, 128, 128], P('curve', 'fish')
- obstacle: bfloat16 [4, 128, 128, 128], P(None, 'curve', 'fish')
The draws below stay inside these ranges and needn't reach their ends.
Inputs may be any that keep to these rules, and one draw needn't show every extreme that they name: `midline`: positions lie within a few cells of the block that an entry names; half-widths are positive. `entry_dest`: within the 64 rows of one device no value appears more than 16 times, and in some devices' rows one value appears exactly 16 times.
All inputs are finite; a program needn't handle non-finite values.
Results may differ from the reference program's by a relative error of at most 0.004.
Values may be sent and summed in bfloat16 or wider, within the bound.
A program may use at most 64 MiB of HBM per device.

```python
import math
import jax
import jax.numpy as jnp
import numpy as np
from jax import lax

BE = 8
BLK = 512
BX_DEV = 2
BZ_DEV = 4
NY = 128
NPTS = 256
SEG = 16
FISH_GRP = 4
ENT_DEV = 64
ITERS = 2
CAP = 16
CZ = 32
NB = 128
X = 128
Z = 128
FISHES = 16
ENTRIES = 2048
N_FISH = 4
N_CURVE = 8


def draw_right_side(key, part):
    across = jnp.arange(X, dtype=jnp.float32) / X - 0.5
    depth = jnp.arange(Z, dtype=jnp.float32) / Z - 0.5
    scaling = (10.0 ** across)[:, None, None] * (3.0 ** depth)[None, :, None]
    base = jnp.clip(jax.random.normal(key, (X, Z, NY), jnp.float32), -6.0, 6.0)
    return base * scaling


def draw_block_inverse(key, part):
    subkeys = jax.random.split(jax.random.fold_in(key, 5), 2)
    spread = jax.random.uniform(subkeys[0], (BLK, BLK), jnp.float32, -1.0, 1.0) * (0.6 / math.sqrt(BLK))
    gains = jax.random.uniform(subkeys[1], (BLK,), jnp.float32, 0.8, 1.25)
    identity = jnp.eye(BLK, dtype=jnp.float32)
    return (identity * gains[None, :] + spread * (1.0 - identity)) / 7.0


def draw_midline(key, part):
    subkeys = jax.random.split(jax.random.fold_in(key, 7), 3)
    placed = jax.random.uniform(subkeys[0], (3, FISHES, NPTS), jnp.float32, -2.0, BE + 2.0)
    velocity = jnp.clip(jax.random.normal(subkeys[1], (3, FISHES, NPTS), jnp.float32), -2.0, 2.0)
    halfwidth = BE * jnp.exp(jax.random.uniform(subkeys[2], (1, FISHES, NPTS), jnp.float32, math.log(0.12), math.log(0.5)))
    return jnp.concatenate([placed, velocity, halfwidth], axis=0)


def touch_ends(drawn, rng, least, high):
    longest = drawn.shape.index(max(drawn.shape))
    spots = []
    for shift in (0, 1):
        where = [jax.random.randint(jax.random.fold_in(rng, axis), (), 0, length) for axis, length in enumerate(drawn.shape)]
        where[longest] = (where[longest] + shift) % drawn.shape[longest]
        spots.append(tuple(where))
    return drawn.at[spots[0]].set(least).at[spots[1]].set(high)


def shared_out(key, own, number, rows, amount, top, limit, skew):
    ranking = jax.random.permutation(key, amount)
    crowded, usual = load_shares(amount, rows * top, limit, skew, True), load_shares(amount, rows * top, limit, skew, False)
    places = jnp.arange(amount)

    def named(sizes, rotation):
        used = int((sizes > 0).sum())
        fixed = max(1, used // 4)
        passed = fixed + (places - fixed + rotation * (used - fixed)) % max(1, amount - fixed)
        return jnp.zeros((amount,), jnp.int32).at[ranking[jnp.where(places < fixed, places, passed)]].set(jnp.asarray(sizes, jnp.int32))

    sizes = jnp.where(number % 4 == 0, named(crowded, number // 4), named(usual, number - number // 4 - 1))
    mixed = jax.random.permutation(jax.random.fold_in(own, 3), amount)
    giver, sink = mixed[0:amount // 2 * 2:2], mixed[1:amount // 2 * 2:2]
    room = jnp.minimum(sizes[giver] - 1, limit - sizes[sink]) // 2
    room = jnp.where((giver == ranking[0]) | (sink == ranking[0]) | (sizes[sink] == 0), 0, jnp.maximum(room, 0))
    passed = jax.random.randint(jax.random.fold_in(own, 4), (amount // 2,), 0, 1 << 20) % (room + 1)
    sizes = sizes.at[giver].add(-passed).at[sink].add(passed)
    labels = jnp.searchsorted(jnp.cumsum(sizes), jnp.arange(rows * top), side="right").astype(jnp.int32)
    grid = labels.reshape(top, rows).T
    grid = grid[jax.random.permutation(jax.random.fold_in(own, 1), rows)]
    rotation = jax.random.randint(jax.random.fold_in(own, 2), (rows, 1), 0, top)
    return jnp.take_along_axis(grid, (jnp.arange(top)[None, :] + rotation) % top, axis=1)


def load_shares(number_of, total, limit, lean, full):
    portions = [(1 << 20) // math.isqrt(grade ** lean) + 1 for grade in range(1, number_of + 1)]
    largest = limit if full else min(limit, max(-(-total // number_of), total * portions[0] // sum(portions)))
    least = 1 if total - largest >= number_of - 1 else 0
    given, spare = [largest] + [least] * (number_of - 1), total - largest - least * (number_of - 1)
    while spare > 0:
        movable = [i for i in range(1, number_of) if given[i] < largest] or [i for i in range(1, number_of) if given[i] < limit]
        whole, left = sum([portions[i] for i in movable]), spare
        for i in movable:
            addition = min(limit - given[i], max(1, left * portions[i] // whole), spare)
            given[i] = given[i] + addition
            spare = spare - addition
    return np.array(given)


def setup_inputs(seed: int = 0) -> dict:
    seeds = jax.random.split(jax.random.key(seed), 8)
    right_side = draw_right_side(jax.random.fold_in(seeds[7], 71), 0)
    block_inverse = draw_block_inverse(jax.random.fold_in(seeds[7], 71), 0)
    midline = draw_midline(jax.random.fold_in(seeds[7], 71), 0)
    entry_fish = touch_ends(jax.random.randint(seeds[3], (ENTRIES,), 0, FISH_GRP), jax.random.fold_in(seeds[3], 1), 0, FISH_GRP - 1).astype(jnp.int32)
    entry_seg = touch_ends(jax.random.randint(seeds[4], (ENTRIES,), 0, NPTS - SEG + 1), jax.random.fold_in(seeds[4], 1), 0, NPTS - SEG).astype(jnp.int32)
    entry_dest_keys = jax.random.split(jax.random.fold_in(seeds[5], 1), ENTRIES // ENT_DEV)
    entry_dest_turns = jax.random.permutation(jax.random.fold_in(seeds[5], 3), ENTRIES // ENT_DEV)
    entry_dest = jax.vmap(lambda own, number: shared_out(jax.random.fold_in(seeds[5], 2), own, number, ENT_DEV, N_CURVE, 1, CAP, 2))(entry_dest_keys, entry_dest_turns).reshape((ENTRIES, 1))
    entry_block = touch_ends(jax.random.randint(seeds[6], (ENTRIES,), 0, NB), jax.random.fold_in(seeds[6], 1), 0, NB - 1).astype(jnp.int32)
    return {"right_side": right_side, "block_inverse": block_inverse, "midline": midline, "entry_fish": entry_fish, "entry_seg": entry_seg, "entry_dest": entry_dest, "entry_block": entry_block}


penalty = 4.0

def cell_coords(block_edge):
    cells = jnp.arange(block_edge * block_edge * block_edge, dtype=jnp.int32)
    xcoord = (cells // (block_edge * block_edge)).astype(jnp.float32) + 0.5
    zcoord = (cells // block_edge % block_edge).astype(jnp.float32) + 0.5
    ycoord = (cells % block_edge).astype(jnp.float32) + 0.5
    return (xcoord, ycoord, zcoord)

def lookup_points(table, which_fish, first_point, seg_len):
    flat_table = table.reshape(table.shape[0], -1)
    point_index = (which_fish * table.shape[2] + first_point)[:, None] + jnp.arange(seg_len, dtype=jnp.int32)[None, :]
    return jnp.take(flat_table, point_index.astype(jnp.int32), axis=1)

def build_payload(points, block_edge):
    xcoord, ycoord, zcoord = cell_coords(block_edge)
    count = points.shape[1]
    cells = xcoord.shape[0]

    def accumulate(index, carry):
        nearest, weight_sum, vel_x, vel_y, vel_z = carry
        column = lax.dynamic_slice_in_dim(points, index, 1, 2)[:, :, 0]
        delta_x = xcoord[None, :] - column[0][:, None]
        delta_y = ycoord[None, :] - column[1][:, None]
        delta_z = zcoord[None, :] - column[2][:, None]
        dist_sq = delta_x * delta_x + delta_y * delta_y + delta_z * delta_z
        signed = jnp.sqrt(dist_sq + 0.25) - column[6][:, None]
        weights = 1.0 / (1.0 + dist_sq)
        return (jnp.minimum(nearest, signed), weight_sum + weights, vel_x + weights * column[3][:, None], vel_y + weights * column[4][:, None], vel_z + weights * column[5][:, None])
    zeros = jnp.zeros((count, cells), jnp.float32)
    start = (jnp.full((count, cells), jnp.inf, jnp.float32), zeros, zeros, zeros, zeros)
    nearest, weight_sum, vel_x, vel_y, vel_z = lax.fori_loop(0, points.shape[2], accumulate, start)
    indicator = 0.5 - 0.5 * jnp.tanh(nearest)
    channels = [indicator, indicator * (vel_x / weight_sum), indicator * (vel_y / weight_sum), indicator * (vel_z / weight_sum)]
    return jnp.stack(channels, axis=1).astype(jnp.bfloat16)

def to_blocks(values, block_edge):
    size_x, size_z, size_y = values.shape
    shaped = values.reshape(size_x // block_edge, block_edge, size_z // block_edge, block_edge, size_y // block_edge, block_edge)
    return shaped.transpose(1, 3, 5, 0, 2, 4).reshape(block_edge ** 3, -1)

def to_field(blocks, block_edge, size_x, size_z, size_y):
    shaped = blocks.reshape(block_edge, block_edge, block_edge, size_x // block_edge, size_z // block_edge, size_y // block_edge)
    return shaped.transpose(3, 0, 4, 1, 5, 2).reshape(size_x, size_z, size_y)

def reference(right_side, block_inverse, midline, entry_fish, entry_seg, entry_dest, entry_block):
    table_groups = midline.reshape(7, N_FISH, FISH_GRP, NPTS).transpose(1, 0, 2, 3)
    per_group = N_CURVE * ENT_DEV

    def group_obstacle(inputs):
        table, which_fish, first_point, target, block_id = inputs

        def one_device(pieces):
            return build_payload(lookup_points(table, pieces[0], pieces[1], SEG), BE)
        payload = lax.map(one_device, (which_fish.reshape(N_CURVE, ENT_DEV), first_point.reshape(N_CURVE, ENT_DEV)))
        payload = payload.reshape(per_group, 4 * BLK).astype(jnp.float32)
        owner_block = (target * NB + block_id).astype(jnp.int32)
        summed = jax.ops.segment_sum(payload, owner_block, num_segments=N_CURVE * NB)
        owned = summed.astype(jnp.bfloat16).reshape(N_CURVE, NB, 4, BLK).transpose(2, 0, 3, 1)
        layout = owned.reshape(4, N_CURVE, BE, BE, BE, BX_DEV, BZ_DEV, NY // BE)
        layout = layout.transpose(0, 1, 5, 2, 6, 3, 7, 4)
        return layout.reshape(4, X, CZ, NY)
    groups = lax.map(group_obstacle, (table_groups, entry_fish.reshape(N_FISH, per_group), entry_seg.reshape(N_FISH, per_group), entry_dest[:, 0].reshape(N_FISH, per_group), entry_block.reshape(N_FISH, per_group)))
    obstacle = groups.transpose(1, 2, 0, 3, 4).reshape(4, X, Z, NY)
    diagonal = 6.0 + penalty * obstacle[0].astype(jnp.float32)
    source = right_side - (obstacle[1].astype(jnp.float32) + obstacle[2].astype(jnp.float32) + obstacle[3].astype(jnp.float32))

    def precondition(values):
        product = jnp.dot(block_inverse, to_blocks(values, BE), precision=lax.Precision.HIGHEST, preferred_element_type=jnp.float32)
        return to_field(product, BE, X, Z, NY)

    def operate(values):
        padded = jnp.pad(values, 1)
        beside = padded[2:, 1:-1, 1:-1] + padded[:-2, 1:-1, 1:-1]
        beside = beside + padded[1:-1, 2:, 1:-1] + padded[1:-1, :-2, 1:-1]
        beside = beside + padded[1:-1, 1:-1, 2:] + padded[1:-1, 1:-1, :-2]
        return diagonal * values - beside
    pressure = jnp.zeros_like(source)
    residual = source
    shadow = source
    direction = source
    rho_now = None
    for iteration in range(ITERS):
        precond_dir = precondition(direction)
        image_dir = operate(precond_dir)
        if iteration == 0:
            rho_now = jnp.sum(shadow * shadow)
        shadow_image = jnp.sum(shadow * image_dir)
        alpha_step = rho_now / shadow_image
        halfway = residual - alpha_step * image_dir
        precond_half = precondition(halfway)
        image_half = operate(precond_half)
        omega_step = jnp.sum(image_half * halfway) / jnp.sum(image_half * image_half)
        pressure = pressure + alpha_step * precond_dir + omega_step * precond_half
        residual = halfway - omega_step * image_half
        if iteration + 1 < ITERS:
            rho_next = jnp.sum(shadow * halfway) - omega_step * jnp.sum(shadow * image_half)
            beta_step = rho_next / rho_now * (alpha_step / omega_step)
            direction = residual + beta_step * (direction - omega_step * image_dir)
            rho_now = rho_next
    return (pressure, residual, obstacle)
```

```python
import functools
import jax
import jax.numpy as jnp
from jax import lax
from jax.experimental import pallas as pl
from jax.experimental.pallas import tpu as pltpu
from jax.sharding import PartitionSpec as P

BE = 8
SEG = 16
PENALTY = 4.0
F32 = jnp.float32
BF16 = jnp.bfloat16
MESH = pl.DeviceIdType.MESH


def nt_dot(a, b):
    return lax.dot_general(a, b, (((1,), (1,)), ((), ())), preferred_element_type=F32)


def nn_dot(a, b):
    return lax.dot_general(a, b, (((1,), (0,)), ((), ())), preferred_element_type=F32)


def split3(x):
    hi = x.astype(BF16)
    rest = x - hi.astype(F32)
    mid = rest.astype(BF16)
    low = (rest - mid.astype(F32)).astype(BF16)
    return hi, mid, low


def swap_bits(arrays, lane):
    arrays = list(arrays)
    lanes = lane.shape[-1]
    for step in (4, 2, 1):
        clear = (lane & step) == 0
        for a in range(8):
            if a & step:
                continue
            low, high = arrays[a], arrays[a | step]
            arrays[a] = jnp.where(clear, low, pltpu.roll(high, step, axis=1))
            arrays[a | step] = jnp.where(clear, pltpu.roll(low, lanes - step, axis=1), high)
    return arrays


def rows_to_field(read_j, write, bx_n, bz_n, lane):
    parts = swap_bits([read_j(j) for j in range(BE)], lane)
    for bx in range(bx_n):
        for i in range(BE):
            plane = jnp.concatenate(
                [parts[bx * bz_n + bz][i * BE : (i + 1) * BE, :] for bz in range(bz_n)], axis=0
            )
            write(bx * BE + i, plane)


VMEM_LIMIT = 40 * 1024 * 1024


def finish(
    tot_ref, r_ref, v_ref, w_ref, u_ref, x_ref, y_ref, m_ref, n_ref, q_ref, oin_ref,
    press_ref, resid_ref, obst_ref, prow, rrow, pf, rf, sems,
):
    slab = BE * BE
    bx_n, bz_n = pf.shape[0] // BE, pf.shape[1] // BE
    lane = lax.broadcasted_iota(jnp.int32, (slab, prow.shape[1]), 1)
    give = [
        pltpu.make_async_copy(a, b, sems.at[n])
        for n, (a, b) in enumerate(((oin_ref, obst_ref), (rf, resid_ref), (pf, press_ref)))
    ]
    give[0].start()
    press, resid = coefficients(tot_ref[0:1, :])
    for rows, coefs, basis in (
        (rrow, resid, (r_ref, v_ref, w_ref, u_ref, x_ref)),
        (prow, press, (y_ref, m_ref, n_ref, q_ref)),
    ):
        total = None
        for coef, ref in zip(coefs, basis):
            term = ref[...] if coef is None else coef * ref[...]
            total = term if total is None else total + term
        rows[...] = total
    for n, (rows, field) in enumerate(((rrow, rf), (prow, pf))):

        def write(x, plane, field=field):
            field[x] = plane

        rows_to_field(
            lambda j, rows=rows: rows[pl.ds(j, slab, stride=BE), :], write, bx_n, bz_n, lane
        )
        give[1 + n].start()
    for copy in give:
        copy.wait()


def coefficients(row):
    gram = {}
    at = 0
    for a in range(5):
        for b in range(a, 5):
            gram[a, b] = gram[b, a] = row[:, at : at + 1]
            at += 1

    def inner(p, q):
        total = None
        for a, pa in p.items():
            part = None
            for b, qb in q.items():
                term = qb * gram[a, b]
                part = term if part is None else part + term
            total = pa * part if total is None else total + pa * part
        return total

    rr, rv, vv, vw, ww, rw = (gram[k] for k in ((0, 0), (0, 1), (1, 1), (1, 2), (2, 2), (0, 2)))
    alpha = rr / rv
    ts = (rv - alpha * vv) - alpha * (rw - alpha * vw)
    tt = (vv - alpha * vw) - alpha * (vw - alpha * ww)
    omega = ts / tt
    rho2 = (rr - alpha * rv) - omega * (rv - alpha * rw)
    beta = rho2 / rr * (alpha / omega)
    both, prod = alpha + omega, alpha * omega
    d0, d1, d2 = 1.0 + beta, -(both + beta * omega), prod
    sv = d0 * rv + (d1 * rw + d2 * gram[0, 3])
    alpha2 = rho2 / sv
    s = {0: jnp.ones_like(alpha), 1: -both - alpha2 * d0, 2: prod - alpha2 * d1, 3: -alpha2 * d2}
    t = {k + 1: c for k, c in s.items()}
    omega2 = inner(t, s) / inner(t, t)
    press = (
        both + alpha2 * d0 + omega2,
        alpha2 * d1 - prod + omega2 * s[1],
        alpha2 * d2 + omega2 * s[2],
        omega2 * s[3],
    )
    resid = (
        None,
        s[1] - omega2,
        s[2] - omega2 * s[1],
        s[3] - omega2 * s[2],
        -omega2 * s[3],
    )
    return press, resid


def kernel(
    nf, nc, cap, npts,
    rs_hbm, inv_hbm, mid_hbm, fish_hbm, seg_hbm, dest_hbm, block_hbm,
    tot_ref, src, v1, w1, u1, x1, y1, m1, n1, q1, obf,
    rs_ref, inv_ref, mid_ref, fish_ref, seg_ref, dest_ref, block_ref, in_sem,
    mh, ml, fh, fl, rhs, ring, meta_ref, tab, shifted, psend, precv, pt, dyz, ob, diag,
    ysend, yxl, yxh, yzl, yzh, ydiag, gsx, gsz, gxl, gxh, gzl, gzh, red,
    psend_sem, precv_sem, ysend_sem, yrecv_sem, gsend_sem, grecv_sem, rsend_sem, rrecv_sem,
):
    mf = lax.axis_index("fish")
    mc = lax.axis_index("curve")
    cells, lanes = src.shape
    slab = BE * BE
    half = slab // 2
    bx_n = rs_ref.shape[0] // BE
    bz_n = rs_ref.shape[1] // BE
    group = bx_n * bz_n
    everyone = nf * nc

    barrier = pltpu.get_barrier_semaphore()

    def greet_fish(k, _):
        pl.semaphore_signal(
            barrier, inc=1, device_id=(lax.rem(mf + k, nf), mc), device_id_type=MESH
        )
        return 0

    def greet_curve(k, _):
        pl.semaphore_signal(
            barrier, inc=1, device_id=(mf, lax.rem(mc + k, nc)), device_id_type=MESH
        )
        return 0

    lax.fori_loop(1, nc, greet_curve, 0)
    lax.fori_loop(1, nf, greet_fish, 0)

    takes = [
        pltpu.make_async_copy(a, b, in_sem.at[n])
        for n, (a, b) in enumerate(
            (
                (fish_hbm, fish_ref), (seg_hbm, seg_ref), (dest_hbm, dest_ref),
                (block_hbm, block_ref), (mid_hbm, mid_ref), (inv_hbm, inv_ref), (rs_hbm, rs_ref),
            )
        )
    ]
    for copy in takes:
        copy.start()

    lane8 = lax.broadcasted_iota(jnp.int32, (BE, lanes), 1)
    lane64 = lax.broadcasted_iota(jnp.int32, (slab, lanes), 1)
    lane32 = lax.broadcasted_iota(jnp.int32, (half, lanes), 1)
    sub8 = lax.broadcasted_iota(jnp.int32, (BE, lanes), 0)
    col = lax.broadcasted_iota(jnp.int32, (lanes, lanes), 1)
    row = lax.broadcasted_iota(jnp.int32, (lanes, lanes), 0)
    colf, rowf = col.astype(F32), row.astype(F32)

    for copy in takes[:5]:
        copy.wait()
    nyb = rs_ref.shape[2] // BE
    count = fish_ref.shape[1]
    rows, fishes, _ = mid_ref.shape
    width = tab.shape[1]
    block = block_ref[...]
    place_in = block % nyb * group + block // nyb + 1
    meta_ref[...] = jnp.full_like(meta_ref, -1.0)
    for r, column in enumerate((fish_ref[...], seg_ref[...], dest_ref[...], place_in)):
        meta_ref[r : r + 1, 0:count] = column.astype(F32)
    for f in range(fishes):
        tab[0:rows, f * npts : (f + 1) * npts] = mid_ref[:, f, :]
    tab[rows:8, :] = jnp.zeros((8 - rows, width), F32)
    table = tab[...]
    for m in range(SEG):
        turned = table if m == 0 else pltpu.roll(table, width - m, axis=1)
        shifted[m * 8 : m * 8 + 8, :] = turned
    meta = meta_ref[...]
    owner = lax.broadcasted_iota(jnp.int32, (nc, lanes), 0).astype(F32)
    mine = owner == meta[2:3, :]
    earlier = jnp.where(row < col, 1.0, 0.0).astype(BF16)
    rank = nn_dot(jnp.where(mine, 1.0, 0.0).astype(BF16), earlier)
    slot = jnp.sum(jnp.where(mine, owner * cap + rank + 1.0, 0.0), axis=0, keepdims=True) - 1.0
    hot = jnp.where(rowf == slot, 1.0, 0.0).astype(BF16)
    picked = nt_dot(hot, meta.astype(BF16))
    index = picked[:, 0:1] * npts + picked[:, 1:2]
    place = picked[:, 3:4] - 1.0
    point_hot = jnp.where(
        lax.broadcasted_iota(jnp.int32, (lanes, width), 1).astype(F32) == index, 1.0, 0.0
    ).astype(BF16)
    hi, mid, low = split3(shifted[...])
    points = (nt_dot(point_hot, hi) + nt_dot(point_hot, mid)) + nt_dot(point_hot, low)
    points = jnp.where(col == 7, place, points)
    for c in range(nc):
        psend[c] = points[c * cap : (c + 1) * cap, :]

    pl.semaphore_wait(barrier, nf - 1 + nc - 1)

    def hand(k, to, slot):
        return pltpu.make_async_remote_copy(
            src_ref=psend.at[to],
            dst_ref=precv.at[slot],
            send_sem=psend_sem.at[k],
            recv_sem=precv_sem.at[k],
            device_id=(mf, to),
            device_id_type=MESH,
        )

    def hand_start(k, _):
        hand(k, lax.rem(mc + k, nc), mc).start()
        return 0

    def hand_finish(k, _):
        origin = lax.rem(mc + nc - k, nc)
        hand(k, origin, origin).wait()
        return 0

    lax.fori_loop(1, nc, hand_start, 0)
    precv[mc] = psend[mc]

    takes[5].wait()
    whole = inv_ref[...]
    top = jnp.max(jnp.max(jnp.abs(whole), axis=0, keepdims=True), axis=1, keepdims=True)
    scale = 1.0 / (slab * top)
    inner_k = slab - 2 * BE
    pieces = [(0, slab), (cells - slab, cells)]
    pieces += [(i * slab, i * slab + BE) for i in range(1, BE - 1)]
    pieces += [((i + 1) * slab - BE, (i + 1) * slab) for i in range(1, BE - 1)]
    pieces += [(i * slab + BE, (i + 1) * slab - BE) for i in range(1, BE - 1)]
    faces = 2 * slab + 2 * BE * (BE - 2)
    arranged = jnp.concatenate([inv_ref[a:b, :] for a, b in pieces], axis=0) * scale
    hi = arranged.astype(BF16)
    mh[...] = hi
    ml[...] = (arranged - hi.astype(F32)).astype(BF16)
    wide = fh.shape[0]
    cell = lax.broadcasted_iota(jnp.int32, (cells, wide), 0)
    face = lax.broadcasted_iota(jnp.int32, (cells, wide), 1)
    side = (face - 2 * slab) // (BE * (BE - 2))
    deep = (face - 2 * slab) % (BE * (BE - 2))
    where_z = (deep // BE + 1) * slab + side * (slab - BE) + deep % BE
    where_x = face // slab * (cells - slab) + face % slab
    at = jnp.where(face < 2 * slab, where_x, jnp.where(face < faces, where_z, -1))
    pick = jnp.where(cell == at, 1.0, 0.0).astype(BF16)
    for full, kept in ((mh, fh), (ml, fl)):
        kept[0:faces, :] = nn_dot(full[0:faces, :], pick).astype(BF16)
        kept[faces:, :] = jnp.zeros((wide - faces, wide), BF16)

    def field_to_rows(read, out_ref):
        parts = []
        for g in range(group):
            bx, bz = g // bz_n, g % bz_n
            parts.append(read(bx, bz).reshape(slab, lanes))
        for j, rows in enumerate(swap_bits(parts, lane64)):
            out_ref[pl.ds(j, slab, stride=BE), :] = rows

    takes[6].wait()
    field_to_rows(
        lambda bx, bz: rs_ref[bx * BE : (bx + 1) * BE, bz * BE : (bz + 1) * BE, :], src
    )

    has = {"xl": mc > 0, "xh": mc < nc - 1, "zl": mf > 0, "zh": mf < nf - 1}
    absent = {k: jnp.logical_not(c) for k, c in has.items()}
    for e in range(2):
        for key, bufs in (
            ("xl", (yxl, gxl)), ("xh", (yxh, gxh)), ("zl", (yzl, gzl)), ("zh", (yzh, gzh))
        ):
            def clear(bufs=bufs, e=e):
                for buf in bufs:
                    buf[e] = jnp.zeros(buf.shape[1:], F32)

            pl.when(absent[key])(clear)
        for d, (a, b) in enumerate((("xl", "zl"), ("xh", "zl"), ("xh", "zh"), ("xl", "zh"))):
            def clear(d=d, e=e):
                ydiag[e, d] = jnp.zeros(ydiag.shape[2:], F32)

            pl.when(jnp.logical_or(absent[a], absent[b]))(clear)

    lax.fori_loop(1, nc, hand_finish, 0)

    for c in range(nc):
        pt[c * cap : (c + 1) * cap, :] = precv[c]
    pt[...] = pt[...].T
    block_hot = jnp.where(rowf == pt[7:8, :], 1.0, 0.0).astype(BF16)

    cell = lax.broadcasted_iota(jnp.int32, (slab, lanes), 0)
    zc = (cell // BE).astype(F32) + 0.5
    yc = (cell % BE).astype(F32) + 0.5
    for m in range(SEG):
        dy = yc - pt[m * 8 + 1 : m * 8 + 2, :]
        dz = zc - pt[m * 8 + 2 : m * 8 + 3, :]
        dyz[m] = (dy * dy + dz * dz) + 0.25

    def build(i, _):
        xc = i.astype(F32) + 0.5
        for h in range(2):
            lo_row = h * half
            near = ws = vx = vy = vz = None
            for m in range(SEG):
                dx = xc - pt[m * 8 : m * 8 + 1, :]
                e = dyz[m, lo_row : lo_row + half, :] + dx * dx
                signed = e * lax.rsqrt(e) - pt[m * 8 + 6 : m * 8 + 7, :]
                a = 1.0 / (e + 0.75)
                ax = a * pt[m * 8 + 3 : m * 8 + 4, :]
                ay = a * pt[m * 8 + 4 : m * 8 + 5, :]
                az = a * pt[m * 8 + 5 : m * 8 + 6, :]
                if m == 0:
                    near, ws, vx, vy, vz = signed, a, ax, ay, az
                else:
                    near = jnp.minimum(near, signed)
                    ws, vx, vy, vz = ws + a, vx + ax, vy + ay, vz + az
            ind = 0.5 - 0.5 * jnp.tanh(near)
            scale = ind / ws
            pay = jnp.concatenate([ind, vx * scale, vy * scale, vz * scale], axis=0).astype(BF16)
            summed = nt_dot(pay, block_hot).astype(BF16).astype(F32)
            base = pl.multiple_of(i * slab + lo_row, half)
            for c in range(4):
                ob[c, pl.ds(base, half), :] = summed[c * half : (c + 1) * half, :]
        return 0

    lax.fori_loop(0, BE, build, 0)
    diag[...] = 6.0 + PENALTY * ob[0]
    src[...] = src[...] - ((ob[1] + ob[2]) + ob[3])

    bz8 = lane8 % bz_n
    bx8 = (lane8 // bz_n) % bx_n
    bx64 = (lane64 // bz_n) % bx_n
    bx32 = (lane32 // bz_n) % bx_n
    bz32 = lane32 % bz_n
    tiles = BE // bz_n

    def turn(x, shift):
        shift = shift % lanes
        return x if shift == 0 else pltpu.roll(x, shift, axis=1)

    def load(value):
        vh = value.astype(BF16)
        rhs[:, :lanes] = vh
        rhs[:, lanes:] = (value - vh.astype(F32)).astype(BF16)

    def product(a, b):
        both = nn_dot(mh[a:b, :], rhs[...])
        return (both[:, :lanes] + both[:, lanes:]) + nn_dot(ml[a:b, :], rhs[:, :lanes])

    def face_low(f, i):
        if i == 0:
            return f[0:BE]
        if i == BE - 1:
            return f[slab : slab + BE]
        a = 2 * slab + (i - 1) * BE
        return f[a : a + BE]

    def face_high(f, i):
        if i == 0:
            return f[slab - BE : slab]
        if i == BE - 1:
            return f[2 * slab - BE : 2 * slab]
        a = 2 * slab + BE * (BE - 2) + (i - 1) * BE
        return f[a : a + BE]

    def pack_x(f):
        f0, f7 = f[:slab], f[slab : 2 * slab]
        low = jnp.where(bx32 == 0, f0[:half], turn(f0[half:], bz_n))
        high = jnp.where(bx32 == 0, turn(f7[:half], -bz_n), f7[half:])
        return low, high

    def pack_z(f):
        lows, highs = [], []
        for t in range(tiles):
            lowp = highp = None
            for a in range(bz_n):
                lo = turn(face_low(f, t * bz_n + a), a)
                hg = turn(face_high(f, t * bz_n + a), a - (bz_n - 1))
                lowp = lo if a == 0 else jnp.where(bz8 == a, lo, lowp)
                highp = hg if a == 0 else jnp.where(bz8 == a, hg, highp)
            lows.append(lowp)
            highs.append(highp)
        return jnp.concatenate(lows, axis=0), jnp.concatenate(highs, axis=0)

    def spread_x(got_low, got_high):
        at_low = [jnp.where(bx32 == 0, p, 0.0) for p in (got_low, turn(got_low, -bz_n))]
        at_high = [
            jnp.where(bx32 == bx_n - 1, p, 0.0) for p in (turn(got_high, bz_n), got_high)
        ]
        return at_low, at_high

    def spread_z(got_low, got_high):
        at_low, at_high = [], []
        for i in range(BE):
            t, a = i // bz_n, i % bz_n
            gl, gh = got_low[t * BE : (t + 1) * BE], got_high[t * BE : (t + 1) * BE]
            at_low.append(jnp.where(bz8 == 0, turn(gl, -a), 0.0))
            at_high.append(jnp.where(bz8 == bz_n - 1, turn(gh, bz_n - 1 - a), 0.0))
        return at_low, at_high

    def take_off(ref, xl, xh, zl, zh):
        at_low, at_high = spread_x(xl, xh)
        for h in range(2):
            a, b = h * half, cells - slab + h * half
            ref[a : a + half, :] = ref[a : a + half, :] - at_low[h]
            ref[b : b + half, :] = ref[b : b + half, :] - at_high[h]
        at_low, at_high = spread_z(zl, zh)
        for i in range(BE):
            a, b = i * slab, (i + 1) * slab - BE
            ref[a : a + BE, :] = ref[a : a + BE, :] - at_low[i]
            ref[b : b + BE, :] = ref[b : b + BE, :] - at_high[i]

    def ring_part(at, xl, xh, zl, zh):
        low, high = spread_x(xl, xh)
        zlow, zhigh = spread_z(zl, zh)
        low, high = jnp.concatenate(low, axis=0), jnp.concatenate(high, axis=0)
        outer = []
        for rows, i in ((low, 0), (high, BE - 1)):
            outer += [rows[:BE] + zlow[i], rows[BE : slab - BE], rows[slab - BE :] + zhigh[i]]
        part = jnp.concatenate(outer + zlow[1:-1] + zhigh[1:-1], axis=0)
        hi = part.astype(BF16)
        count = ring.shape[1] // 4
        ring[0:faces, at * count : (at + 1) * count] = hi
        ring[0:faces, (2 + at) * count : (3 + at) * count] = (part - hi.astype(F32)).astype(BF16)

    ring[faces:, :] = jnp.zeros((wide - faces, ring.shape[1]), BF16)

    def stencil(v_ref, out_ref):
        v0 = v_ref[0:slab, :]
        v7 = v_ref[cells - slab : cells, :]
        for i in range(BE):
            v = v_ref[i * slab : (i + 1) * slab, :]
            if i > 0:
                beside = v_ref[(i - 1) * slab : i * slab, :]
            else:
                beside = jnp.where(bx64 > 0, turn(v7, bz_n), 0.0)
            if i < BE - 1:
                beside = beside + v_ref[(i + 1) * slab : (i + 2) * slab, :]
            else:
                beside = beside + jnp.where(bx64 < bx_n - 1, turn(v0, -bz_n), 0.0)
            rows = []
            for k in range(BE):
                t = v[k * BE : (k + 1) * BE, :]
                if k > 0:
                    s = v[(k - 1) * BE : k * BE, :]
                else:
                    s = jnp.where(bz8 > 0, turn(v[slab - BE :, :], 1), 0.0)
                if k < BE - 1:
                    s = s + v[(k + 1) * BE : (k + 2) * BE, :]
                else:
                    s = s + jnp.where(bz8 < bz_n - 1, turn(v[:BE, :], -1), 0.0)
                down = pltpu.roll(t, 1, axis=0)
                edge = jnp.where(lane8 < group, 0.0, turn(down, group))
                s = s + jnp.where(sub8 == 0, edge, down)
                up = pltpu.roll(t, BE - 1, axis=0)
                edge = jnp.where(lane8 >= lanes - group, 0.0, turn(up, -group))
                s = s + jnp.where(sub8 == BE - 1, edge, up)
                rows.append(s)
            beside = beside + jnp.concatenate(rows, axis=0)
            out_ref[i * slab : (i + 1) * slab, :] = (
                diag[i * slab : (i + 1) * slab, :] * v - beside
            )

    def store(ref, f):
        for (a, b), c in zip(pieces, starts):
            if c < faces:
                ref[a:b, :] = f[c : c + b - a]

    starts = []
    for a, b in pieces:
        starts.append(starts[-1] + size if starts else 0)
        size = b - a

    def store_rest(ref, f):
        for (a, b), c in zip(pieces, starts):
            if c >= faces:
                ref[a:b, :] = f[c - faces : c - faces + b - a]

    ways = {
        "xl": (0, -1), "xh": (0, 1), "zl": (-1, 0), "zh": (1, 0),
        "xlzl": (-1, -1), "xhzl": (-1, 1), "xhzh": (1, 1), "xlzh": (1, -1),
    }
    zrows = tiles * BE
    span = half + zrows
    first_rows = {
        "xl": (0, half), "zl": (half, zrows), "xh": (span, half), "zh": (span + half, zrows),
        "xlzl": (0, span), "xhzl": (half, span), "xhzh": (span, span), "xlzh": (span + half, span),
    }
    order = ("xlzl", "xhzl", "xhzh", "xlzh", "xl", "xh", "zl", "zh")
    back = {"xl": "xh", "xh": "xl", "zl": "zh", "zh": "zl"}

    def present(key):
        return jnp.logical_and(has[key[:2]], has[key[2:]]) if len(key) == 4 else has[key]

    def opposite(key):
        return back[key[:2]] + back[key[2:]] if len(key) == 4 else back[key]

    def device(key):
        df, dc = ways[key]
        return (
            lax.min(lax.max(mf + df, 0), nf - 1),
            lax.min(lax.max(mc + dc, 0), nc - 1),
        )

    def face_copy(e, key):
        a, size = first_rows[key]
        if len(key) == 4:
            target = ydiag.at[e, order.index(opposite(key))]
        else:
            target = {"xl": yxl, "xh": yxh, "zl": yzl, "zh": yzh}[opposite(key)].at[e]
        n = order.index(key)
        return pltpu.make_async_remote_copy(
            src_ref=ysend.at[e, pl.ds(a, size)],
            dst_ref=target,
            send_sem=ysend_sem.at[e, n],
            recv_sem=yrecv_sem.at[e, n],
            device_id=device(key),
            device_id_type=MESH,
        )

    def second_copy(e, key):
        source = {"xl": gsx.at[e, 0], "xh": gsx.at[e, 1], "zl": gsz.at[e, 0], "zh": gsz.at[e, 1]}
        target = {"xl": gxl, "xh": gxh, "zl": gzl, "zh": gzh}[opposite(key)].at[e]
        n = order.index(key) - 4
        return pltpu.make_async_remote_copy(
            src_ref=source[key],
            dst_ref=target,
            send_sem=gsend_sem.at[e, n],
            recv_sem=grecv_sem.at[e, n],
            device_id=device(key),
            device_id_type=MESH,
        )

    def twice(e, p_ref, first_ref, image_ref, second_ref, out_ref, during):
        load(p_ref[...])
        f = product(0, faces)
        xl, xh = pack_x(f)
        zl, zh = pack_z(f)
        for key, value in (("xl", xl), ("zl", zl), ("xh", xh), ("zh", zh)):
            a, size = first_rows[key]
            ysend[e, a : a + size, :] = value
        ysend[e, 2 * span : 2 * span + half, :] = xl
        for key in order:
            pl.when(present(key))(face_copy(e, key).start)
        store(first_ref, f)
        store_rest(first_ref, product(faces, cells))
        stencil(first_ref, image_ref)
        load(image_ref[...])
        g = product(0, faces)
        gx, gz = pack_x(g), pack_z(g)
        for n in range(2):
            gsx[e, n] = gx[n]
            gsz[e, n] = gz[n]
        for key in order[4:]:
            pl.when(has[key])(second_copy(e, key).start)
        during()
        for key in order[4:]:
            pl.when(has[back[key]])(face_copy(e, key).wait_recv)
        take_off(image_ref, yxl[e], yxh[e], yzl[e], yzh[e])
        load(image_ref[...])
        f = product(0, faces)
        store(second_ref, f)
        store_rest(second_ref, product(faces, cells))
        stencil(second_ref, out_ref)
        for key in order[:4]:
            pl.when(present(opposite(key)))(face_copy(e, key).wait_recv)
        ll, hl, hh, lh = (ydiag.at[e, order.index(k)] for k in order[:4])
        xrow = {"xl": 0, "xh": zrows}
        def corner(ref, key):
            a, size = first_rows[opposite(key)]
            xa = first_rows[opposite(key)[:2]][0] - a if opposite(key) != "xlzh" else zrows
            za = first_rows[opposite(key)[2:]][0] - a
            return ref[xa : xa + half, :], ref[za : za + zrows, :]
        llx, llz = corner(ll, "xlzl")
        hlx, hlz = corner(hl, "xhzl")
        hhx, hhz = corner(hh, "xhzh")
        lhx, lhz = corner(lh, "xlzh")
        bxz = jnp.concatenate([bx8] * tiles, axis=0)
        ring_part(
            0, ysend[e, span : span + half, :], ysend[e, 0:half, :],
            jnp.where(bxz == 0, hlz, llz), jnp.where(bxz == 0, hhz, lhz),
        )
        zero = jnp.zeros_like(llx)
        ring_part(
            1,
            jnp.where(bz32 == 0, lhx, jnp.where(bz32 == bz_n - 1, llx, zero)),
            jnp.where(bz32 == 0, hhx, jnp.where(bz32 == bz_n - 1, hlx, zero)),
            ysend[e, span + half : 2 * span, :], ysend[e, half : span, :],
        )
        count = ring.shape[1] // 2
        both = nn_dot(fh[...], ring[...])
        full = (both[:, :count] + both[:, count:]) + nn_dot(fl[...], ring[:, :count])
        cxl, cxh = pack_x(full[:, :lanes])
        czl, czh = pack_z(full[:, lanes:])
        for key in order[4:]:
            pl.when(has[back[key]])(second_copy(e, key).wait_recv)
        take_off(
            out_ref,
            jnp.where(has["xl"], gxl[e] - cxh, 0.0),
            jnp.where(has["xh"], gxh[e] - cxl, 0.0),
            jnp.where(has["zl"], gzl[e] - czh, 0.0),
            jnp.where(has["zh"], gzh[e] - czl, 0.0),
        )

    def gram(pairs):
        total = [None] * len(pairs)
        for i in range(BE):
            read = {}
            for p in pairs:
                for ref in p:
                    if id(ref) not in read:
                        read[id(ref)] = ref[i * slab : (i + 1) * slab, :]
            for n, (a, b) in enumerate(pairs):
                part = jnp.sum((read[id(a)] * read[id(b)]).reshape(BE, BE, lanes), axis=0)
                total[n] = part if i == 0 else total[n] + part
        return [jnp.sum(t, axis=0, keepdims=True) for t in total]

    def show_obstacle():
        for c in range(4):
            def write(x, plane, c=c):
                obf[c, x] = plane.astype(BF16)

            rows_to_field(
                lambda j, c=c: ob[c, pl.ds(j, slab, stride=BE), :], write, bx_n, bz_n, lane64
            )

    early = {}
    basis = (src, v1, w1, u1, x1)
    known = [(a, b) for a in range(3) for b in range(a, 3)]

    def sum_known():
        sums = gram([(basis[a], basis[b]) for a, b in known])
        early.update(zip(known, sums))

    twice(0, src, y1, v1, m1, w1, show_obstacle)
    twice(1, w1, n1, u1, q1, x1, sum_known)
    late = [(a, b) for a in range(5) for b in range(a, 5) if b > 2]
    early.update(zip(late, gram([(basis[a], basis[b]) for a, b in late])))
    lines = [early[a, b] for a in range(5) for b in range(a, 5)]
    lines.append(jnp.zeros((1, lanes), F32))
    tile = jnp.sum(jnp.concatenate(lines, axis=0), axis=1, keepdims=True)
    number = len(lines)
    spot = lax.broadcasted_iota(jnp.int32, (number, lanes), 0) == lax.broadcasted_iota(
        jnp.int32, (number, lanes), 1
    )
    me = mf * nc + mc
    red[me] = jnp.sum(jnp.where(spot, tile, 0.0), axis=0, keepdims=True)

    def tell(k, _):
        to = lax.rem(me + k, everyone)
        pltpu.make_async_remote_copy(
            src_ref=red.at[me],
            dst_ref=red.at[me],
            send_sem=rsend_sem,
            recv_sem=rrecv_sem,
            device_id=(to // nc, lax.rem(to, nc)),
            device_id_type=MESH,
        ).start()
        return 0

    lax.fori_loop(1, everyone, tell, 0)

    for e in range(2):
        for key in order:
            pl.when(present(key))(face_copy(e, key).wait_send)
        for key in order[4:]:
            pl.when(has[key])(second_copy(e, key).wait_send)
    heard = red.at[pl.ds(0, everyone - 1)]
    pltpu.make_async_copy(heard, heard, rrecv_sem).wait()
    tot_ref[0:1, :] = jnp.sum(red[...], axis=0)
    pltpu.make_async_copy(heard, heard, rsend_sem).wait()


def local(right_side, block_inverse, midline, entry_fish, entry_seg, entry_dest, entry_block):
    nf, nc = lax.axis_size("fish"), lax.axis_size("curve")
    count = entry_fish.shape[0]
    cap = max(2, 2 * count // nc)
    cx, cz, ny = right_side.shape
    lanes = (cx // BE) * (cz // BE) * (ny // BE)
    cells = BE**3
    slab = BE * BE
    half = slab // 2
    zrows = BE // (cz // BE) * BE
    span = half + zrows
    wide = 4 * slab
    rows, fishes, npts = midline.shape
    width = fishes * npts
    vmem = pl.BlockSpec(memory_space=pltpu.VMEM)
    big = pltpu.VMEM((cells, lanes), F32)
    dma = pltpu.SemaphoreType.DMA
    anywhere = pl.BlockSpec(memory_space=pl.ANY)
    field = jax.ShapeDtypeStruct((cx, cz, ny), F32)
    fields = jax.ShapeDtypeStruct((4, cx, cz, ny), BF16)
    small = pltpu.VMEM((1, count), jnp.int32)
    solved = pl.pallas_call(
        functools.partial(kernel, nf, nc, cap, npts),
        out_shape=(pltpu.VMEM((8, lanes), F32),) + (big,) * 9 + (pltpu.VMEM((4, cx, cz, ny), BF16),),
        in_specs=[anywhere] * 7,
        out_specs=(vmem,) * 11,
        scratch_shapes=[
            pltpu.VMEM((cx, cz, ny), F32),
            pltpu.VMEM((cells, cells), F32),
            pltpu.VMEM((rows, fishes, npts), F32),
            small, small, small, small,
            dma((7,)),
            pltpu.VMEM((cells, cells), BF16),
            pltpu.VMEM((cells, cells), BF16),
            pltpu.VMEM((wide, wide), BF16),
            pltpu.VMEM((wide, wide), BF16),
            pltpu.VMEM((cells, 2 * lanes), BF16),
            pltpu.VMEM((wide, 4 * lanes), BF16),
            pltpu.VMEM((8, lanes), F32),
            pltpu.VMEM((8, width), F32),
            pltpu.VMEM((SEG * 8, width), F32),
            pltpu.VMEM((nc, cap, lanes), F32),
            pltpu.VMEM((nc, cap, lanes), F32),
            pltpu.VMEM((SEG * 8, lanes), F32),
            pltpu.VMEM((SEG, slab, lanes), F32),
            pltpu.VMEM((4, cells, lanes), F32),
            big,
            pltpu.VMEM((2, 2 * span + half, lanes), F32),
            pltpu.VMEM((2, half, lanes), F32),
            pltpu.VMEM((2, half, lanes), F32),
            pltpu.VMEM((2, zrows, lanes), F32),
            pltpu.VMEM((2, zrows, lanes), F32),
            pltpu.VMEM((2, 4, span, lanes), F32),
            pltpu.VMEM((2, 2, half, lanes), F32),
            pltpu.VMEM((2, 2, zrows, lanes), F32),
            pltpu.VMEM((2, half, lanes), F32),
            pltpu.VMEM((2, half, lanes), F32),
            pltpu.VMEM((2, zrows, lanes), F32),
            pltpu.VMEM((2, zrows, lanes), F32),
            pltpu.VMEM((nf * nc, 1, lanes), F32),
            dma((nc,)),
            dma((nc,)),
            dma((2, 8)),
            dma((2, 8)),
            dma((2, 4)),
            dma((2, 4)),
            dma,
            dma,
        ],
        compiler_params=pltpu.CompilerParams(
            collective_id=0, has_side_effects=True, vmem_limit_bytes=VMEM_LIMIT
        ),
    )(
        right_side,
        block_inverse,
        midline,
        *(e.reshape(1, count) for e in (entry_fish, entry_seg, entry_dest, entry_block)),
    )
    return pl.pallas_call(
        finish,
        out_shape=(field, field, fields),
        in_specs=[vmem] * 11,
        out_specs=(anywhere,) * 3,
        scratch_shapes=[
            big,
            big,
            pltpu.VMEM((cx, cz, ny), F32),
            pltpu.VMEM((cx, cz, ny), F32),
            dma((3,)),
        ],
        compiler_params=pltpu.CompilerParams(vmem_limit_bytes=VMEM_LIMIT),
    )(*(pltpu.with_memory_space_constraint(a, pltpu.VMEM) for a in solved))


def solution(mesh):
    return jax.shard_map(
        local,
        mesh=mesh,
        in_specs=(
            P("curve", "fish", None),
            P(),
            P(None, "fish", None),
            P(("fish", "curve")),
            P(("fish", "curve")),
            P(("fish", "curve"), None),
            P(("fish", "curve")),
        ),
        out_specs=(
            P("curve", "fish", None),
            P("curve", "fish", None),
            P(None, "curve", "fish", None),
        ),
        check_vma=False,
    )
```

```python
import functools
import jax
import jax.numpy as jnp
from jax import lax
from jax.experimental import pallas as pl
from jax.experimental.pallas import tpu as pltpu
from jax.sharding import PartitionSpec as P

BE = 8
SEG = 16
PENALTY = 4.0
F32 = jnp.float32
BF16 = jnp.bfloat16
MESH = pl.DeviceIdType.MESH


def nt_dot(a, b):
    return lax.dot_general(a, b, (((1,), (1,)), ((), ())), preferred_element_type=F32)


def nn_dot(a, b):
    return lax.dot_general(a, b, (((1,), (0,)), ((), ())), preferred_element_type=F32)


def split3(x):
    hi = x.astype(BF16)
    rest = x - hi.astype(F32)
    mid = rest.astype(BF16)
    low = (rest - mid.astype(F32)).astype(BF16)
    return hi, mid, low


def swap_bits(arrays, lane):
    arrays = list(arrays)
    lanes = lane.shape[-1]
    for step in (4, 2, 1):
        clear = (lane & step) == 0
        for a in range(8):
            if a & step:
                continue
            low, high = arrays[a], arrays[a | step]
            arrays[a] = jnp.where(clear, low, pltpu.roll(high, step, axis=1))
            arrays[a | step] = jnp.where(clear, pltpu.roll(low, lanes - step, axis=1), high)
    return arrays


def rows_to_field(read_j, write, bx_n, bz_n, lane):
    parts = swap_bits([read_j(j) for j in range(BE)], lane)
    for bx in range(bx_n):
        for i in range(BE):
            plane = jnp.concatenate(
                [parts[bx * bz_n + bz][i * BE : (i + 1) * BE, :] for bz in range(bz_n)], axis=0
            )
            write(bx * BE + i, plane)


VMEM_LIMIT = 40 * 1024 * 1024


def finish(
    coef_ref, r_ref, v_ref, w_ref, u_ref, x_ref, y_ref, m_ref, n_ref, q_ref, oin_ref,
    press_ref, resid_ref, obst_ref, pf, rf, osem, sems,
):
    give = pltpu.make_async_copy(oin_ref, obst_ref, osem)
    give.start()
    chunks = sems.shape[1]
    size = rf.shape[0] // chunks
    outs = []
    for c in range(chunks):
        part = pl.ds(c * size, size)
        for n, (out, dst, basis, first) in enumerate(
            (
                (rf, resid_ref, (r_ref, v_ref, w_ref, u_ref, x_ref), 0),
                (pf, press_ref, (y_ref, m_ref, n_ref, q_ref), 8),
            )
        ):
            total = None
            for k, ref in enumerate(basis):
                term = ref[part]
                if first or k:
                    term = coef_ref[first + k : first + k + 1, :] * term
                total = term if total is None else total + term
            out[part] = total
            copy = pltpu.make_async_copy(out.at[part], dst.at[part], sems.at[n, c])
            copy.start()
            outs.append(copy)
    for copy in outs:
        copy.wait()
    give.wait()


def entries(row, count):
    lane = lax.broadcasted_iota(jnp.int32, row.shape, 1)
    return [
        jnp.sum(jnp.where(lane == k, row, 0.0), axis=1, keepdims=True) for k in range(count)
    ]


def first_scalars(gram):
    rr, rv, vv, vw, ww, rw = (gram[k] for k in ((0, 0), (0, 1), (1, 1), (1, 2), (2, 2), (0, 2)))
    alpha = rr / rv
    ts = (rv - alpha * vv) - alpha * (rw - alpha * vw)
    tt = (vv - alpha * vw) - alpha * (vw - alpha * ww)
    omega = ts / tt
    rho2 = (rr - alpha * rv) - omega * (rv - alpha * rw)
    beta = rho2 / rr * (alpha / omega)
    both, prod = alpha + omega, alpha * omega
    d0, d1, d2 = 1.0 + beta, -(both + beta * omega), prod
    return rho2, both, prod, d0, d1, d2, d0 * rv + d1 * rw


def coefficients(gram, scalars):
    rho2, both, prod, d0, d1, d2, known = scalars
    gram = {**gram, **{(b, a): g for (a, b), g in gram.items()}}
    alpha2 = rho2 / (known + d2 * gram[0, 3])
    s1, s2, s3 = -both - alpha2 * d0, prod - alpha2 * d1, -alpha2 * d2
    ts = tt = None
    for a, sa in ((1, None), (2, s1), (3, s2), (4, s3)):
        q = (gram[a, 0] + s1 * gram[a, 1]) + (s2 * gram[a, 2] + s3 * gram[a, 3])
        z = (gram[a, 1] + s1 * gram[a, 2]) + (s2 * gram[a, 3] + s3 * gram[a, 4])
        ts = q if sa is None else ts + sa * q
        tt = z if sa is None else tt + sa * z
    omega2 = ts / tt
    resid = (omega2, s1 - omega2, s2 - omega2 * s1, s3 - omega2 * s2, -omega2 * s3)
    press = (
        both + alpha2 * d0 + omega2,
        alpha2 * d1 - prod + omega2 * s1,
        alpha2 * d2 + omega2 * s2,
        omega2 * s3,
    )
    return resid, press


def kernel(
    nf, nc, cap, npts,
    rs_hbm, inv_hbm, mid_hbm, fish_hbm, seg_hbm, dest_hbm, block_hbm,
    coef_ref, rfield, vfield, wfield, ufield, xfield, yfield, mfield, nfield, qfield, obf,
    src, v1, w1, u1, x1, y1, m1, n1, q1, rs_ref, inv_ref, mid_ref, fish_ref, seg_ref, dest_ref, block_ref, in_sem,
    mh, ml, fh, fl, rhs, ring, meta_ref, tab, shifted, psend, precv, pt, dyz, ob, diag,
    ysend, yxl, yxh, yzl, yzh, ydiag, gsx, gsz, gxl, gxh, gzl, gzh, red,
    psend_sem, precv_sem, ysend_sem, yrecv_sem, gsend_sem, grecv_sem, rsend_sem, rrecv_sem,
):
    mf = lax.axis_index("fish")
    mc = lax.axis_index("curve")
    cells, lanes = src.shape
    slab = BE * BE
    half = slab // 2
    bx_n = rs_ref.shape[0] // BE
    bz_n = rs_ref.shape[1] // BE
    group = bx_n * bz_n
    everyone = nf * nc

    barrier = pltpu.get_barrier_semaphore()

    def greet_fish(k, _):
        pl.semaphore_signal(
            barrier, inc=1, device_id=(lax.rem(mf + k, nf), mc), device_id_type=MESH
        )
        return 0

    def greet_curve(k, _):
        pl.semaphore_signal(
            barrier, inc=1, device_id=(mf, lax.rem(mc + k, nc)), device_id_type=MESH
        )
        return 0

    lax.fori_loop(1, nc, greet_curve, 0)
    lax.fori_loop(1, nf, greet_fish, 0)

    takes = [
        pltpu.make_async_copy(a, b, in_sem.at[n])
        for n, (a, b) in enumerate(
            (
                (fish_hbm, fish_ref), (seg_hbm, seg_ref), (dest_hbm, dest_ref),
                (block_hbm, block_ref), (mid_hbm, mid_ref), (inv_hbm, inv_ref), (rs_hbm, rs_ref),
            )
        )
    ]
    for copy in takes:
        copy.start()

    lane8 = lax.broadcasted_iota(jnp.int32, (BE, lanes), 1)
    lane64 = lax.broadcasted_iota(jnp.int32, (slab, lanes), 1)
    lane32 = lax.broadcasted_iota(jnp.int32, (half, lanes), 1)
    sub8 = lax.broadcasted_iota(jnp.int32, (BE, lanes), 0)
    col = lax.broadcasted_iota(jnp.int32, (lanes, lanes), 1)
    row = lax.broadcasted_iota(jnp.int32, (lanes, lanes), 0)
    colf, rowf = col.astype(F32), row.astype(F32)

    for copy in takes[:5]:
        copy.wait()
    nyb = rs_ref.shape[2] // BE
    count = fish_ref.shape[1]
    rows, fishes, _ = mid_ref.shape
    width = tab.shape[1]
    block = block_ref[...]
    place_in = block % nyb * group + block // nyb + 1
    meta_ref[...] = jnp.full_like(meta_ref, -1.0)
    for r, column in enumerate((fish_ref[...], seg_ref[...], dest_ref[...], place_in)):
        meta_ref[r : r + 1, 0:count] = column.astype(F32)
    for f in range(fishes):
        tab[0:rows, f * npts : (f + 1) * npts] = mid_ref[:, f, :]
    tab[rows:8, :] = jnp.zeros((8 - rows, width), F32)
    table = tab[...]
    for m in range(SEG):
        turned = table if m == 0 else pltpu.roll(table, width - m, axis=1)
        shifted[m * 8 : m * 8 + 8, :] = turned
    meta = meta_ref[...]
    owner = lax.broadcasted_iota(jnp.int32, (nc, lanes), 0).astype(F32)
    mine = owner == meta[2:3, :]
    earlier = jnp.where(row < col, 1.0, 0.0).astype(BF16)
    rank = nn_dot(jnp.where(mine, 1.0, 0.0).astype(BF16), earlier)
    slot = jnp.sum(jnp.where(mine, owner * cap + rank + 1.0, 0.0), axis=0, keepdims=True) - 1.0
    hot = jnp.where(rowf == slot, 1.0, 0.0).astype(BF16)
    picked = nt_dot(hot, meta.astype(BF16))
    index = picked[:, 0:1] * npts + picked[:, 1:2]
    place = picked[:, 3:4] - 1.0
    point_hot = jnp.where(
        lax.broadcasted_iota(jnp.int32, (lanes, width), 1).astype(F32) == index, 1.0, 0.0
    ).astype(BF16)
    hi, mid, low = split3(shifted[...])
    points = (nt_dot(point_hot, hi) + nt_dot(point_hot, mid)) + nt_dot(point_hot, low)
    points = jnp.where(col == 7, place, points)
    for c in range(nc):
        psend[c] = points[c * cap : (c + 1) * cap, :]

    pl.semaphore_wait(barrier, nf - 1 + nc - 1)

    def hand(k, to, slot):
        return pltpu.make_async_remote_copy(
            src_ref=psend.at[to],
            dst_ref=precv.at[slot],
            send_sem=psend_sem.at[k],
            recv_sem=precv_sem.at[k],
            device_id=(mf, to),
            device_id_type=MESH,
        )

    def hand_start(k, _):
        hand(k, lax.rem(mc + k, nc), mc).start()
        return 0

    def hand_finish(k, _):
        origin = lax.rem(mc + nc - k, nc)
        hand(k, origin, origin).wait()
        return 0

    lax.fori_loop(1, nc, hand_start, 0)
    precv[mc] = psend[mc]

    takes[5].wait()
    whole = inv_ref[...]
    top = jnp.max(jnp.max(jnp.abs(whole), axis=0, keepdims=True), axis=1, keepdims=True)
    scale = 1.0 / (slab * top)
    inner_k = slab - 2 * BE
    pieces = [(0, slab), (cells - slab, cells)]
    pieces += [(i * slab, i * slab + BE) for i in range(1, BE - 1)]
    pieces += [((i + 1) * slab - BE, (i + 1) * slab) for i in range(1, BE - 1)]
    pieces += [(i * slab + BE, (i + 1) * slab - BE) for i in range(1, BE - 1)]
    faces = 2 * slab + 2 * BE * (BE - 2)
    arranged = jnp.concatenate([inv_ref[a:b, :] for a, b in pieces], axis=0) * scale
    hi = arranged.astype(BF16)
    mh[...] = hi
    ml[...] = (arranged - hi.astype(F32)).astype(BF16)
    wide = fh.shape[0]
    cell = lax.broadcasted_iota(jnp.int32, (cells, wide), 0)
    face = lax.broadcasted_iota(jnp.int32, (cells, wide), 1)
    side = (face - 2 * slab) // (BE * (BE - 2))
    deep = (face - 2 * slab) % (BE * (BE - 2))
    where_z = (deep // BE + 1) * slab + side * (slab - BE) + deep % BE
    where_x = face // slab * (cells - slab) + face % slab
    at = jnp.where(face < 2 * slab, where_x, jnp.where(face < faces, where_z, -1))
    pick = jnp.where(cell == at, 1.0, 0.0).astype(BF16)
    for full, kept in ((mh, fh), (ml, fl)):
        kept[0:faces, :] = nn_dot(full[0:faces, :], pick).astype(BF16)
        kept[faces:, :] = jnp.zeros((wide - faces, wide), BF16)

    def field_to_rows(read, out_ref):
        parts = []
        for g in range(group):
            bx, bz = g // bz_n, g % bz_n
            parts.append(read(bx, bz).reshape(slab, lanes))
        for j, rows in enumerate(swap_bits(parts, lane64)):
            out_ref[pl.ds(j, slab, stride=BE), :] = rows

    takes[6].wait()
    field_to_rows(
        lambda bx, bz: rs_ref[bx * BE : (bx + 1) * BE, bz * BE : (bz + 1) * BE, :], src
    )

    has = {"xl": mc > 0, "xh": mc < nc - 1, "zl": mf > 0, "zh": mf < nf - 1}
    absent = {k: jnp.logical_not(c) for k, c in has.items()}
    for e in range(2):
        for key, bufs in (
            ("xl", (yxl, gxl)), ("xh", (yxh, gxh)), ("zl", (yzl, gzl)), ("zh", (yzh, gzh))
        ):
            def clear(bufs=bufs, e=e):
                for buf in bufs:
                    buf[e] = jnp.zeros(buf.shape[1:], F32)

            pl.when(absent[key])(clear)
        for d, (a, b) in enumerate((("xl", "zl"), ("xh", "zl"), ("xh", "zh"), ("xl", "zh"))):
            def clear(d=d, e=e):
                ydiag[e, d] = jnp.zeros(ydiag.shape[2:], F32)

            pl.when(jnp.logical_or(absent[a], absent[b]))(clear)

    lax.fori_loop(1, nc, hand_finish, 0)

    for c in range(nc):
        pt[c * cap : (c + 1) * cap, :] = precv[c]
    pt[...] = pt[...].T
    block_hot = jnp.where(rowf == pt[7:8, :], 1.0, 0.0).astype(BF16)

    cell = lax.broadcasted_iota(jnp.int32, (slab, lanes), 0)
    zc = (cell // BE).astype(F32) + 0.5
    yc = (cell % BE).astype(F32) + 0.5
    for m in range(SEG):
        dy = yc - pt[m * 8 + 1 : m * 8 + 2, :]
        dz = zc - pt[m * 8 + 2 : m * 8 + 3, :]
        dyz[m] = (dy * dy + dz * dz) + 0.25

    def build(i, _):
        xc = i.astype(F32) + 0.5
        for h in range(2):
            lo_row = h * half
            near = ws = vx = vy = vz = None
            for m in range(SEG):
                dx = xc - pt[m * 8 : m * 8 + 1, :]
                e = dyz[m, lo_row : lo_row + half, :] + dx * dx
                signed = e * lax.rsqrt(e) - pt[m * 8 + 6 : m * 8 + 7, :]
                a = 1.0 / (e + 0.75)
                ax = a * pt[m * 8 + 3 : m * 8 + 4, :]
                ay = a * pt[m * 8 + 4 : m * 8 + 5, :]
                az = a * pt[m * 8 + 5 : m * 8 + 6, :]
                if m == 0:
                    near, ws, vx, vy, vz = signed, a, ax, ay, az
                else:
                    near = jnp.minimum(near, signed)
                    ws, vx, vy, vz = ws + a, vx + ax, vy + ay, vz + az
            ind = 0.5 - 0.5 * jnp.tanh(near)
            scale = ind / ws
            pay = jnp.concatenate([ind, vx * scale, vy * scale, vz * scale], axis=0).astype(BF16)
            summed = nt_dot(pay, block_hot).astype(BF16).astype(F32)
            base = pl.multiple_of(i * slab + lo_row, half)
            for c in range(4):
                ob[c, pl.ds(base, half), :] = summed[c * half : (c + 1) * half, :]
        return 0

    lax.fori_loop(0, BE, build, 0)
    diag[...] = 6.0 + PENALTY * ob[0]
    src[...] = src[...] - ((ob[1] + ob[2]) + ob[3])

    bz8 = lane8 % bz_n
    bx8 = (lane8 // bz_n) % bx_n
    bx64 = (lane64 // bz_n) % bx_n
    bx32 = (lane32 // bz_n) % bx_n
    bz32 = lane32 % bz_n
    tiles = BE // bz_n

    def turn(x, shift):
        shift = shift % lanes
        return x if shift == 0 else pltpu.roll(x, shift, axis=1)

    def load(value):
        vh = value.astype(BF16)
        rhs[:, :lanes] = vh
        rhs[:, lanes:] = (value - vh.astype(F32)).astype(BF16)

    def product(a, b):
        both = nn_dot(mh[a:b, :], rhs[...])
        return (both[:, :lanes] + both[:, lanes:]) + nn_dot(ml[a:b, :], rhs[:, :lanes])

    def face_low(f, i):
        if i == 0:
            return f[0:BE]
        if i == BE - 1:
            return f[slab : slab + BE]
        a = 2 * slab + (i - 1) * BE
        return f[a : a + BE]

    def face_high(f, i):
        if i == 0:
            return f[slab - BE : slab]
        if i == BE - 1:
            return f[2 * slab - BE : 2 * slab]
        a = 2 * slab + BE * (BE - 2) + (i - 1) * BE
        return f[a : a + BE]

    def pack_x(f):
        f0, f7 = f[:slab], f[slab : 2 * slab]
        low = jnp.where(bx32 == 0, f0[:half], turn(f0[half:], bz_n))
        high = jnp.where(bx32 == 0, turn(f7[:half], -bz_n), f7[half:])
        return low, high

    def pack_z(f):
        lows, highs = [], []
        for t in range(tiles):
            lowp = highp = None
            for a in range(bz_n):
                lo = turn(face_low(f, t * bz_n + a), a)
                hg = turn(face_high(f, t * bz_n + a), a - (bz_n - 1))
                lowp = lo if a == 0 else jnp.where(bz8 == a, lo, lowp)
                highp = hg if a == 0 else jnp.where(bz8 == a, hg, highp)
            lows.append(lowp)
            highs.append(highp)
        return jnp.concatenate(lows, axis=0), jnp.concatenate(highs, axis=0)

    def spread_x(got_low, got_high):
        at_low = [jnp.where(bx32 == 0, p, 0.0) for p in (got_low, turn(got_low, -bz_n))]
        at_high = [
            jnp.where(bx32 == bx_n - 1, p, 0.0) for p in (turn(got_high, bz_n), got_high)
        ]
        return at_low, at_high

    def spread_z(got_low, got_high):
        at_low, at_high = [], []
        for i in range(BE):
            t, a = i // bz_n, i % bz_n
            gl, gh = got_low[t * BE : (t + 1) * BE], got_high[t * BE : (t + 1) * BE]
            at_low.append(jnp.where(bz8 == 0, turn(gl, -a), 0.0))
            at_high.append(jnp.where(bz8 == bz_n - 1, turn(gh, bz_n - 1 - a), 0.0))
        return at_low, at_high

    def take_off(ref, xl, xh, zl, zh):
        at_low, at_high = spread_x(xl, xh)
        for h in range(2):
            a, b = h * half, cells - slab + h * half
            ref[a : a + half, :] = ref[a : a + half, :] - at_low[h]
            ref[b : b + half, :] = ref[b : b + half, :] - at_high[h]
        at_low, at_high = spread_z(zl, zh)
        for i in range(BE):
            a, b = i * slab, (i + 1) * slab - BE
            ref[a : a + BE, :] = ref[a : a + BE, :] - at_low[i]
            ref[b : b + BE, :] = ref[b : b + BE, :] - at_high[i]

    def ring_part(at, xl, xh, zl, zh):
        low, high = spread_x(xl, xh)
        zlow, zhigh = spread_z(zl, zh)
        low, high = jnp.concatenate(low, axis=0), jnp.concatenate(high, axis=0)
        outer = []
        for rows, i in ((low, 0), (high, BE - 1)):
            outer += [rows[:BE] + zlow[i], rows[BE : slab - BE], rows[slab - BE :] + zhigh[i]]
        part = jnp.concatenate(outer + zlow[1:-1] + zhigh[1:-1], axis=0)
        hi = part.astype(BF16)
        count = ring.shape[1] // 4
        ring[0:faces, at * count : (at + 1) * count] = hi
        ring[0:faces, (2 + at) * count : (3 + at) * count] = (part - hi.astype(F32)).astype(BF16)

    ring[faces:, :] = jnp.zeros((wide - faces, ring.shape[1]), BF16)

    def stencil(v_ref, out_ref):
        v0 = v_ref[0:slab, :]
        v7 = v_ref[cells - slab : cells, :]
        for i in range(BE):
            v = v_ref[i * slab : (i + 1) * slab, :]
            if i > 0:
                beside = v_ref[(i - 1) * slab : i * slab, :]
            else:
                beside = jnp.where(bx64 > 0, turn(v7, bz_n), 0.0)
            if i < BE - 1:
                beside = beside + v_ref[(i + 1) * slab : (i + 2) * slab, :]
            else:
                beside = beside + jnp.where(bx64 < bx_n - 1, turn(v0, -bz_n), 0.0)
            rows = []
            for k in range(BE):
                t = v[k * BE : (k + 1) * BE, :]
                if k > 0:
                    s = v[(k - 1) * BE : k * BE, :]
                else:
                    s = jnp.where(bz8 > 0, turn(v[slab - BE :, :], 1), 0.0)
                if k < BE - 1:
                    s = s + v[(k + 1) * BE : (k + 2) * BE, :]
                else:
                    s = s + jnp.where(bz8 < bz_n - 1, turn(v[:BE, :], -1), 0.0)
                down = pltpu.roll(t, 1, axis=0)
                edge = jnp.where(lane8 < group, 0.0, turn(down, group))
                s = s + jnp.where(sub8 == 0, edge, down)
                up = pltpu.roll(t, BE - 1, axis=0)
                edge = jnp.where(lane8 >= lanes - group, 0.0, turn(up, -group))
                s = s + jnp.where(sub8 == BE - 1, edge, up)
                rows.append(s)
            beside = beside + jnp.concatenate(rows, axis=0)
            out_ref[i * slab : (i + 1) * slab, :] = (
                diag[i * slab : (i + 1) * slab, :] * v - beside
            )

    def store(ref, f):
        for (a, b), c in zip(pieces, starts):
            if c < faces:
                ref[a:b, :] = f[c : c + b - a]

    starts = []
    for a, b in pieces:
        starts.append(starts[-1] + size if starts else 0)
        size = b - a

    def store_rest(ref, f):
        for (a, b), c in zip(pieces, starts):
            if c >= faces:
                ref[a:b, :] = f[c - faces : c - faces + b - a]

    ways = {
        "xl": (0, -1), "xh": (0, 1), "zl": (-1, 0), "zh": (1, 0),
        "xlzl": (-1, -1), "xhzl": (-1, 1), "xhzh": (1, 1), "xlzh": (1, -1),
    }
    zrows = tiles * BE
    span = half + zrows
    first_rows = {
        "xl": (0, half), "zl": (half, zrows), "xh": (span, half), "zh": (span + half, zrows),
        "xlzl": (0, span), "xhzl": (half, span), "xhzh": (span, span), "xlzh": (span + half, span),
    }
    order = ("xlzl", "xhzl", "xhzh", "xlzh", "xl", "xh", "zl", "zh")
    back = {"xl": "xh", "xh": "xl", "zl": "zh", "zh": "zl"}

    def present(key):
        return jnp.logical_and(has[key[:2]], has[key[2:]]) if len(key) == 4 else has[key]

    def opposite(key):
        return back[key[:2]] + back[key[2:]] if len(key) == 4 else back[key]

    def device(key):
        df, dc = ways[key]
        return (
            lax.min(lax.max(mf + df, 0), nf - 1),
            lax.min(lax.max(mc + dc, 0), nc - 1),
        )

    def face_copy(e, key):
        a, size = first_rows[key]
        if len(key) == 4:
            target = ydiag.at[e, order.index(opposite(key))]
        else:
            target = {"xl": yxl, "xh": yxh, "zl": yzl, "zh": yzh}[opposite(key)].at[e]
        n = order.index(key)
        return pltpu.make_async_remote_copy(
            src_ref=ysend.at[e, pl.ds(a, size)],
            dst_ref=target,
            send_sem=ysend_sem.at[e, n],
            recv_sem=yrecv_sem.at[e, n],
            device_id=device(key),
            device_id_type=MESH,
        )

    def second_copy(e, key):
        source = {"xl": gsx.at[e, 0], "xh": gsx.at[e, 1], "zl": gsz.at[e, 0], "zh": gsz.at[e, 1]}
        target = {"xl": gxl, "xh": gxh, "zl": gzl, "zh": gzh}[opposite(key)].at[e]
        n = order.index(key) - 4
        return pltpu.make_async_remote_copy(
            src_ref=source[key],
            dst_ref=target,
            send_sem=gsend_sem.at[e, n],
            recv_sem=grecv_sem.at[e, n],
            device_id=device(key),
            device_id_type=MESH,
        )

    def twice(e, p_ref, first_ref, image_ref, second_ref, out_ref, during):
        load(p_ref[...])
        f = product(0, faces)
        xl, xh = pack_x(f)
        zl, zh = pack_z(f)
        for key, value in (("xl", xl), ("zl", zl), ("xh", xh), ("zh", zh)):
            a, size = first_rows[key]
            ysend[e, a : a + size, :] = value
        ysend[e, 2 * span : 2 * span + half, :] = xl
        for key in order:
            pl.when(present(key))(face_copy(e, key).start)
        store(first_ref, f)
        store_rest(first_ref, product(faces, cells))
        stencil(first_ref, image_ref)
        load(image_ref[...])
        g = product(0, faces)
        gx, gz = pack_x(g), pack_z(g)
        for n in range(2):
            gsx[e, n] = gx[n]
            gsz[e, n] = gz[n]
        for key in order[4:]:
            pl.when(has[key])(second_copy(e, key).start)
        during()
        for key in order[4:]:
            pl.when(has[back[key]])(face_copy(e, key).wait_recv)
        take_off(image_ref, yxl[e], yxh[e], yzl[e], yzh[e])
        load(image_ref[...])
        f = product(0, faces)
        store(second_ref, f)
        store_rest(second_ref, product(faces, cells))
        stencil(second_ref, out_ref)
        for key in order[:4]:
            pl.when(present(opposite(key)))(face_copy(e, key).wait_recv)
        ll, hl, hh, lh = (ydiag.at[e, order.index(k)] for k in order[:4])
        xrow = {"xl": 0, "xh": zrows}
        def corner(ref, key):
            a, size = first_rows[opposite(key)]
            xa = first_rows[opposite(key)[:2]][0] - a if opposite(key) != "xlzh" else zrows
            za = first_rows[opposite(key)[2:]][0] - a
            return ref[xa : xa + half, :], ref[za : za + zrows, :]
        llx, llz = corner(ll, "xlzl")
        hlx, hlz = corner(hl, "xhzl")
        hhx, hhz = corner(hh, "xhzh")
        lhx, lhz = corner(lh, "xlzh")
        bxz = jnp.concatenate([bx8] * tiles, axis=0)
        ring_part(
            0, ysend[e, span : span + half, :], ysend[e, 0:half, :],
            jnp.where(bxz == 0, hlz, llz), jnp.where(bxz == 0, hhz, lhz),
        )
        zero = jnp.zeros_like(llx)
        ring_part(
            1,
            jnp.where(bz32 == 0, lhx, jnp.where(bz32 == bz_n - 1, llx, zero)),
            jnp.where(bz32 == 0, hhx, jnp.where(bz32 == bz_n - 1, hlx, zero)),
            ysend[e, span + half : 2 * span, :], ysend[e, half : span, :],
        )
        count = ring.shape[1] // 2
        both = nn_dot(fh[...], ring[...])
        full = (both[:, :count] + both[:, count:]) + nn_dot(fl[...], ring[:, :count])
        cxl, cxh = pack_x(full[:, :lanes])
        czl, czh = pack_z(full[:, lanes:])
        for key in order[4:]:
            pl.when(has[back[key]])(second_copy(e, key).wait_recv)
        take_off(
            out_ref,
            jnp.where(has["xl"], gxl[e] - cxh, 0.0),
            jnp.where(has["xh"], gxh[e] - cxl, 0.0),
            jnp.where(has["zl"], gzl[e] - czh, 0.0),
            jnp.where(has["zh"], gzh[e] - czl, 0.0),
        )

    def gram(pairs):
        total = [None] * len(pairs)
        for i in range(BE):
            read = {}
            for p in pairs:
                for ref in p:
                    if id(ref) not in read:
                        read[id(ref)] = ref[i * slab : (i + 1) * slab, :]
            for n, (a, b) in enumerate(pairs):
                part = jnp.sum((read[id(a)] * read[id(b)]).reshape(BE, BE, lanes), axis=0)
                total[n] = part if i == 0 else total[n] + part
        return [jnp.sum(t, axis=0, keepdims=True) for t in total]

    def show_obstacle():
        for c in range(4):
            def write(x, plane, c=c):
                obf[c, x] = plane.astype(BF16)

            rows_to_field(
                lambda j, c=c: ob[c, pl.ds(j, slab, stride=BE), :], write, bx_n, bz_n, lane64
            )

    basis = (src, v1, w1, u1, x1)
    known = [(a, b) for a in range(3) for b in range(a, 3)]
    late = [(a, b) for a in range(5) for b in range(a, 5) if b > 2]
    me = mf * nc + mc

    def tell(no, pairs):
        lines = gram([(basis[a], basis[b]) for a, b in pairs])
        number = -(-len(lines) // 8) * 8
        lines += [jnp.zeros((1, lanes), F32)] * (number - len(lines))
        tile = jnp.sum(jnp.concatenate(lines, axis=0), axis=1, keepdims=True)
        spot = lax.broadcasted_iota(jnp.int32, (number, lanes), 0) == lax.broadcasted_iota(
            jnp.int32, (number, lanes), 1
        )
        red[no, me] = jnp.sum(jnp.where(spot, tile, 0.0), axis=0, keepdims=True)

        def send(df, dc):
            pltpu.make_async_remote_copy(
                src_ref=red.at[no, me],
                dst_ref=red.at[no, me],
                send_sem=rsend_sem.at[no],
                recv_sem=rrecv_sem.at[no],
                device_id=(lax.rem(mf + df, nf), lax.rem(mc + dc, nc)),
                device_id_type=MESH,
            ).start()

        if everyone <= 64:
            for df in reversed(range(nf)):
                for dc in reversed(range(nc)):
                    if df or dc:
                        send(df, dc)
        else:

            def body(k, _):
                send(k // nc, lax.rem(k, nc))
                return 0

            lax.fori_loop(1, everyone, body, 0)

    def hear(no, pairs):
        heard = red.at[no, pl.ds(0, everyone - 1)]
        pltpu.make_async_copy(heard, heard, rrecv_sem.at[no]).wait()
        row = jnp.sum(red[no], axis=0)
        return dict(zip(pairs, entries(row, len(pairs))))

    def show(ref, out):
        def write(x, plane):
            out[x] = plane

        rows_to_field(lambda j: ref[pl.ds(j, slab, stride=BE), :], write, bx_n, bz_n, lane64)

    twice(0, src, y1, v1, m1, w1, show_obstacle)
    twice(1, w1, n1, u1, q1, x1, lambda: tell(0, known))
    tell(1, late)
    sums = hear(0, known)
    scalars = first_scalars(sums)
    for ref, out in (
        (src, rfield), (v1, vfield), (w1, wfield), (u1, ufield), (x1, xfield),
        (y1, yfield), (m1, mfield), (n1, nfield), (q1, qfield),
    ):
        show(ref, out)
    for e in range(2):
        for key in order:
            pl.when(present(key))(face_copy(e, key).wait_send)
        for key in order[4:]:
            pl.when(has[key])(second_copy(e, key).wait_send)
    sums.update(hear(1, late))
    resid, press = coefficients(sums, scalars)
    for first, coefs in ((0, resid), (8, press)):
        for k, coef in enumerate(coefs):
            coef_ref[first + k : first + k + 1, :] = jnp.broadcast_to(coef, (1, lanes))
    for no in range(2):
        heard = red.at[no, pl.ds(0, everyone - 1)]
        pltpu.make_async_copy(heard, heard, rsend_sem.at[no]).wait()


def local(right_side, block_inverse, midline, entry_fish, entry_seg, entry_dest, entry_block):
    nf, nc = lax.axis_size("fish"), lax.axis_size("curve")
    count = entry_fish.shape[0]
    cap = max(2, 2 * count // nc)
    cx, cz, ny = right_side.shape
    lanes = (cx // BE) * (cz // BE) * (ny // BE)
    cells = BE**3
    slab = BE * BE
    half = slab // 2
    zrows = BE // (cz // BE) * BE
    span = half + zrows
    wide = 4 * slab
    rows, fishes, npts = midline.shape
    width = fishes * npts
    vmem = pl.BlockSpec(memory_space=pltpu.VMEM)
    big = pltpu.VMEM((cells, lanes), F32)
    dma = pltpu.SemaphoreType.DMA
    anywhere = pl.BlockSpec(memory_space=pl.ANY)
    field = jax.ShapeDtypeStruct((cx, cz, ny), F32)
    fields = jax.ShapeDtypeStruct((4, cx, cz, ny), BF16)
    small = pltpu.VMEM((1, count), jnp.int32)
    solved = pl.pallas_call(
        functools.partial(kernel, nf, nc, cap, npts),
        out_shape=(
            (pltpu.VMEM((16, lanes), F32),)
            + (pltpu.VMEM((cx, cz, ny), F32),) * 9
            + (pltpu.VMEM((4, cx, cz, ny), BF16),)
        ),
        in_specs=[anywhere] * 7,
        out_specs=(vmem,) * 11,
        scratch_shapes=[big] * 9
        + [
            pltpu.VMEM((cx, cz, ny), F32),
            pltpu.VMEM((cells, cells), F32),
            pltpu.VMEM((rows, fishes, npts), F32),
            small, small, small, small,
            dma((7,)),
            pltpu.VMEM((cells, cells), BF16),
            pltpu.VMEM((cells, cells), BF16),
            pltpu.VMEM((wide, wide), BF16),
            pltpu.VMEM((wide, wide), BF16),
            pltpu.VMEM((cells, 2 * lanes), BF16),
            pltpu.VMEM((wide, 4 * lanes), BF16),
            pltpu.VMEM((8, lanes), F32),
            pltpu.VMEM((8, width), F32),
            pltpu.VMEM((SEG * 8, width), F32),
            pltpu.VMEM((nc, cap, lanes), F32),
            pltpu.VMEM((nc, cap, lanes), F32),
            pltpu.VMEM((SEG * 8, lanes), F32),
            pltpu.VMEM((SEG, slab, lanes), F32),
            pltpu.VMEM((4, cells, lanes), F32),
            big,
            pltpu.VMEM((2, 2 * span + half, lanes), F32),
            pltpu.VMEM((2, half, lanes), F32),
            pltpu.VMEM((2, half, lanes), F32),
            pltpu.VMEM((2, zrows, lanes), F32),
            pltpu.VMEM((2, zrows, lanes), F32),
            pltpu.VMEM((2, 4, span, lanes), F32),
            pltpu.VMEM((2, 2, half, lanes), F32),
            pltpu.VMEM((2, 2, zrows, lanes), F32),
            pltpu.VMEM((2, half, lanes), F32),
            pltpu.VMEM((2, half, lanes), F32),
            pltpu.VMEM((2, zrows, lanes), F32),
            pltpu.VMEM((2, zrows, lanes), F32),
            pltpu.VMEM((2, nf * nc, 1, lanes), F32),
            dma((nc,)),
            dma((nc,)),
            dma((2, 8)),
            dma((2, 8)),
            dma((2, 4)),
            dma((2, 4)),
            dma((2,)),
            dma((2,)),
        ],
        compiler_params=pltpu.CompilerParams(
            collective_id=0, has_side_effects=True, vmem_limit_bytes=VMEM_LIMIT
        ),
    )(
        *(
            pltpu.with_memory_space_constraint(a, pltpu.HBM)
            for a in (
                right_side,
                block_inverse,
                midline,
                *(e.reshape(1, count) for e in (entry_fish, entry_seg, entry_dest, entry_block)),
            )
        )
    )
    return pl.pallas_call(
        finish,
        out_shape=(field, field, fields),
        in_specs=[vmem] * 11,
        out_specs=(anywhere,) * 3,
        scratch_shapes=[
            pltpu.VMEM((cx, cz, ny), F32),
            pltpu.VMEM((cx, cz, ny), F32),
            dma,
            dma((2, 4)),
        ],
        compiler_params=pltpu.CompilerParams(vmem_limit_bytes=VMEM_LIMIT),
    )(*(pltpu.with_memory_space_constraint(a, pltpu.VMEM) for a in solved))


def solution(mesh):
    return jax.shard_map(
        local,
        mesh=mesh,
        in_specs=(
            P("curve", "fish", None),
            P(),
            P(None, "fish", None),
            P(("fish", "curve")),
            P(("fish", "curve")),
            P(("fish", "curve"), None),
            P(("fish", "curve")),
        ),
        out_specs=(
            P("curve", "fish", None),
            P("curve", "fish", None),
            P(None, "curve", "fish", None),
        ),
        check_vma=False,
    )
```

```python
import functools
import jax
import jax.numpy as jnp
from jax import lax
from jax.experimental import pallas as pl
from jax.experimental.pallas import tpu as pltpu
from jax.sharding import PartitionSpec as P

BE = 8
SEG = 16
PENALTY = 4.0
F32 = jnp.float32
BF16 = jnp.bfloat16
MESH = pl.DeviceIdType.MESH


def nt_dot(a, b):
    return lax.dot_general(a, b, (((1,), (1,)), ((), ())), preferred_element_type=F32)


def nn_dot(a, b):
    return lax.dot_general(a, b, (((1,), (0,)), ((), ())), preferred_element_type=F32)


def split3(x):
    hi = x.astype(BF16)
    rest = x - hi.astype(F32)
    mid = rest.astype(BF16)
    low = (rest - mid.astype(F32)).astype(BF16)
    return hi, mid, low


def swap_bits(arrays, lane):
    arrays = list(arrays)
    lanes = lane.shape[-1]
    for step in (4, 2, 1):
        clear = (lane & step) == 0
        for a in range(8):
            if a & step:
                continue
            low, high = arrays[a], arrays[a | step]
            arrays[a] = jnp.where(clear, low, pltpu.roll(high, step, axis=1))
            arrays[a | step] = jnp.where(clear, pltpu.roll(low, lanes - step, axis=1), high)
    return arrays


def rows_to_field(read_j, write, bx_n, bz_n, lane):
    parts = swap_bits([read_j(j) for j in range(BE)], lane)
    for bx in range(bx_n):
        for i in range(BE):
            plane = jnp.concatenate(
                [parts[bx * bz_n + bz][i * BE : (i + 1) * BE, :] for bz in range(bz_n)], axis=0
            )
            write(bx * BE + i, plane)


VMEM_LIMIT = 40 * 1024 * 1024


def finish(
    coef_ref, r_ref, v_ref, w_ref, u_ref, x_ref, y_ref, m_ref, n_ref, q_ref, oin_ref,
    press_ref, resid_ref, obst_ref, pf, rf, osem, sems,
):
    give = pltpu.make_async_copy(oin_ref, obst_ref, osem)
    give.start()
    chunks = sems.shape[1]
    size = rf.shape[0] // chunks
    outs = []
    for c in range(chunks):
        part = pl.ds(c * size, size)
        for n, (out, dst, basis, first) in enumerate(
            (
                (rf, resid_ref, (r_ref, v_ref, w_ref, u_ref, x_ref), 0),
                (pf, press_ref, (y_ref, m_ref, n_ref, q_ref), 8),
            )
        ):
            total = None
            for k, ref in enumerate(basis):
                term = ref[part]
                if first or k:
                    term = coef_ref[first + k : first + k + 1, :] * term
                total = term if total is None else total + term
            out[part] = total
            copy = pltpu.make_async_copy(out.at[part], dst.at[part], sems.at[n, c])
            copy.start()
            outs.append(copy)
    for copy in outs:
        copy.wait()
    give.wait()


def entries(row, count):
    lane = lax.broadcasted_iota(jnp.int32, row.shape, 1)
    return [
        jnp.sum(jnp.where(lane == k, row, 0.0), axis=1, keepdims=True) for k in range(count)
    ]


def first_scalars(gram):
    rr, rv, vv, vw, ww, rw = (gram[k] for k in ((0, 0), (0, 1), (1, 1), (1, 2), (2, 2), (0, 2)))
    alpha = rr / rv
    ts = (rv - alpha * vv) - alpha * (rw - alpha * vw)
    tt = (vv - alpha * vw) - alpha * (vw - alpha * ww)
    omega = ts / tt
    rho2 = (rr - alpha * rv) - omega * (rv - alpha * rw)
    beta = rho2 / rr * (alpha / omega)
    both, prod = alpha + omega, alpha * omega
    d0, d1, d2 = 1.0 + beta, -(both + beta * omega), prod
    return rho2, both, prod, d0, d1, d2, d0 * rv + d1 * rw


def coefficients(gram, scalars):
    rho2, both, prod, d0, d1, d2, known = scalars
    gram = {**gram, **{(b, a): g for (a, b), g in gram.items()}}
    alpha2 = rho2 / (known + d2 * gram[0, 3])
    s1, s2, s3 = -both - alpha2 * d0, prod - alpha2 * d1, -alpha2 * d2
    ts = tt = None
    for a, sa in ((1, None), (2, s1), (3, s2), (4, s3)):
        q = (gram[a, 0] + s1 * gram[a, 1]) + (s2 * gram[a, 2] + s3 * gram[a, 3])
        z = (gram[a, 1] + s1 * gram[a, 2]) + (s2 * gram[a, 3] + s3 * gram[a, 4])
        ts = q if sa is None else ts + sa * q
        tt = z if sa is None else tt + sa * z
    omega2 = ts / tt
    resid = (omega2, s1 - omega2, s2 - omega2 * s1, s3 - omega2 * s2, -omega2 * s3)
    press = (
        both + alpha2 * d0 + omega2,
        alpha2 * d1 - prod + omega2 * s1,
        alpha2 * d2 + omega2 * s2,
        omega2 * s3,
    )
    return resid, press


def kernel(
    nf, nc, cap, npts,
    rs_hbm, inv_hbm, mid_hbm, fish_hbm, seg_hbm, dest_hbm, block_hbm,
    coef_ref, rfield, vfield, wfield, ufield, xfield, yfield, mfield, nfield, qfield, obf,
    src, v1, w1, u1, x1, y1, m1, n1, q1, rs_ref, inv_ref, mid_ref, ent_ref, in_sem,
    mh, ml, fh, fl, rhs, own, ring, meta_ref, tab, shifted, psend, precv, pt, dyz, paid, ob, diag,
    ysend, yx, yz, ydiag, gsx, gsz, gx, gz, red,
    psend_sem, precv_sem, ysend_sem, yrecv_sem, gsend_sem, grecv_sem, rsend_sem, rrecv_sem,
):
    mf = lax.axis_index("fish")
    mc = lax.axis_index("curve")
    cells, lanes = src.shape
    slab = BE * BE
    half = slab // 2
    bx_n = rs_ref.shape[0] // BE
    bz_n = rs_ref.shape[1] // BE
    group = bx_n * bz_n
    everyone = nf * nc

    barrier = pltpu.get_barrier_semaphore()

    def greet_fish(k, _):
        pl.semaphore_signal(
            barrier, inc=1, device_id=(lax.rem(mf + k, nf), mc), device_id_type=MESH
        )
        return 0

    def greet_curve(k, _):
        pl.semaphore_signal(
            barrier, inc=1, device_id=(mf, lax.rem(mc + k, nc)), device_id_type=MESH
        )
        return 0

    lax.fori_loop(1, nc, greet_curve, 0)
    lax.fori_loop(1, nf, greet_fish, 0)

    takes = [
        pltpu.make_async_copy(a, b, in_sem.at[max(n - 3, 0)])
        for n, (a, b) in enumerate(
            [(a, ent_ref.at[k]) for k, a in enumerate((fish_hbm, seg_hbm, dest_hbm, block_hbm))]
            + [(mid_hbm, mid_ref), (inv_hbm, inv_ref), (rs_hbm, rs_ref)]
        )
    ]
    for copy in takes:
        copy.start()

    lane8 = lax.broadcasted_iota(jnp.int32, (BE, lanes), 1)
    lane64 = lax.broadcasted_iota(jnp.int32, (slab, lanes), 1)
    lane32 = lax.broadcasted_iota(jnp.int32, (half, lanes), 1)
    sub8 = lax.broadcasted_iota(jnp.int32, (BE, lanes), 0)
    col = lax.broadcasted_iota(jnp.int32, (lanes, lanes), 1)
    row = lax.broadcasted_iota(jnp.int32, (lanes, lanes), 0)
    colf, rowf = col.astype(F32), row.astype(F32)

    pltpu.make_async_copy(ent_ref, ent_ref, in_sem.at[0]).wait()
    takes[4].wait()
    nyb = rs_ref.shape[2] // BE
    count = ent_ref.shape[2]
    rows, fishes, _ = mid_ref.shape
    width = tab.shape[1]
    block = ent_ref[3]
    place_in = block % nyb * group + block // nyb + 1
    meta_ref[...] = jnp.full_like(meta_ref, -1.0)
    for r, column in enumerate((ent_ref[0], ent_ref[1], ent_ref[2], place_in)):
        meta_ref[r : r + 1, 0:count] = column.astype(F32)
    for f in range(fishes):
        tab[0:rows, f * npts : (f + 1) * npts] = mid_ref[:, f, :]
    tab[rows:8, :] = jnp.zeros((8 - rows, width), F32)
    table = tab[...]
    for m in range(SEG):
        turned = table if m == 0 else pltpu.roll(table, width - m, axis=1)
        shifted[m * 8 : m * 8 + 8, :] = turned
    meta = meta_ref[...]
    owner = lax.broadcasted_iota(jnp.int32, (nc, lanes), 0).astype(F32)
    mine = owner == meta[2:3, :]
    earlier = jnp.where(row < col, 1.0, 0.0).astype(BF16)
    rank = nn_dot(jnp.where(mine, 1.0, 0.0).astype(BF16), earlier)
    slot = jnp.sum(jnp.where(mine, owner * cap + rank + 1.0, 0.0), axis=0, keepdims=True) - 1.0
    hot = jnp.where(rowf == slot, 1.0, 0.0).astype(BF16)
    picked = nt_dot(hot, meta.astype(BF16))
    index = picked[:, 0:1] * npts + picked[:, 1:2]
    place = picked[:, 3:4] - 1.0
    point_hot = jnp.where(
        lax.broadcasted_iota(jnp.int32, (lanes, width), 1).astype(F32) == index, 1.0, 0.0
    ).astype(BF16)
    hi, mid, low = split3(shifted[...])
    points = (nt_dot(point_hot, hi) + nt_dot(point_hot, mid)) + nt_dot(point_hot, low)
    points = jnp.where(col == 7, place, points)
    for c in range(nc):
        psend[c] = points[c * cap : (c + 1) * cap, :]

    pl.semaphore_wait(barrier, nf - 1 + nc - 1)

    def hand_start(k, _):
        to = lax.rem(mc + k, nc)
        pltpu.make_async_remote_copy(
            src_ref=psend.at[to],
            dst_ref=precv.at[mc],
            send_sem=psend_sem,
            recv_sem=precv_sem,
            device_id=(mf, to),
            device_id_type=MESH,
        ).start()
        return 0

    lax.fori_loop(1, nc, hand_start, 0)
    precv[mc] = psend[mc]

    takes[5].wait()
    whole = inv_ref[...]
    top = jnp.max(jnp.max(jnp.abs(whole), axis=0, keepdims=True), axis=1, keepdims=True)
    scale = 1.0 / (slab * top)
    inner_k = slab - 2 * BE
    pieces = [(0, slab), (cells - slab, cells)]
    pieces += [(i * slab, i * slab + BE) for i in range(1, BE - 1)]
    pieces += [((i + 1) * slab - BE, (i + 1) * slab) for i in range(1, BE - 1)]
    pieces += [(i * slab + BE, (i + 1) * slab - BE) for i in range(1, BE - 1)]
    faces = 2 * slab + 2 * BE * (BE - 2)
    arranged = jnp.concatenate([inv_ref[a:b, :] for a, b in pieces], axis=0) * scale
    hi = arranged.astype(BF16)
    mh[...] = hi
    ml[...] = (arranged - hi.astype(F32)).astype(BF16)
    wide = fh.shape[1]
    cell = lax.broadcasted_iota(jnp.int32, (cells, wide), 0)
    face = lax.broadcasted_iota(jnp.int32, (cells, wide), 1)
    side = (face - 2 * slab) // (BE * (BE - 2))
    deep = (face - 2 * slab) % (BE * (BE - 2))
    where_z = (deep // BE + 1) * slab + side * (slab - BE) + deep % BE
    where_x = face // slab * (cells - slab) + face % slab
    at = jnp.where(face < 2 * slab, where_x, jnp.where(face < faces, where_z, -1))
    pick = jnp.where(cell == at, 1.0, 0.0).astype(BF16)
    for full, kept in ((mh, fh), (ml, fl)):
        kept[...] = nn_dot(full[...], pick).astype(BF16)

    def field_to_rows(read, out_ref):
        parts = []
        for g in range(group):
            bx, bz = g // bz_n, g % bz_n
            parts.append(read(bx, bz).reshape(slab, lanes))
        for j, rows in enumerate(swap_bits(parts, lane64)):
            out_ref[pl.ds(j, slab, stride=BE), :] = rows

    takes[6].wait()
    field_to_rows(
        lambda bx, bz: rs_ref[bx * BE : (bx + 1) * BE, bz * BE : (bz + 1) * BE, :], src
    )

    has = {"xl": mc > 0, "xh": mc < nc - 1, "zl": mf > 0, "zh": mf < nf - 1}
    handed = precv.at[pl.ds(0, nc - 1)]
    pltpu.make_async_copy(handed, handed, precv_sem).wait()

    for c in range(nc):
        pt[c * cap : (c + 1) * cap, :] = precv[c]
    block_hot = jnp.where(colf == pt[:, 7:8], 1.0, 0.0).astype(BF16)
    pt[...] = pt[...].T

    cell = lax.broadcasted_iota(jnp.int32, (slab, lanes), 0)
    zc = (cell // BE).astype(F32) + 0.5
    yc = (cell % BE).astype(F32) + 0.5
    for m in range(SEG):
        dy = yc - pt[m * 8 + 1 : m * 8 + 2, :]
        dz = zc - pt[m * 8 + 2 : m * 8 + 3, :]
        dyz[m] = (dy * dy + dz * dz) + 0.25

    def build(i, _):
        xc = i.astype(F32) + 0.5
        for h in range(2):
            lo_row = h * half
            near = ws = vx = vy = vz = None
            for m in range(SEG):
                dx = xc - pt[m * 8 : m * 8 + 1, :]
                e = dyz[m, lo_row : lo_row + half, :] + dx * dx
                signed = e * lax.rsqrt(e) - pt[m * 8 + 6 : m * 8 + 7, :]
                a = pl.reciprocal(e + 0.75, approx=True)
                ax = a * pt[m * 8 + 3 : m * 8 + 4, :]
                ay = a * pt[m * 8 + 4 : m * 8 + 5, :]
                az = a * pt[m * 8 + 5 : m * 8 + 6, :]
                if m == 0:
                    near, ws, vx, vy, vz = signed, a, ax, ay, az
                else:
                    near = jnp.minimum(near, signed)
                    ws, vx, vy, vz = ws + a, vx + ax, vy + ay, vz + az
            ind = 0.5 - 0.5 * jnp.tanh(near)
            scale = ind / ws
            pay = jnp.concatenate([ind, vx * scale, vy * scale, vz * scale], axis=0).astype(BF16)
            base = pl.multiple_of(i * slab + lo_row, half)
            for c in range(4):
                paid[c, pl.ds(base, half), :] = pay[c * half : (c + 1) * half, :]
        return 0

    lax.fori_loop(0, BE, build, 0)
    for c in range(4):
        ob[c] = nn_dot(paid[c], block_hot).astype(BF16).astype(F32)
    diag[...] = 6.0 + PENALTY * ob[0]
    src[...] = src[...] - ((ob[1] + ob[2]) + ob[3])

    bz8 = lane8 % bz_n
    bx8 = (lane8 // bz_n) % bx_n
    bx64 = (lane64 // bz_n) % bx_n
    bx32 = (lane32 // bz_n) % bx_n
    bz32 = lane32 % bz_n
    tiles = BE // bz_n

    def turn(x, shift):
        shift = shift % lanes
        return x if shift == 0 else pltpu.roll(x, shift, axis=1)

    def load(value):
        vh = value.astype(BF16)
        rhs[:, :lanes] = vh
        rhs[:, lanes:] = (value - vh.astype(F32)).astype(BF16)

    def product(a, b):
        both = nn_dot(mh[a:b, :], rhs[...])
        return (both[:, :lanes] + both[:, lanes:]) + nn_dot(ml[a:b, :], rhs[:, :lanes])

    def face_low(f, i):
        if i == 0:
            return f[0:BE]
        if i == BE - 1:
            return f[slab : slab + BE]
        a = 2 * slab + (i - 1) * BE
        return f[a : a + BE]

    def face_high(f, i):
        if i == 0:
            return f[slab - BE : slab]
        if i == BE - 1:
            return f[2 * slab - BE : 2 * slab]
        a = 2 * slab + BE * (BE - 2) + (i - 1) * BE
        return f[a : a + BE]

    def pack_x(f):
        f0, f7 = f[:slab], f[slab : 2 * slab]
        low = jnp.where(bx32 == 0, f0[:half], turn(f0[half:], bz_n))
        high = jnp.where(bx32 == 0, turn(f7[:half], -bz_n), f7[half:])
        return low, high

    def pack_z(f):
        lows, highs = [], []
        for t in range(tiles):
            lowp = highp = None
            for a in range(bz_n):
                lo = turn(face_low(f, t * bz_n + a), a)
                hg = turn(face_high(f, t * bz_n + a), a - (bz_n - 1))
                lowp = lo if a == 0 else jnp.where(bz8 == a, lo, lowp)
                highp = hg if a == 0 else jnp.where(bz8 == a, hg, highp)
            lows.append(lowp)
            highs.append(highp)
        return jnp.concatenate(lows, axis=0), jnp.concatenate(highs, axis=0)

    def spread_x(got_low, got_high):
        at_low = [jnp.where(bx32 == 0, p, 0.0) for p in (got_low, turn(got_low, -bz_n))]
        at_high = [
            jnp.where(bx32 == bx_n - 1, p, 0.0) for p in (turn(got_high, bz_n), got_high)
        ]
        return at_low, at_high

    def spread_z(got_low, got_high):
        at_low, at_high = [], []
        for i in range(BE):
            t, a = i // bz_n, i % bz_n
            gl, gh = got_low[t * BE : (t + 1) * BE], got_high[t * BE : (t + 1) * BE]
            at_low.append(jnp.where(bz8 == 0, turn(gl, -a), 0.0))
            at_high.append(jnp.where(bz8 == bz_n - 1, turn(gh, bz_n - 1 - a), 0.0))
        return at_low, at_high

    def take_off(ref, xl, xh, zl, zh):
        at_low, at_high = spread_x(xl, xh)
        for h in range(2):
            a, b = h * half, cells - slab + h * half
            ref[a : a + half, :] = ref[a : a + half, :] - at_low[h]
            ref[b : b + half, :] = ref[b : b + half, :] - at_high[h]
        at_low, at_high = spread_z(zl, zh)
        for i in range(BE):
            a, b = i * slab, (i + 1) * slab - BE
            ref[a : a + BE, :] = ref[a : a + BE, :] - at_low[i]
            ref[b : b + BE, :] = ref[b : b + BE, :] - at_high[i]

    def ring_part(ring, at, xl, xh, zl, zh):
        low, high = spread_x(xl, xh)
        zlow, zhigh = spread_z(zl, zh)
        low, high = jnp.concatenate(low, axis=0), jnp.concatenate(high, axis=0)
        outer = []
        for rows, i in ((low, 0), (high, BE - 1)):
            outer += [rows[:BE] + zlow[i], rows[BE : slab - BE], rows[slab - BE :] + zhigh[i]]
        part = jnp.concatenate(outer + zlow[1:-1] + zhigh[1:-1], axis=0)
        hi = part.astype(BF16)
        low_at = ring.shape[1] // 2 + at
        ring[0:faces, at : at + lanes] = hi
        ring[0:faces, low_at : low_at + lanes] = (part - hi.astype(F32)).astype(BF16)

    for part in (own, ring):
        part[faces:, :] = jnp.zeros((wide - faces, part.shape[1]), BF16)

    def stencil(v_ref, out_ref):
        v0 = v_ref[0:slab, :]
        v7 = v_ref[cells - slab : cells, :]
        for i in range(BE):
            v = v_ref[i * slab : (i + 1) * slab, :]
            if i > 0:
                beside = v_ref[(i - 1) * slab : i * slab, :]
            else:
                beside = jnp.where(bx64 > 0, turn(v7, bz_n), 0.0)
            if i < BE - 1:
                beside = beside + v_ref[(i + 1) * slab : (i + 2) * slab, :]
            else:
                beside = beside + jnp.where(bx64 < bx_n - 1, turn(v0, -bz_n), 0.0)
            rows = []
            for k in range(BE):
                t = v[k * BE : (k + 1) * BE, :]
                if k > 0:
                    s = v[(k - 1) * BE : k * BE, :]
                else:
                    s = jnp.where(bz8 > 0, turn(v[slab - BE :, :], 1), 0.0)
                if k < BE - 1:
                    s = s + v[(k + 1) * BE : (k + 2) * BE, :]
                else:
                    s = s + jnp.where(bz8 < bz_n - 1, turn(v[:BE, :], -1), 0.0)
                down = pltpu.roll(t, 1, axis=0)
                edge = jnp.where(lane8 < group, 0.0, turn(down, group))
                s = s + jnp.where(sub8 == 0, edge, down)
                up = pltpu.roll(t, BE - 1, axis=0)
                edge = jnp.where(lane8 >= lanes - group, 0.0, turn(up, -group))
                s = s + jnp.where(sub8 == BE - 1, edge, up)
                rows.append(s)
            beside = beside + jnp.concatenate(rows, axis=0)
            out_ref[i * slab : (i + 1) * slab, :] = (
                diag[i * slab : (i + 1) * slab, :] * v - beside
            )

    def store(ref, f):
        for (a, b), c in zip(pieces, starts):
            if c < faces:
                ref[a:b, :] = f[c : c + b - a]

    starts = []
    for a, b in pieces:
        starts.append(starts[-1] + size if starts else 0)
        size = b - a

    def store_rest(ref, f):
        for (a, b), c in zip(pieces, starts):
            if c >= faces:
                ref[a:b, :] = f[c - faces : c - faces + b - a]

    ways = {
        "xl": (0, -1), "xh": (0, 1), "zl": (-1, 0), "zh": (1, 0),
        "xlzl": (-1, -1), "xhzl": (-1, 1), "xhzh": (1, 1), "xlzh": (1, -1),
    }
    zrows = tiles * BE
    span = half + zrows
    first_rows = {
        "xl": (0, half), "zl": (half, zrows), "xh": (span, half), "zh": (span + half, zrows),
        "xlzl": (0, span), "xhzl": (half, span), "xhzh": (span, span), "xlzh": (span + half, span),
    }
    order = ("xlzl", "xhzl", "xhzh", "xlzh", "xl", "xh", "zl", "zh")
    back = {"xl": "xh", "xh": "xl", "zl": "zh", "zh": "zl"}

    def opposite(key):
        return back[key[:2]] + back[key[2:]] if len(key) == 4 else back[key]

    def device(key):
        df, dc = ways[key]
        return lax.rem(mf + df + nf, nf), lax.min(lax.max(mc + dc, 0), nc - 1)

    groups = {"xl": ("xlzl", "xlzh", "xl"), "xh": ("xhzl", "xhzh", "xh"), "z": ("zl", "zh")}
    number = {key: n for n, keys in enumerate(groups.values()) for key in keys}

    def face_copy(e, key):
        a, size = first_rows[key]
        if len(key) == 4:
            target = ydiag.at[e, order.index(opposite(key))]
        else:
            target = (yz if key[0] == "z" else yx).at[e, int(key[1] == "l")]
        return pltpu.make_async_remote_copy(
            src_ref=ysend.at[e, pl.ds(a, size)],
            dst_ref=target,
            send_sem=ysend_sem.at[e, number[key]],
            recv_sem=yrecv_sem.at[e, number[key]],
            device_id=device(key),
            device_id_type=MESH,
        )

    def second_copy(e, key):
        side = int(key[1] == "h")
        return pltpu.make_async_remote_copy(
            src_ref=(gsz if key[0] == "z" else gsx).at[e, side],
            dst_ref=(gz if key[0] == "z" else gx).at[e, 1 - side],
            send_sem=gsend_sem.at[e, number[key]],
            recv_sem=grecv_sem.at[e, number[key]],
            device_id=device(key),
            device_id_type=MESH,
        )

    def start_all(copies):
        for copy in copies:
            copy.start()

    def start_group(copy, e, x_only=False):
        for side in ("xl", "xh"):
            keys = [side] if x_only else groups[side]
            pl.when(has[side])(functools.partial(start_all, [copy(e, k) for k in keys]))
        start_all([copy(e, k) for k in groups["z"]])

    def wait_bytes(ref, sem):
        pltpu.make_async_copy(ref, ref, sem).wait()

    def wait_group(e, sems, x_bytes, z_bytes, received):
        for n, side in enumerate(("xl", "xh")):
            cond = has[back[side]] if received else has[side]
            pl.when(cond)(functools.partial(wait_bytes, x_bytes, sems.at[e, n]))
        wait_bytes(z_bytes, sems.at[e, 2])

    def keep(cond, value):
        return jnp.where(cond, value, 0.0)

    def twice(e, p_ref, first_ref, image_ref, second_ref, out_ref, during):
        load(p_ref[...])
        f = product(0, faces)
        xl, xh = pack_x(f)
        zl, zh = pack_z(f)
        for key, value in (("xl", xl), ("zl", zl), ("xh", xh), ("zh", zh)):
            a, size = first_rows[key]
            ysend[e, a : a + size, :] = value
        ysend[e, 2 * span : 2 * span + half, :] = xl
        start_group(face_copy, e)
        store(first_ref, f)
        store_rest(first_ref, product(faces, cells))
        stencil(first_ref, image_ref)
        load(image_ref[...])
        g = product(0, faces)
        packed_x, packed_z = pack_x(g), pack_z(g)
        for n in range(2):
            gsx[e, n] = packed_x[n]
            gsz[e, n] = packed_z[n]
        start_group(second_copy, e, True)
        store(second_ref, g)
        store_rest(second_ref, product(faces, cells))
        during()
        wait_group(e, yrecv_sem, ysend.at[e], yz.at[e], True)
        first = (
            keep(has["xl"], yx[e, 0]), keep(has["xh"], yx[e, 1]),
            keep(has["zl"], yz[e, 0]), keep(has["zh"], yz[e, 1]),
        )
        ring_part(own, 0, *first)
        both = nn_dot(fh[...], own[...])
        change = (both[:, :lanes] + both[:, lanes:]) + nn_dot(fl[...], own[:, :lanes])
        for (a, b), c in zip(pieces, starts):
            second_ref[a:b, :] = second_ref[a:b, :] - change[c : c + b - a]

        def corner(key):
            a, size = first_rows[opposite(key)]
            xa = first_rows[opposite(key)[:2]][0] - a if opposite(key) != "xlzh" else zrows
            za = first_rows[opposite(key)[2:]][0] - a
            at = order.index(key)
            return ydiag[e, at, xa : xa + half, :], ydiag[e, at, za : za + zrows, :]

        (llx, llz), (hlx, hlz), (hhx, hhz), (lhx, lhz) = (corner(k) for k in order[:4])
        bxz = jnp.concatenate([bx8] * tiles, axis=0)
        lowx, highx = has["xl"], has["xh"]

        def by_x(high, low):
            return jnp.where(bxz == 0, keep(highx, high), keep(lowx, low))

        def by_z(low, high):
            low = jnp.where(bz32 == 0, keep(has["zh"], high), 0.0) + jnp.where(
                bz32 == bz_n - 1, keep(has["zl"], low), 0.0
            )
            return low

        ring_part(
            ring, 0, ysend[e, span : span + half, :], ysend[e, 0:half, :],
            keep(has["zl"], by_x(hlz, llz)), keep(has["zh"], by_x(hhz, lhz)),
        )
        ring_part(
            ring, lanes, keep(lowx, by_z(llx, lhx)), keep(highx, by_z(hlx, hhx)),
            ysend[e, span + half : 2 * span, :], ysend[e, half : span, :],
        )
        count = ring.shape[1] // 2
        both = nn_dot(fh[0:faces, :], ring[...])
        full = (both[:, :count] + both[:, count:]) + nn_dot(fl[0:faces, :], ring[:, :count])
        cxl, cxh = pack_x(full[:, :lanes])
        czl, czh = pack_z(full[:, lanes:])
        stencil(second_ref, out_ref)
        take_off(image_ref, *first)
        wait_group(e, grecv_sem, gx.at[e, 0], gz.at[e], True)
        take_off(
            out_ref,
            keep(has["xl"], gx[e, 0] - cxh),
            keep(has["xh"], gx[e, 1] - cxl),
            keep(has["zl"], gz[e, 0] - czh),
            keep(has["zh"], gz[e, 1] - czl),
        )

    def gram(pairs):
        total = [None] * len(pairs)
        for i in range(BE):
            read = {}
            for p in pairs:
                for ref in p:
                    if id(ref) not in read:
                        read[id(ref)] = ref[i * slab : (i + 1) * slab, :]
            for n, (a, b) in enumerate(pairs):
                part = jnp.sum((read[id(a)] * read[id(b)]).reshape(BE, BE, lanes), axis=0)
                total[n] = part if i == 0 else total[n] + part
        return [jnp.sum(t, axis=0, keepdims=True) for t in total]

    def show_obstacle():
        for c in range(4):
            def write(x, plane, c=c):
                obf[c, x] = plane.astype(BF16)

            rows_to_field(
                lambda j, c=c: ob[c, pl.ds(j, slab, stride=BE), :], write, bx_n, bz_n, lane64
            )

    basis = (src, v1, w1, u1, x1)
    known = [(a, b) for a in range(3) for b in range(a, 3)]
    late = [(a, b) for a in range(5) for b in range(a, 5) if b > 2]
    me = mf * nc + mc

    def tell(no, pairs):
        lines = gram([(basis[a], basis[b]) for a, b in pairs])
        number = -(-len(lines) // 8) * 8
        lines += [jnp.zeros((1, lanes), F32)] * (number - len(lines))
        tile = jnp.sum(jnp.concatenate(lines, axis=0), axis=1, keepdims=True)
        spot = lax.broadcasted_iota(jnp.int32, (number, lanes), 0) == lax.broadcasted_iota(
            jnp.int32, (number, lanes), 1
        )
        red[no, me] = jnp.sum(jnp.where(spot, tile, 0.0), axis=0, keepdims=True)

        def send(df, dc):
            pltpu.make_async_remote_copy(
                src_ref=red.at[no, me],
                dst_ref=red.at[no, me],
                send_sem=rsend_sem.at[no],
                recv_sem=rrecv_sem.at[no],
                device_id=(lax.rem(mf + df, nf), lax.rem(mc + dc, nc)),
                device_id_type=MESH,
            ).start()

        if everyone <= 64:
            for df in reversed(range(nf)):
                for dc in reversed(range(nc)):
                    if df or dc:
                        send(df, dc)
        else:

            def body(k, _):
                send(k // nc, lax.rem(k, nc))
                return 0

            lax.fori_loop(1, everyone, body, 0)

    def hear(no, pairs):
        heard = red.at[no, pl.ds(0, everyone - 1)]
        pltpu.make_async_copy(heard, heard, rrecv_sem.at[no]).wait()
        row = jnp.sum(red[no], axis=0)
        return dict(zip(pairs, entries(row, len(pairs))))

    def show(ref, out):
        def write(x, plane):
            out[x] = plane

        rows_to_field(lambda j: ref[pl.ds(j, slab, stride=BE), :], write, bx_n, bz_n, lane64)

    twice(0, src, y1, v1, m1, w1, show_obstacle)
    twice(1, w1, n1, u1, q1, x1, lambda: tell(0, known))
    tell(1, late)
    sums = hear(0, known)
    scalars = first_scalars(sums)
    for ref, out in (
        (src, rfield), (v1, vfield), (w1, wfield), (u1, ufield), (x1, xfield),
        (y1, yfield), (m1, mfield), (n1, nfield), (q1, qfield),
    ):
        show(ref, out)
    wait_bytes(handed, psend_sem)
    for e in range(2):
        wait_group(e, ysend_sem, ysend.at[e], yz.at[e], False)
        wait_group(e, gsend_sem, gx.at[e, 0], gz.at[e], False)
    sums.update(hear(1, late))
    resid, press = coefficients(sums, scalars)
    for first, coefs in ((0, resid), (8, press)):
        for k, coef in enumerate(coefs):
            coef_ref[first + k : first + k + 1, :] = jnp.broadcast_to(coef, (1, lanes))
    for no in range(2):
        heard = red.at[no, pl.ds(0, everyone - 1)]
        pltpu.make_async_copy(heard, heard, rsend_sem.at[no]).wait()


def local(right_side, block_inverse, midline, entry_fish, entry_seg, entry_dest, entry_block):
    nf, nc = lax.axis_size("fish"), lax.axis_size("curve")
    count = entry_fish.shape[0]
    cap = max(2, 2 * count // nc)
    cx, cz, ny = right_side.shape
    lanes = (cx // BE) * (cz // BE) * (ny // BE)
    cells = BE**3
    slab = BE * BE
    half = slab // 2
    zrows = BE // (cz // BE) * BE
    span = half + zrows
    wide = 4 * slab
    rows, fishes, npts = midline.shape
    width = fishes * npts
    vmem = pl.BlockSpec(memory_space=pltpu.VMEM)
    big = pltpu.VMEM((cells, lanes), F32)
    dma = pltpu.SemaphoreType.DMA
    anywhere = pl.BlockSpec(memory_space=pl.ANY)
    field = jax.ShapeDtypeStruct((cx, cz, ny), F32)
    fields = jax.ShapeDtypeStruct((4, cx, cz, ny), BF16)
    solved = pl.pallas_call(
        functools.partial(kernel, nf, nc, cap, npts),
        out_shape=(
            (pltpu.VMEM((16, lanes), F32),)
            + (pltpu.VMEM((cx, cz, ny), F32),) * 9
            + (pltpu.VMEM((4, cx, cz, ny), BF16),)
        ),
        in_specs=[anywhere] * 7,
        out_specs=(vmem,) * 11,
        scratch_shapes=[big] * 9
        + [
            pltpu.VMEM((cx, cz, ny), F32),
            pltpu.VMEM((cells, cells), F32),
            pltpu.VMEM((rows, fishes, npts), F32),
            pltpu.VMEM((4, 1, count), jnp.int32),
            dma((4,)),
            pltpu.VMEM((cells, cells), BF16),
            pltpu.VMEM((cells, cells), BF16),
            pltpu.VMEM((cells, wide), BF16),
            pltpu.VMEM((cells, wide), BF16),
            pltpu.VMEM((cells, 2 * lanes), BF16),
            pltpu.VMEM((wide, 2 * lanes), BF16),
            pltpu.VMEM((wide, 4 * lanes), BF16),
            pltpu.VMEM((8, lanes), F32),
            pltpu.VMEM((8, width), F32),
            pltpu.VMEM((SEG * 8, width), F32),
            pltpu.VMEM((nc, cap, lanes), F32),
            pltpu.VMEM((nc, cap, lanes), F32),
            pltpu.VMEM((SEG * 8, lanes), F32),
            pltpu.VMEM((SEG, slab, lanes), F32),
            pltpu.VMEM((4, cells, lanes), BF16),
            pltpu.VMEM((4, cells, lanes), F32),
            big,
            pltpu.VMEM((2, 2 * span + half, lanes), F32),
            pltpu.VMEM((2, 2, half, lanes), F32),
            pltpu.VMEM((2, 2, zrows, lanes), F32),
            pltpu.VMEM((2, 4, span, lanes), F32),
            pltpu.VMEM((2, 2, half, lanes), F32),
            pltpu.VMEM((2, 2, zrows, lanes), F32),
            pltpu.VMEM((2, 2, half, lanes), F32),
            pltpu.VMEM((2, 2, zrows, lanes), F32),
            pltpu.VMEM((2, nf * nc, 1, lanes), F32),
            dma,
            dma,
            dma((2, 3)),
            dma((2, 3)),
            dma((2, 3)),
            dma((2, 3)),
            dma((2,)),
            dma((2,)),
        ],
        compiler_params=pltpu.CompilerParams(
            collective_id=0, has_side_effects=True, vmem_limit_bytes=VMEM_LIMIT
        ),
    )(
        *(
            pltpu.with_memory_space_constraint(a, pltpu.HBM)
            for a in (
                right_side,
                block_inverse,
                midline,
                *(e.reshape(1, count) for e in (entry_fish, entry_seg, entry_dest, entry_block)),
            )
        )
    )
    return pl.pallas_call(
        finish,
        out_shape=(field, field, fields),
        in_specs=[vmem] * 11,
        out_specs=(anywhere,) * 3,
        scratch_shapes=[
            pltpu.VMEM((cx, cz, ny), F32),
            pltpu.VMEM((cx, cz, ny), F32),
            dma,
            dma((2, 4)),
        ],
        compiler_params=pltpu.CompilerParams(vmem_limit_bytes=VMEM_LIMIT),
    )(*(pltpu.with_memory_space_constraint(a, pltpu.VMEM) for a in solved))


def solution(mesh):
    return jax.shard_map(
        local,
        mesh=mesh,
        in_specs=(
            P("curve", "fish", None),
            P(),
            P(None, "fish", None),
            P(("fish", "curve")),
            P(("fish", "curve")),
            P(("fish", "curve"), None),
            P(("fish", "curve")),
        ),
        out_specs=(
            P("curve", "fish", None),
            P("curve", "fish", None),
            P(None, "curve", "fish", None),
        ),
        check_vma=False,
    )
```

```python
import functools
import jax
import jax.numpy as jnp
from jax import lax
from jax.experimental import pallas as pl
from jax.experimental.pallas import tpu as pltpu
from jax.sharding import PartitionSpec as P

BE = 8
SEG = 16
PENALTY = 4.0
F32 = jnp.float32
BF16 = jnp.bfloat16
MESH = pl.DeviceIdType.MESH


def nt_dot(a, b):
    return lax.dot_general(a, b, (((1,), (1,)), ((), ())), preferred_element_type=F32)


def nn_dot(a, b):
    return lax.dot_general(a, b, (((1,), (0,)), ((), ())), preferred_element_type=F32)


def split3(x):
    hi = x.astype(BF16)
    rest = x - hi.astype(F32)
    mid = rest.astype(BF16)
    low = (rest - mid.astype(F32)).astype(BF16)
    return hi, mid, low


def swap_bits(arrays, lane):
    arrays = list(arrays)
    lanes = lane.shape[-1]
    for step in (4, 2, 1):
        clear = (lane & step) == 0
        for a in range(8):
            if a & step:
                continue
            low, high = arrays[a], arrays[a | step]
            arrays[a] = jnp.where(clear, low, pltpu.roll(high, step, axis=1))
            arrays[a | step] = jnp.where(clear, pltpu.roll(low, lanes - step, axis=1), high)
    return arrays


def rows_to_field(read_j, write, bx_n, bz_n, lane):
    parts = swap_bits([read_j(j) for j in range(BE)], lane)
    for bx in range(bx_n):
        for i in range(BE):
            plane = jnp.concatenate(
                [parts[bx * bz_n + bz][i * BE : (i + 1) * BE, :] for bz in range(bz_n)], axis=0
            )
            write(bx * BE + i, plane)


VMEM_LIMIT = 40 * 1024 * 1024


def finish(
    coef_ref, r_ref, v_ref, w_ref, u_ref, x_ref, y_ref, m_ref, n_ref, q_ref, oin_ref,
    press_ref, resid_ref, obst_ref, pf, rf, osem, sems,
):
    give = pltpu.make_async_copy(oin_ref, obst_ref, osem)
    give.start()
    chunks = sems.shape[1]
    size = rf.shape[0] // chunks
    outs = []
    for c in range(chunks):
        part = pl.ds(c * size, size)
        for n, (out, dst, basis, first) in enumerate(
            (
                (rf, resid_ref, (r_ref, v_ref, w_ref, u_ref, x_ref), 0),
                (pf, press_ref, (y_ref, m_ref, n_ref, q_ref), 8),
            )
        ):
            total = None
            for k, ref in enumerate(basis):
                term = ref[part]
                if first or k:
                    term = coef_ref[first + k : first + k + 1, :] * term
                total = term if total is None else total + term
            out[part] = total
            copy = pltpu.make_async_copy(out.at[part], dst.at[part], sems.at[n, c])
            copy.start()
            outs.append(copy)
    for copy in outs:
        copy.wait()
    give.wait()


def entries(row, count):
    lane = lax.broadcasted_iota(jnp.int32, row.shape, 1)
    return [
        jnp.sum(jnp.where(lane == k, row, 0.0), axis=1, keepdims=True) for k in range(count)
    ]


def first_scalars(gram):
    rr, rv, vv, vw, ww, rw = (gram[k] for k in ((0, 0), (0, 1), (1, 1), (1, 2), (2, 2), (0, 2)))
    alpha = rr / rv
    ts = (rv - alpha * vv) - alpha * (rw - alpha * vw)
    tt = (vv - alpha * vw) - alpha * (vw - alpha * ww)
    omega = ts / tt
    rho2 = (rr - alpha * rv) - omega * (rv - alpha * rw)
    beta = rho2 / rr * (alpha / omega)
    both, prod = alpha + omega, alpha * omega
    d0, d1, d2 = 1.0 + beta, -(both + beta * omega), prod
    return rho2, both, prod, d0, d1, d2, d0 * rv + d1 * rw


def coefficients(gram, scalars):
    rho2, both, prod, d0, d1, d2, known = scalars
    gram = {**gram, **{(b, a): g for (a, b), g in gram.items()}}
    alpha2 = rho2 / (known + d2 * gram[0, 3])
    s1, s2, s3 = -both - alpha2 * d0, prod - alpha2 * d1, -alpha2 * d2
    ts = tt = None
    for a, sa in ((1, None), (2, s1), (3, s2), (4, s3)):
        q = (gram[a, 0] + s1 * gram[a, 1]) + (s2 * gram[a, 2] + s3 * gram[a, 3])
        z = (gram[a, 1] + s1 * gram[a, 2]) + (s2 * gram[a, 3] + s3 * gram[a, 4])
        ts = q if sa is None else ts + sa * q
        tt = z if sa is None else tt + sa * z
    omega2 = ts / tt
    resid = (omega2, s1 - omega2, s2 - omega2 * s1, s3 - omega2 * s2, -omega2 * s3)
    press = (
        both + alpha2 * d0 + omega2,
        alpha2 * d1 - prod + omega2 * s1,
        alpha2 * d2 + omega2 * s2,
        omega2 * s3,
    )
    return resid, press


def kernel(
    nf, nc, cap, npts,
    rs_hbm, inv_hbm, mid_hbm, fish_hbm, seg_hbm, dest_hbm, block_hbm,
    coef_ref, rfield, vfield, wfield, ufield, xfield, yfield, mfield, nfield, qfield, obf,
    src, v1, w1, u1, x1, y1, m1, n1, q1, rs_ref, inv_ref, mid_ref, ent_ref, in_sem,
    mh, ml, fh, fl, rhs, own, ring, meta_ref, tab, shifted, psend, precv, pt, dyz, paid, spread, ob, diag,
    ysend, yx, yz, ydiag, gsx, gsz, gx, gz, red,
    psend_sem, precv_sem, ysend_sem, yrecv_sem, gsend_sem, grecv_sem, rsend_sem, rrecv_sem,
):
    mf = lax.axis_index("fish")
    mc = lax.axis_index("curve")
    cells, lanes = src.shape
    slab = BE * BE
    half = slab // 2
    bx_n = rs_ref.shape[0] // BE
    bz_n = rs_ref.shape[1] // BE
    group = bx_n * bz_n
    everyone = nf * nc

    barrier = pltpu.get_barrier_semaphore()

    def greet_fish(k, _):
        pl.semaphore_signal(
            barrier, inc=1, device_id=(lax.rem(mf + k, nf), mc), device_id_type=MESH
        )
        return 0

    def greet_curve(k, _):
        pl.semaphore_signal(
            barrier, inc=1, device_id=(mf, lax.rem(mc + k, nc)), device_id_type=MESH
        )
        return 0

    lax.fori_loop(1, nc, greet_curve, 0)
    lax.fori_loop(1, nf, greet_fish, 0)

    takes = [
        pltpu.make_async_copy(a, b, in_sem.at[max(n - 3, 0)])
        for n, (a, b) in enumerate(
            [(a, ent_ref.at[k]) for k, a in enumerate((fish_hbm, seg_hbm, dest_hbm, block_hbm))]
            + [(mid_hbm, mid_ref), (inv_hbm, inv_ref), (rs_hbm, rs_ref)]
        )
    ]
    for copy in takes:
        copy.start()

    lane8 = lax.broadcasted_iota(jnp.int32, (BE, lanes), 1)
    lane64 = lax.broadcasted_iota(jnp.int32, (slab, lanes), 1)
    lane32 = lax.broadcasted_iota(jnp.int32, (half, lanes), 1)
    sub8 = lax.broadcasted_iota(jnp.int32, (BE, lanes), 0)
    col = lax.broadcasted_iota(jnp.int32, (lanes, lanes), 1)
    row = lax.broadcasted_iota(jnp.int32, (lanes, lanes), 0)
    colf, rowf = col.astype(F32), row.astype(F32)

    pltpu.make_async_copy(ent_ref, ent_ref, in_sem.at[0]).wait()
    takes[4].wait()
    nyb = rs_ref.shape[2] // BE
    count = ent_ref.shape[2]
    rows, fishes, _ = mid_ref.shape
    width = tab.shape[1]
    block = ent_ref[3]
    place_in = block % nyb * group + block // nyb + 1
    meta_ref[...] = jnp.full_like(meta_ref, -1.0)
    for r, column in enumerate((ent_ref[0], ent_ref[1], ent_ref[2], place_in)):
        meta_ref[r : r + 1, 0:count] = column.astype(F32)
    for f in range(fishes):
        tab[0:rows, f * npts : (f + 1) * npts] = mid_ref[:, f, :]
    tab[rows:8, :] = jnp.zeros((8 - rows, width), F32)
    table = tab[...]
    for m in range(SEG):
        turned = table if m == 0 else pltpu.roll(table, width - m, axis=1)
        shifted[m * 8 : m * 8 + 8, :] = turned
    meta = meta_ref[...]
    owner = lax.broadcasted_iota(jnp.int32, (nc, lanes), 0).astype(F32)
    mine = owner == meta[2:3, :]
    earlier = jnp.where(row < col, 1.0, 0.0).astype(BF16)
    rank = nn_dot(jnp.where(mine, 1.0, 0.0).astype(BF16), earlier)
    slot = jnp.sum(jnp.where(mine, owner * cap + rank + 1.0, 0.0), axis=0, keepdims=True) - 1.0
    hot = jnp.where(rowf == slot, 1.0, 0.0).astype(BF16)
    picked = nt_dot(hot, meta.astype(BF16))
    index = picked[:, 0:1] * npts + picked[:, 1:2]
    place = picked[:, 3:4] - 1.0
    point_hot = jnp.where(
        lax.broadcasted_iota(jnp.int32, (lanes, width), 1).astype(F32) == index, 1.0, 0.0
    ).astype(BF16)
    hi, mid, low = split3(shifted[...])
    points = (nt_dot(point_hot, hi) + nt_dot(point_hot, mid)) + nt_dot(point_hot, low)
    points = jnp.where(col == 7, place, points)
    for c in range(nc):
        psend[c] = points[c * cap : (c + 1) * cap, :]

    pl.semaphore_wait(barrier, nf - 1 + nc - 1)

    part = nc // 2
    near = mc // part * part
    bases = (near, part - near)

    def hand_start(far):
        def body(k, _):
            to = bases[far] + lax.rem(mc - near + k, part)
            pltpu.make_async_remote_copy(
                src_ref=psend.at[to],
                dst_ref=precv.at[mc],
                send_sem=psend_sem,
                recv_sem=precv_sem.at[far],
                device_id=(mf, to),
                device_id_type=MESH,
            ).start()
            return 0

        lax.fori_loop(1 - far, part, body, 0)

    hand_start(1)
    hand_start(0)
    precv[mc] = psend[mc]
    spread[...] = jnp.zeros_like(spread)

    takes[5].wait()
    whole = inv_ref[...]
    top = jnp.max(jnp.max(jnp.abs(whole), axis=0, keepdims=True), axis=1, keepdims=True)
    scale = 1.0 / (slab * top)
    inner_k = slab - 2 * BE
    pieces = [(0, slab), (cells - slab, cells)]
    pieces += [(i * slab, i * slab + BE) for i in range(1, BE - 1)]
    pieces += [((i + 1) * slab - BE, (i + 1) * slab) for i in range(1, BE - 1)]
    pieces += [(i * slab + BE, (i + 1) * slab - BE) for i in range(1, BE - 1)]
    faces = 2 * slab + 2 * BE * (BE - 2)
    arranged = jnp.concatenate([inv_ref[a:b, :] for a, b in pieces], axis=0) * scale
    hi = arranged.astype(BF16)
    mh[...] = hi
    ml[...] = (arranged - hi.astype(F32)).astype(BF16)
    wide = fh.shape[1]
    cell = lax.broadcasted_iota(jnp.int32, (cells, wide), 0)
    face = lax.broadcasted_iota(jnp.int32, (cells, wide), 1)
    side = (face - 2 * slab) // (BE * (BE - 2))
    deep = (face - 2 * slab) % (BE * (BE - 2))
    where_z = (deep // BE + 1) * slab + side * (slab - BE) + deep % BE
    where_x = face // slab * (cells - slab) + face % slab
    at = jnp.where(face < 2 * slab, where_x, jnp.where(face < faces, where_z, -1))
    pick = jnp.where(cell == at, 1.0, 0.0).astype(BF16)
    for full, kept in ((mh, fh), (ml, fl)):
        kept[...] = nn_dot(full[...], pick).astype(BF16)

    def field_to_rows(read, out_ref):
        parts = []
        for g in range(group):
            bx, bz = g // bz_n, g % bz_n
            parts.append(read(bx, bz).reshape(slab, lanes))
        for j, rows in enumerate(swap_bits(parts, lane64)):
            out_ref[pl.ds(j, slab, stride=BE), :] = rows

    takes[6].wait()
    field_to_rows(
        lambda bx, bz: rs_ref[bx * BE : (bx + 1) * BE, bz * BE : (bz + 1) * BE, :], src
    )

    has = {"xl": mc > 0, "xh": mc < nc - 1, "zl": mf > 0, "zh": mf < nf - 1}
    cell = lax.broadcasted_iota(jnp.int32, (slab, lanes), 0)
    zc = (cell // BE).astype(F32) + 0.5
    yc = (cell % BE).astype(F32) + 0.5
    slots = part * cap
    deep = BE // 2
    xbase = jnp.where(lane8[0:1, :] < slots, 0.5, 0.5 + deep)

    for far in range(2):
        handed = precv.at[pl.ds(0, part - 1 + far)]
        pltpu.make_async_copy(handed, handed, precv_sem.at[far]).wait()
        for c in range(part):
            value = precv[bases[far] + c]
            for h in range(2):
                pt[h * slots + c * cap : h * slots + (c + 1) * cap, :] = value
        got = pt[...]
        hot = jnp.where(colf[0:slots, :] == got[0:slots, 7:8], 1.0, 0.0).astype(BF16)
        for h in range(2):
            a = (2 * far + h) * slots
            spread[a : a + slots, h * lanes : (h + 1) * lanes] = hot
        pt[...] = got.T
        for m in range(SEG):
            dy = yc - pt[m * 8 + 1 : m * 8 + 2, :]
            dz = zc - pt[m * 8 + 2 : m * 8 + 3, :]
            dyz[m] = (dy * dy + dz * dz) + 0.25

        def build(i, _):
            xc = i.astype(F32) + xbase
            for h in range(2):
                lo_row = h * half
                near = ws = vx = vy = vz = None
                for m in range(SEG):
                    dx = xc - pt[m * 8 : m * 8 + 1, :]
                    e = dyz[m, lo_row : lo_row + half, :] + dx * dx
                    signed = e * lax.rsqrt(e) - pt[m * 8 + 6 : m * 8 + 7, :]
                    a = pl.reciprocal(e + 0.75, approx=True)
                    ax = a * pt[m * 8 + 3 : m * 8 + 4, :]
                    ay = a * pt[m * 8 + 4 : m * 8 + 5, :]
                    az = a * pt[m * 8 + 5 : m * 8 + 6, :]
                    if m == 0:
                        near, ws, vx, vy, vz = signed, a, ax, ay, az
                    else:
                        near = jnp.minimum(near, signed)
                        ws, vx, vy, vz = ws + a, vx + ax, vy + ay, vz + az
                ind = 0.5 - 0.5 * jnp.tanh(near)
                scale = ind / ws
                base = pl.multiple_of(i * slab + lo_row, half)
                for c, value in enumerate((ind, vx * scale, vy * scale, vz * scale)):
                    paid[c, pl.ds(base, half), far * lanes : (far + 1) * lanes] = value.astype(BF16)
            return 0

        lax.fori_loop(0, deep, build, 0)

    for c in range(4):
        summed = nn_dot(paid[c], spread[...]).astype(BF16).astype(F32)
        ob[c, 0 : deep * slab, :] = summed[:, :lanes]
        ob[c, deep * slab :, :] = summed[:, lanes:]
    diag[...] = 6.0 + PENALTY * ob[0]
    src[...] = src[...] - ((ob[1] + ob[2]) + ob[3])

    bz8 = lane8 % bz_n
    bx8 = (lane8 // bz_n) % bx_n
    bx64 = (lane64 // bz_n) % bx_n
    bx32 = (lane32 // bz_n) % bx_n
    bz32 = lane32 % bz_n
    tiles = BE // bz_n

    def turn(x, shift):
        shift = shift % lanes
        return x if shift == 0 else pltpu.roll(x, shift, axis=1)

    def load(value):
        vh = value.astype(BF16)
        rhs[:, :lanes] = vh
        rhs[:, lanes:] = (value - vh.astype(F32)).astype(BF16)

    def product(a, b):
        both = nn_dot(mh[a:b, :], rhs[...])
        return (both[:, :lanes] + both[:, lanes:]) + nn_dot(ml[a:b, :], rhs[:, :lanes])

    def face_low(f, i):
        if i == 0:
            return f[0:BE]
        if i == BE - 1:
            return f[slab : slab + BE]
        a = 2 * slab + (i - 1) * BE
        return f[a : a + BE]

    def face_high(f, i):
        if i == 0:
            return f[slab - BE : slab]
        if i == BE - 1:
            return f[2 * slab - BE : 2 * slab]
        a = 2 * slab + BE * (BE - 2) + (i - 1) * BE
        return f[a : a + BE]

    def pack_x(f):
        f0, f7 = f[:slab], f[slab : 2 * slab]
        low = jnp.where(bx32 == 0, f0[:half], turn(f0[half:], bz_n))
        high = jnp.where(bx32 == 0, turn(f7[:half], -bz_n), f7[half:])
        return low, high

    def pack_z(f):
        lows, highs = [], []
        for t in range(tiles):
            lowp = highp = None
            for a in range(bz_n):
                lo = turn(face_low(f, t * bz_n + a), a)
                hg = turn(face_high(f, t * bz_n + a), a - (bz_n - 1))
                lowp = lo if a == 0 else jnp.where(bz8 == a, lo, lowp)
                highp = hg if a == 0 else jnp.where(bz8 == a, hg, highp)
            lows.append(lowp)
            highs.append(highp)
        return jnp.concatenate(lows, axis=0), jnp.concatenate(highs, axis=0)

    def spread_x(got_low, got_high):
        at_low = [jnp.where(bx32 == 0, p, 0.0) for p in (got_low, turn(got_low, -bz_n))]
        at_high = [
            jnp.where(bx32 == bx_n - 1, p, 0.0) for p in (turn(got_high, bz_n), got_high)
        ]
        return at_low, at_high

    def spread_z(got_low, got_high):
        at_low, at_high = [], []
        for i in range(BE):
            t, a = i // bz_n, i % bz_n
            gl, gh = got_low[t * BE : (t + 1) * BE], got_high[t * BE : (t + 1) * BE]
            at_low.append(jnp.where(bz8 == 0, turn(gl, -a), 0.0))
            at_high.append(jnp.where(bz8 == bz_n - 1, turn(gh, bz_n - 1 - a), 0.0))
        return at_low, at_high

    def take_off(ref, xl, xh, zl, zh):
        at_low, at_high = spread_x(xl, xh)
        for h in range(2):
            a, b = h * half, cells - slab + h * half
            ref[a : a + half, :] = ref[a : a + half, :] - at_low[h]
            ref[b : b + half, :] = ref[b : b + half, :] - at_high[h]
        at_low, at_high = spread_z(zl, zh)
        for i in range(BE):
            a, b = i * slab, (i + 1) * slab - BE
            ref[a : a + BE, :] = ref[a : a + BE, :] - at_low[i]
            ref[b : b + BE, :] = ref[b : b + BE, :] - at_high[i]

    def ring_part(ring, at, xl, xh, zl, zh):
        low, high = spread_x(xl, xh)
        zlow, zhigh = spread_z(zl, zh)
        low, high = jnp.concatenate(low, axis=0), jnp.concatenate(high, axis=0)
        outer = []
        for rows, i in ((low, 0), (high, BE - 1)):
            outer += [rows[:BE] + zlow[i], rows[BE : slab - BE], rows[slab - BE :] + zhigh[i]]
        part = jnp.concatenate(outer + zlow[1:-1] + zhigh[1:-1], axis=0)
        hi = part.astype(BF16)
        low_at = ring.shape[1] // 2 + at
        ring[0:faces, at : at + lanes] = hi
        ring[0:faces, low_at : low_at + lanes] = (part - hi.astype(F32)).astype(BF16)

    for part in (own, ring):
        part[faces:, :] = jnp.zeros((wide - faces, part.shape[1]), BF16)

    def stencil(v_ref, out_ref):
        v0 = v_ref[0:slab, :]
        v7 = v_ref[cells - slab : cells, :]
        for i in range(BE):
            v = v_ref[i * slab : (i + 1) * slab, :]
            if i > 0:
                beside = v_ref[(i - 1) * slab : i * slab, :]
            else:
                beside = jnp.where(bx64 > 0, turn(v7, bz_n), 0.0)
            if i < BE - 1:
                beside = beside + v_ref[(i + 1) * slab : (i + 2) * slab, :]
            else:
                beside = beside + jnp.where(bx64 < bx_n - 1, turn(v0, -bz_n), 0.0)
            rows = []
            for k in range(BE):
                t = v[k * BE : (k + 1) * BE, :]
                if k > 0:
                    s = v[(k - 1) * BE : k * BE, :]
                else:
                    s = jnp.where(bz8 > 0, turn(v[slab - BE :, :], 1), 0.0)
                if k < BE - 1:
                    s = s + v[(k + 1) * BE : (k + 2) * BE, :]
                else:
                    s = s + jnp.where(bz8 < bz_n - 1, turn(v[:BE, :], -1), 0.0)
                down = pltpu.roll(t, 1, axis=0)
                edge = jnp.where(lane8 < group, 0.0, turn(down, group))
                s = s + jnp.where(sub8 == 0, edge, down)
                up = pltpu.roll(t, BE - 1, axis=0)
                edge = jnp.where(lane8 >= lanes - group, 0.0, turn(up, -group))
                s = s + jnp.where(sub8 == BE - 1, edge, up)
                rows.append(s)
            beside = beside + jnp.concatenate(rows, axis=0)
            out_ref[i * slab : (i + 1) * slab, :] = (
                diag[i * slab : (i + 1) * slab, :] * v - beside
            )

    def store(ref, f):
        for (a, b), c in zip(pieces, starts):
            if c < faces:
                ref[a:b, :] = f[c : c + b - a]

    starts = []
    for a, b in pieces:
        starts.append(starts[-1] + size if starts else 0)
        size = b - a

    def store_rest(ref, f):
        for (a, b), c in zip(pieces, starts):
            if c >= faces:
                ref[a:b, :] = f[c - faces : c - faces + b - a]

    ways = {
        "xl": (0, -1), "xh": (0, 1), "zl": (-1, 0), "zh": (1, 0),
        "xlzl": (-1, -1), "xhzl": (-1, 1), "xhzh": (1, 1), "xlzh": (1, -1),
    }
    zrows = tiles * BE
    span = half + zrows
    first_rows = {
        "xl": (0, half), "zl": (half, zrows), "xh": (span, half), "zh": (span + half, zrows),
        "xlzl": (0, span), "xhzl": (half, span), "xhzh": (span, span), "xlzh": (span + half, span),
    }
    order = ("xlzl", "xhzl", "xhzh", "xlzh", "xl", "xh", "zl", "zh")
    back = {"xl": "xh", "xh": "xl", "zl": "zh", "zh": "zl"}

    def opposite(key):
        return back[key[:2]] + back[key[2:]] if len(key) == 4 else back[key]

    def device(key):
        df, dc = ways[key]
        return lax.rem(mf + df + nf, nf), lax.min(lax.max(mc + dc, 0), nc - 1)

    groups = {"xl": ("xlzl", "xlzh", "xl"), "xh": ("xhzl", "xhzh", "xh"), "z": ("zl", "zh")}
    number = {key: n for n, keys in enumerate(groups.values()) for key in keys}

    def face_copy(e, key):
        a, size = first_rows[key]
        if len(key) == 4:
            target = ydiag.at[e, order.index(opposite(key))]
        else:
            target = (yz if key[0] == "z" else yx).at[e, int(key[1] == "l")]
        return pltpu.make_async_remote_copy(
            src_ref=ysend.at[e, pl.ds(a, size)],
            dst_ref=target,
            send_sem=ysend_sem.at[e, number[key]],
            recv_sem=yrecv_sem.at[e, number[key]],
            device_id=device(key),
            device_id_type=MESH,
        )

    def second_copy(e, key):
        side = int(key[1] == "h")
        return pltpu.make_async_remote_copy(
            src_ref=(gsz if key[0] == "z" else gsx).at[e, side],
            dst_ref=(gz if key[0] == "z" else gx).at[e, 1 - side],
            send_sem=gsend_sem.at[e, number[key]],
            recv_sem=grecv_sem.at[e, number[key]],
            device_id=device(key),
            device_id_type=MESH,
        )

    def start_all(copies):
        for copy in copies:
            copy.start()

    def start_group(copy, e, x_only=False):
        for side in ("xl", "xh"):
            keys = [side] if x_only else groups[side]
            pl.when(has[side])(functools.partial(start_all, [copy(e, k) for k in keys]))
        start_all([copy(e, k) for k in groups["z"]])

    def wait_bytes(ref, sem):
        pltpu.make_async_copy(ref, ref, sem).wait()

    def wait_group(e, sems, x_bytes, z_bytes, received):
        for n, side in enumerate(("xl", "xh")):
            cond = has[back[side]] if received else has[side]
            pl.when(cond)(functools.partial(wait_bytes, x_bytes, sems.at[e, n]))
        wait_bytes(z_bytes, sems.at[e, 2])

    def keep(cond, value):
        return jnp.where(cond, value, 0.0)

    def twice(e, p_ref, first_ref, image_ref, second_ref, out_ref, during):
        load(p_ref[...])
        f = product(0, faces)
        xl, xh = pack_x(f)
        zl, zh = pack_z(f)
        for key, value in (("xl", xl), ("zl", zl), ("xh", xh), ("zh", zh)):
            a, size = first_rows[key]
            ysend[e, a : a + size, :] = value
        ysend[e, 2 * span : 2 * span + half, :] = xl
        start_group(face_copy, e)
        store(first_ref, f)
        store_rest(first_ref, product(faces, cells))
        stencil(first_ref, image_ref)
        load(image_ref[...])
        g = product(0, faces)
        packed_x, packed_z = pack_x(g), pack_z(g)
        for n in range(2):
            gsx[e, n] = packed_x[n]
            gsz[e, n] = packed_z[n]
        start_group(second_copy, e, True)
        store(second_ref, g)
        store_rest(second_ref, product(faces, cells))
        during()
        wait_group(e, yrecv_sem, ysend.at[e], yz.at[e], True)
        first = (
            keep(has["xl"], yx[e, 0]), keep(has["xh"], yx[e, 1]),
            keep(has["zl"], yz[e, 0]), keep(has["zh"], yz[e, 1]),
        )
        ring_part(own, 0, *first)
        both = nn_dot(fh[...], own[...])
        change = (both[:, :lanes] + both[:, lanes:]) + nn_dot(fl[...], own[:, :lanes])
        for (a, b), c in zip(pieces, starts):
            second_ref[a:b, :] = second_ref[a:b, :] - change[c : c + b - a]

        def corner(key):
            a, size = first_rows[opposite(key)]
            xa = first_rows[opposite(key)[:2]][0] - a if opposite(key) != "xlzh" else zrows
            za = first_rows[opposite(key)[2:]][0] - a
            at = order.index(key)
            return ydiag[e, at, xa : xa + half, :], ydiag[e, at, za : za + zrows, :]

        (llx, llz), (hlx, hlz), (hhx, hhz), (lhx, lhz) = (corner(k) for k in order[:4])
        bxz = jnp.concatenate([bx8] * tiles, axis=0)
        lowx, highx = has["xl"], has["xh"]

        def by_x(high, low):
            return jnp.where(bxz == 0, keep(highx, high), keep(lowx, low))

        def by_z(low, high):
            low = jnp.where(bz32 == 0, keep(has["zh"], high), 0.0) + jnp.where(
                bz32 == bz_n - 1, keep(has["zl"], low), 0.0
            )
            return low

        ring_part(
            ring, 0, ysend[e, span : span + half, :], ysend[e, 0:half, :],
            keep(has["zl"], by_x(hlz, llz)), keep(has["zh"], by_x(hhz, lhz)),
        )
        ring_part(
            ring, lanes, keep(lowx, by_z(llx, lhx)), keep(highx, by_z(hlx, hhx)),
            ysend[e, span + half : 2 * span, :], ysend[e, half : span, :],
        )
        count = ring.shape[1] // 2
        both = nn_dot(fh[0:faces, :], ring[...])
        full = (both[:, :count] + both[:, count:]) + nn_dot(fl[0:faces, :], ring[:, :count])
        cxl, cxh = pack_x(full[:, :lanes])
        czl, czh = pack_z(full[:, lanes:])
        stencil(second_ref, out_ref)
        take_off(image_ref, *first)
        wait_group(e, grecv_sem, gx.at[e, 0], gz.at[e], True)
        take_off(
            out_ref,
            keep(has["xl"], gx[e, 0] - cxh),
            keep(has["xh"], gx[e, 1] - cxl),
            keep(has["zl"], gz[e, 0] - czh),
            keep(has["zh"], gz[e, 1] - czl),
        )

    def gram(pairs):
        total = [None] * len(pairs)
        for i in range(BE):
            read = {}
            for p in pairs:
                for ref in p:
                    if id(ref) not in read:
                        read[id(ref)] = ref[i * slab : (i + 1) * slab, :]
            for n, (a, b) in enumerate(pairs):
                part = jnp.sum((read[id(a)] * read[id(b)]).reshape(BE, BE, lanes), axis=0)
                total[n] = part if i == 0 else total[n] + part
        return [jnp.sum(t, axis=0, keepdims=True) for t in total]

    def show_obstacle():
        for c in range(4):
            def write(x, plane, c=c):
                obf[c, x] = plane.astype(BF16)

            rows_to_field(
                lambda j, c=c: ob[c, pl.ds(j, slab, stride=BE), :], write, bx_n, bz_n, lane64
            )

    basis = (src, v1, w1, u1, x1)
    known = [(a, b) for a in range(3) for b in range(a, 3)]
    late = [(a, b) for a in range(5) for b in range(a, 5) if b > 2]
    me = mf * nc + mc

    def tell(no, pairs):
        lines = gram([(basis[a], basis[b]) for a, b in pairs])
        number = -(-len(lines) // 8) * 8
        lines += [jnp.zeros((1, lanes), F32)] * (number - len(lines))
        tile = jnp.sum(jnp.concatenate(lines, axis=0), axis=1, keepdims=True)
        spot = lax.broadcasted_iota(jnp.int32, (number, lanes), 0) == lax.broadcasted_iota(
            jnp.int32, (number, lanes), 1
        )
        red[no, me] = jnp.sum(jnp.where(spot, tile, 0.0), axis=0, keepdims=True)

        def send(df, dc):
            pltpu.make_async_remote_copy(
                src_ref=red.at[no, me],
                dst_ref=red.at[no, me],
                send_sem=rsend_sem.at[no],
                recv_sem=rrecv_sem.at[no],
                device_id=(lax.rem(mf + df, nf), lax.rem(mc + dc, nc)),
                device_id_type=MESH,
            ).start()

        if everyone <= 64:
            for df in reversed(range(nf)):
                for dc in reversed(range(nc)):
                    if df or dc:
                        send(df, dc)
        else:

            def body(k, _):
                send(k // nc, lax.rem(k, nc))
                return 0

            lax.fori_loop(1, everyone, body, 0)

    def hear(no, pairs):
        heard = red.at[no, pl.ds(0, everyone - 1)]
        pltpu.make_async_copy(heard, heard, rrecv_sem.at[no]).wait()
        row = jnp.sum(red[no], axis=0)
        return dict(zip(pairs, entries(row, len(pairs))))

    def show(ref, out):
        def write(x, plane):
            out[x] = plane

        rows_to_field(lambda j: ref[pl.ds(j, slab, stride=BE), :], write, bx_n, bz_n, lane64)

    twice(0, src, y1, v1, m1, w1, show_obstacle)
    twice(1, w1, n1, u1, q1, x1, lambda: tell(0, known))
    tell(1, late)
    sums = hear(0, known)
    scalars = first_scalars(sums)
    for ref, out in (
        (src, rfield), (v1, vfield), (w1, wfield), (u1, ufield), (x1, xfield),
        (y1, yfield), (m1, mfield), (n1, nfield), (q1, qfield),
    ):
        show(ref, out)
    wait_bytes(precv.at[pl.ds(0, nc - 1)], psend_sem)
    for e in range(2):
        wait_group(e, ysend_sem, ysend.at[e], yz.at[e], False)
        wait_group(e, gsend_sem, gx.at[e, 0], gz.at[e], False)
    sums.update(hear(1, late))
    resid, press = coefficients(sums, scalars)
    for first, coefs in ((0, resid), (8, press)):
        for k, coef in enumerate(coefs):
            coef_ref[first + k : first + k + 1, :] = jnp.broadcast_to(coef, (1, lanes))
    for no in range(2):
        heard = red.at[no, pl.ds(0, everyone - 1)]
        pltpu.make_async_copy(heard, heard, rsend_sem.at[no]).wait()


def local(right_side, block_inverse, midline, entry_fish, entry_seg, entry_dest, entry_block):
    nf, nc = lax.axis_size("fish"), lax.axis_size("curve")
    count = entry_fish.shape[0]
    cap = max(2, 2 * count // nc)
    cx, cz, ny = right_side.shape
    lanes = (cx // BE) * (cz // BE) * (ny // BE)
    cells = BE**3
    slab = BE * BE
    half = slab // 2
    zrows = BE // (cz // BE) * BE
    span = half + zrows
    wide = 4 * slab
    rows, fishes, npts = midline.shape
    width = fishes * npts
    vmem = pl.BlockSpec(memory_space=pltpu.VMEM)
    big = pltpu.VMEM((cells, lanes), F32)
    dma = pltpu.SemaphoreType.DMA
    anywhere = pl.BlockSpec(memory_space=pl.ANY)
    field = jax.ShapeDtypeStruct((cx, cz, ny), F32)
    fields = jax.ShapeDtypeStruct((4, cx, cz, ny), BF16)
    solved = pl.pallas_call(
        functools.partial(kernel, nf, nc, cap, npts),
        out_shape=(
            (pltpu.VMEM((16, lanes), F32),)
            + (pltpu.VMEM((cx, cz, ny), F32),) * 9
            + (pltpu.VMEM((4, cx, cz, ny), BF16),)
        ),
        in_specs=[anywhere] * 7,
        out_specs=(vmem,) * 11,
        scratch_shapes=[big] * 9
        + [
            pltpu.VMEM((cx, cz, ny), F32),
            pltpu.VMEM((cells, cells), F32),
            pltpu.VMEM((rows, fishes, npts), F32),
            pltpu.VMEM((4, 1, count), jnp.int32),
            dma((4,)),
            pltpu.VMEM((cells, cells), BF16),
            pltpu.VMEM((cells, cells), BF16),
            pltpu.VMEM((cells, wide), BF16),
            pltpu.VMEM((cells, wide), BF16),
            pltpu.VMEM((cells, 2 * lanes), BF16),
            pltpu.VMEM((wide, 2 * lanes), BF16),
            pltpu.VMEM((wide, 4 * lanes), BF16),
            pltpu.VMEM((8, lanes), F32),
            pltpu.VMEM((8, width), F32),
            pltpu.VMEM((SEG * 8, width), F32),
            pltpu.VMEM((nc, cap, lanes), F32),
            pltpu.VMEM((nc, cap, lanes), F32),
            pltpu.VMEM((SEG * 8, lanes), F32),
            pltpu.VMEM((SEG, slab, lanes), F32),
            pltpu.VMEM((4, cells // 2, 2 * lanes), BF16),
            pltpu.VMEM((2 * lanes, 2 * lanes), BF16),
            pltpu.VMEM((4, cells, lanes), F32),
            big,
            pltpu.VMEM((2, 2 * span + half, lanes), F32),
            pltpu.VMEM((2, 2, half, lanes), F32),
            pltpu.VMEM((2, 2, zrows, lanes), F32),
            pltpu.VMEM((2, 4, span, lanes), F32),
            pltpu.VMEM((2, 2, half, lanes), F32),
            pltpu.VMEM((2, 2, zrows, lanes), F32),
            pltpu.VMEM((2, 2, half, lanes), F32),
            pltpu.VMEM((2, 2, zrows, lanes), F32),
            pltpu.VMEM((2, nf * nc, 1, lanes), F32),
            dma,
            dma((2,)),
            dma((2, 3)),
            dma((2, 3)),
            dma((2, 3)),
            dma((2, 3)),
            dma((2,)),
            dma((2,)),
        ],
        compiler_params=pltpu.CompilerParams(
            collective_id=0, has_side_effects=True, vmem_limit_bytes=VMEM_LIMIT
        ),
    )(
        *(
            pltpu.with_memory_space_constraint(a, pltpu.HBM)
            for a in (
                right_side,
                block_inverse,
                midline,
                *(e.reshape(1, count) for e in (entry_fish, entry_seg, entry_dest, entry_block)),
            )
        )
    )
    return pl.pallas_call(
        finish,
        out_shape=(field, field, fields),
        in_specs=[vmem] * 11,
        out_specs=(anywhere,) * 3,
        scratch_shapes=[
            pltpu.VMEM((cx, cz, ny), F32),
            pltpu.VMEM((cx, cz, ny), F32),
            dma,
            dma((2, 4)),
        ],
        compiler_params=pltpu.CompilerParams(vmem_limit_bytes=VMEM_LIMIT),
    )(*(pltpu.with_memory_space_constraint(a, pltpu.VMEM) for a in solved))


def solution(mesh):
    return jax.shard_map(
        local,
        mesh=mesh,
        in_specs=(
            P("curve", "fish", None),
            P(),
            P(None, "fish", None),
            P(("fish", "curve")),
            P(("fish", "curve")),
            P(("fish", "curve"), None),
            P(("fish", "curve")),
        ),
        out_specs=(
            P("curve", "fish", None),
            P("curve", "fish", None),
            P(None, "curve", "fish", None),
        ),
        check_vma=False,
    )
```

```python
import functools
import jax
import jax.numpy as jnp
from jax import lax
from jax.experimental import pallas as pl
from jax.experimental.pallas import tpu as pltpu
from jax.sharding import PartitionSpec as P

BE = 8
SEG = 16
PENALTY = 4.0
F32 = jnp.float32
BF16 = jnp.bfloat16
MESH = pl.DeviceIdType.MESH


def nt_dot(a, b):
    return lax.dot_general(a, b, (((1,), (1,)), ((), ())), preferred_element_type=F32)


def nn_dot(a, b):
    return lax.dot_general(a, b, (((1,), (0,)), ((), ())), preferred_element_type=F32)


def split3(x):
    hi = x.astype(BF16)
    rest = x - hi.astype(F32)
    mid = rest.astype(BF16)
    low = (rest - mid.astype(F32)).astype(BF16)
    return hi, mid, low


def swap_bits(arrays, lane):
    arrays = list(arrays)
    lanes = lane.shape[-1]
    for step in (4, 2, 1):
        clear = (lane & step) == 0
        for a in range(8):
            if a & step:
                continue
            low, high = arrays[a], arrays[a | step]
            arrays[a] = jnp.where(clear, low, pltpu.roll(high, step, axis=1))
            arrays[a | step] = jnp.where(clear, pltpu.roll(low, lanes - step, axis=1), high)
    return arrays


def rows_to_field(read_j, write, bx_n, bz_n, lane):
    parts = swap_bits([read_j(j) for j in range(BE)], lane)
    for bx in range(bx_n):
        for i in range(BE):
            plane = jnp.concatenate(
                [parts[bx * bz_n + bz][i * BE : (i + 1) * BE, :] for bz in range(bz_n)], axis=0
            )
            write(bx * BE + i, plane)


VMEM_LIMIT = 40 * 1024 * 1024


def finish(
    coef_ref, r_ref, v_ref, w_ref, u_ref, x_ref, y_ref, m_ref, n_ref, q_ref, oin_ref,
    press_ref, resid_ref, obst_ref, pf, rf, osem, sems,
):
    give = pltpu.make_async_copy(oin_ref, obst_ref, osem)
    give.start()
    chunks = sems.shape[1]
    size = rf.shape[0] // chunks
    outs = []
    for c in range(chunks):
        part = pl.ds(c * size, size)
        for n, (out, dst, basis, first) in enumerate(
            (
                (rf, resid_ref, (r_ref, v_ref, w_ref, u_ref, x_ref), 0),
                (pf, press_ref, (y_ref, m_ref, n_ref, q_ref), 8),
            )
        ):
            total = None
            for k, ref in enumerate(basis):
                term = ref[part]
                if first or k:
                    term = coef_ref[first + k : first + k + 1, :] * term
                total = term if total is None else total + term
            out[part] = total
            copy = pltpu.make_async_copy(out.at[part], dst.at[part], sems.at[n, c])
            copy.start()
            outs.append(copy)
    for copy in outs:
        copy.wait()
    give.wait()


def entries(row, count):
    lane = lax.broadcasted_iota(jnp.int32, row.shape, 1)
    return [
        jnp.sum(jnp.where(lane == k, row, 0.0), axis=1, keepdims=True) for k in range(count)
    ]


def first_scalars(gram):
    rr, rv, vv, vw, ww, rw = (gram[k] for k in ((0, 0), (0, 1), (1, 1), (1, 2), (2, 2), (0, 2)))
    alpha = rr / rv
    ts = (rv - alpha * vv) - alpha * (rw - alpha * vw)
    tt = (vv - alpha * vw) - alpha * (vw - alpha * ww)
    omega = ts / tt
    rho2 = (rr - alpha * rv) - omega * (rv - alpha * rw)
    beta = rho2 / rr * (alpha / omega)
    both, prod = alpha + omega, alpha * omega
    d0, d1, d2 = 1.0 + beta, -(both + beta * omega), prod
    return rho2, both, prod, d0, d1, d2, d0 * rv + d1 * rw


def coefficients(gram, scalars):
    rho2, both, prod, d0, d1, d2, known = scalars
    gram = {**gram, **{(b, a): g for (a, b), g in gram.items()}}
    alpha2 = rho2 / (known + d2 * gram[0, 3])
    s1, s2, s3 = -both - alpha2 * d0, prod - alpha2 * d1, -alpha2 * d2
    ts = tt = None
    for a, sa in ((1, None), (2, s1), (3, s2), (4, s3)):
        q = (gram[a, 0] + s1 * gram[a, 1]) + (s2 * gram[a, 2] + s3 * gram[a, 3])
        z = (gram[a, 1] + s1 * gram[a, 2]) + (s2 * gram[a, 3] + s3 * gram[a, 4])
        ts = q if sa is None else ts + sa * q
        tt = z if sa is None else tt + sa * z
    omega2 = ts / tt
    resid = (omega2, s1 - omega2, s2 - omega2 * s1, s3 - omega2 * s2, -omega2 * s3)
    press = (
        both + alpha2 * d0 + omega2,
        alpha2 * d1 - prod + omega2 * s1,
        alpha2 * d2 + omega2 * s2,
        omega2 * s3,
    )
    return resid, press


def kernel(
    nf, nc, cap, npts,
    rs_hbm, inv_hbm, mid_hbm, fish_hbm, seg_hbm, dest_hbm, block_hbm,
    coef_ref, rfield, vfield, wfield, ufield, xfield, yfield, mfield, nfield, qfield, obf,
    src, v1, w1, u1, x1, y1, m1, n1, q1, rs_ref, inv_ref, mid_ref, ent_ref, in_sem,
    mh, ml, fh, fl, rhs, own, ring, meta_ref, tab, shifted, psend, precv, pt, dyz, paid, spread, ob, diag,
    ysend, csend, yx, yz, ydiag, gsx, gsz, gx, gz, red,
    psend_sem, precv_sem, ysend_sem, yrecv_sem, gsend_sem, grecv_sem, rsend_sem, rrecv_sem,
):
    mf = lax.axis_index("fish")
    mc = lax.axis_index("curve")
    cells, lanes = src.shape
    slab = BE * BE
    half = slab // 2
    bx_n = rs_ref.shape[0] // BE
    bz_n = rs_ref.shape[1] // BE
    group = bx_n * bz_n
    everyone = nf * nc

    barrier = pltpu.get_barrier_semaphore()

    def greet_fish(k, _):
        pl.semaphore_signal(
            barrier, inc=1, device_id=(lax.rem(mf + k, nf), mc), device_id_type=MESH
        )
        return 0

    def greet_curve(k, _):
        pl.semaphore_signal(
            barrier, inc=1, device_id=(mf, lax.rem(mc + k, nc)), device_id_type=MESH
        )
        return 0

    lax.fori_loop(1, nc, greet_curve, 0)
    lax.fori_loop(1, nf, greet_fish, 0)

    takes = [
        pltpu.make_async_copy(a, b, in_sem.at[max(n - 3, 0)])
        for n, (a, b) in enumerate(
            [(a, ent_ref.at[k]) for k, a in enumerate((fish_hbm, seg_hbm, dest_hbm, block_hbm))]
            + [(mid_hbm, mid_ref), (inv_hbm, inv_ref), (rs_hbm, rs_ref)]
        )
    ]
    for copy in takes:
        copy.start()

    lane8 = lax.broadcasted_iota(jnp.int32, (BE, lanes), 1)
    lane64 = lax.broadcasted_iota(jnp.int32, (slab, lanes), 1)
    lane32 = lax.broadcasted_iota(jnp.int32, (half, lanes), 1)
    sub8 = lax.broadcasted_iota(jnp.int32, (BE, lanes), 0)
    col = lax.broadcasted_iota(jnp.int32, (lanes, lanes), 1)
    row = lax.broadcasted_iota(jnp.int32, (lanes, lanes), 0)
    colf, rowf = col.astype(F32), row.astype(F32)

    pltpu.make_async_copy(ent_ref, ent_ref, in_sem.at[0]).wait()
    takes[4].wait()
    nyb = rs_ref.shape[2] // BE
    count = ent_ref.shape[2]
    rows, fishes, _ = mid_ref.shape
    width = tab.shape[1]
    block = ent_ref[3]
    place_in = block % nyb * group + block // nyb + 1
    meta_ref[...] = jnp.full_like(meta_ref, -1.0)
    for r, column in enumerate((ent_ref[0], ent_ref[1], ent_ref[2], place_in)):
        meta_ref[r : r + 1, 0:count] = column.astype(F32)
    for f in range(fishes):
        tab[0:rows, f * npts : (f + 1) * npts] = mid_ref[:, f, :]
    tab[rows:8, :] = jnp.zeros((8 - rows, width), F32)
    table = tab[...]
    for m in range(SEG):
        turned = table if m == 0 else pltpu.roll(table, width - m, axis=1)
        shifted[m * 8 : m * 8 + 8, :] = turned
    meta = meta_ref[...]
    owner = lax.broadcasted_iota(jnp.int32, (nc, lanes), 0).astype(F32)
    mine = owner == meta[2:3, :]
    earlier = jnp.where(row < col, 1.0, 0.0).astype(BF16)
    rank = nn_dot(jnp.where(mine, 1.0, 0.0).astype(BF16), earlier)
    slot = jnp.sum(jnp.where(mine, owner * cap + rank + 1.0, 0.0), axis=0, keepdims=True) - 1.0
    hot = jnp.where(rowf == slot, 1.0, 0.0).astype(BF16)
    picked = nt_dot(hot, meta.astype(BF16))
    index = picked[:, 0:1] * npts + picked[:, 1:2]
    place = picked[:, 3:4] - 1.0
    point_hot = jnp.where(
        lax.broadcasted_iota(jnp.int32, (lanes, width), 1).astype(F32) == index, 1.0, 0.0
    ).astype(BF16)
    hi, mid, low = split3(shifted[...])
    points = (nt_dot(point_hot, hi) + nt_dot(point_hot, mid)) + nt_dot(point_hot, low)
    points = jnp.where(col == 7, place, points)
    for c in range(nc):
        psend[c] = points[c * cap : (c + 1) * cap, :]

    pl.semaphore_wait(barrier, nf - 1 + nc - 1)

    part = nc // 2
    near = mc // part * part
    bases = (near, part - near)

    def hand_start(far):
        def body(k, _):
            to = bases[far] + lax.rem(mc - near + k, part)
            pltpu.make_async_remote_copy(
                src_ref=psend.at[to],
                dst_ref=precv.at[mc],
                send_sem=psend_sem,
                recv_sem=precv_sem.at[far],
                device_id=(mf, to),
                device_id_type=MESH,
            ).start()
            return 0

        lax.fori_loop(1 - far, part, body, 0)

    hand_start(1)
    hand_start(0)
    precv[mc] = psend[mc]
    spread[...] = jnp.zeros_like(spread)

    takes[5].wait()
    whole = inv_ref[...]
    top = jnp.max(jnp.max(jnp.abs(whole), axis=0, keepdims=True), axis=1, keepdims=True)
    scale = 1.0 / (slab * top)
    inner_k = slab - 2 * BE
    pieces = [(0, slab), (cells - slab, cells)]
    pieces += [(i * slab, i * slab + BE) for i in range(1, BE - 1)]
    pieces += [((i + 1) * slab - BE, (i + 1) * slab) for i in range(1, BE - 1)]
    pieces += [(i * slab + BE, (i + 1) * slab - BE) for i in range(1, BE - 1)]
    faces = 2 * slab + 2 * BE * (BE - 2)
    arranged = jnp.concatenate([inv_ref[a:b, :] for a, b in pieces], axis=0) * scale
    hi = arranged.astype(BF16)
    mh[...] = hi
    ml[...] = (arranged - hi.astype(F32)).astype(BF16)
    wide = fh.shape[1]
    cell = lax.broadcasted_iota(jnp.int32, (cells, wide), 0)
    face = lax.broadcasted_iota(jnp.int32, (1, wide), 1)
    side = (face - 2 * slab) // (BE * (BE - 2))
    deep = (face - 2 * slab) % (BE * (BE - 2))
    where_z = (deep // BE + 1) * slab + side * (slab - BE) + deep % BE
    where_x = face // slab * (cells - slab) + face % slab
    at = jnp.where(face < 2 * slab, where_x, jnp.where(face < faces, where_z, -1))
    pick = jnp.where(cell == at, 1.0, 0.0).astype(BF16)
    for full, kept in ((mh, fh), (ml, fl)):
        kept[...] = nn_dot(full[...], pick).astype(BF16)

    def field_to_rows(read, out_ref):
        parts = []
        for g in range(group):
            bx, bz = g // bz_n, g % bz_n
            parts.append(read(bx, bz).reshape(slab, lanes))
        for j, rows in enumerate(swap_bits(parts, lane64)):
            out_ref[pl.ds(j, slab, stride=BE), :] = rows

    takes[6].wait()
    field_to_rows(
        lambda bx, bz: rs_ref[bx * BE : (bx + 1) * BE, bz * BE : (bz + 1) * BE, :], src
    )

    has = {"xl": mc > 0, "xh": mc < nc - 1, "zl": mf > 0, "zh": mf < nf - 1}
    cell = lax.broadcasted_iota(jnp.int32, (slab, lanes), 0)
    zc = (cell // BE).astype(F32) + 0.5
    yc = (cell % BE).astype(F32) + 0.5
    slots = part * cap
    deep = BE // 2
    xbase = jnp.where(lane8[0:1, :] < slots, 0.5, 0.5 + deep)

    for far in range(2):
        handed = precv.at[pl.ds(0, part - 1 + far)]
        pltpu.make_async_copy(handed, handed, precv_sem.at[far]).wait()
        for c in range(part):
            value = precv[bases[far] + c]
            for h in range(2):
                pt[h * slots + c * cap : h * slots + (c + 1) * cap, :] = value
        got = pt[...]
        hot = jnp.where(colf[0:slots, :] == got[0:slots, 7:8], 1.0, 0.0).astype(BF16)
        for h in range(2):
            a = (2 * far + h) * slots
            spread[a : a + slots, h * lanes : (h + 1) * lanes] = hot
        pt[...] = got.T
        for m in range(SEG):
            dy = yc - pt[m * 8 + 1 : m * 8 + 2, :]
            dz = zc - pt[m * 8 + 2 : m * 8 + 3, :]
            dyz[m] = (dy * dy + dz * dz) + 0.25

        def build(i, _):
            xc = i.astype(F32) + xbase
            for h in range(2):
                lo_row = h * half
                near = ws = vx = vy = vz = None
                for m in range(SEG):
                    dx = xc - pt[m * 8 : m * 8 + 1, :]
                    e = dyz[m, lo_row : lo_row + half, :] + dx * dx
                    signed = e * lax.rsqrt(e) - pt[m * 8 + 6 : m * 8 + 7, :]
                    a = pl.reciprocal(e + 0.75, approx=True)
                    ax = a * pt[m * 8 + 3 : m * 8 + 4, :]
                    ay = a * pt[m * 8 + 4 : m * 8 + 5, :]
                    az = a * pt[m * 8 + 5 : m * 8 + 6, :]
                    if m == 0:
                        near, ws, vx, vy, vz = signed, a, ax, ay, az
                    else:
                        near = jnp.minimum(near, signed)
                        ws, vx, vy, vz = ws + a, vx + ax, vy + ay, vz + az
                ind = 0.5 - 0.5 * jnp.tanh(near)
                scale = ind / ws
                base = pl.multiple_of(i * slab + lo_row, half)
                for c, value in enumerate((ind, vx * scale, vy * scale, vz * scale)):
                    paid[c, pl.ds(base, half), far * lanes : (far + 1) * lanes] = value.astype(BF16)
            return 0

        lax.fori_loop(0, deep, build, 0)

    for c in range(4):
        summed = nn_dot(paid[c], spread[...]).astype(BF16).astype(F32)
        ob[c, 0 : deep * slab, :] = summed[:, :lanes]
        ob[c, deep * slab :, :] = summed[:, lanes:]
    diag[...] = 6.0 + PENALTY * ob[0]
    src[...] = src[...] - ((ob[1] + ob[2]) + ob[3])

    bz8 = lane8 % bz_n
    bx8 = (lane8 // bz_n) % bx_n
    bx64 = (lane64 // bz_n) % bx_n
    bx32 = (lane32 // bz_n) % bx_n
    bz32 = lane32 % bz_n
    tiles = BE // bz_n

    def turn(x, shift):
        shift = shift % lanes
        return x if shift == 0 else pltpu.roll(x, shift, axis=1)

    def load(value):
        vh = value.astype(BF16)
        rhs[:, :lanes] = vh
        rhs[:, lanes:] = (value - vh.astype(F32)).astype(BF16)

    def product(a, b):
        both = nn_dot(mh[a:b, :], rhs[...])
        return (both[:, :lanes] + both[:, lanes:]) + nn_dot(ml[a:b, :], rhs[:, :lanes])

    def face_low(f, i):
        if i == 0:
            return f[0:BE]
        if i == BE - 1:
            return f[slab : slab + BE]
        a = 2 * slab + (i - 1) * BE
        return f[a : a + BE]

    def face_high(f, i):
        if i == 0:
            return f[slab - BE : slab]
        if i == BE - 1:
            return f[2 * slab - BE : 2 * slab]
        a = 2 * slab + BE * (BE - 2) + (i - 1) * BE
        return f[a : a + BE]

    def pack_x(f):
        f0, f7 = f[:slab], f[slab : 2 * slab]
        low = jnp.where(bx32 == 0, f0[:half], turn(f0[half:], bz_n))
        high = jnp.where(bx32 == 0, turn(f7[:half], -bz_n), f7[half:])
        return low, high

    def pack_z(f):
        lows, highs = [], []
        for t in range(tiles):
            lowp = highp = None
            for a in range(bz_n):
                lo = turn(face_low(f, t * bz_n + a), a)
                hg = turn(face_high(f, t * bz_n + a), a - (bz_n - 1))
                lowp = lo if a == 0 else jnp.where(bz8 == a, lo, lowp)
                highp = hg if a == 0 else jnp.where(bz8 == a, hg, highp)
            lows.append(lowp)
            highs.append(highp)
        return jnp.concatenate(lows, axis=0), jnp.concatenate(highs, axis=0)

    def spread_x(got_low, got_high):
        at_low = [jnp.where(bx32 == 0, p, 0.0) for p in (got_low, turn(got_low, -bz_n))]
        at_high = [
            jnp.where(bx32 == bx_n - 1, p, 0.0) for p in (turn(got_high, bz_n), got_high)
        ]
        return at_low, at_high

    def spread_z(got_low, got_high):
        at_low, at_high = [], []
        for i in range(BE):
            t, a = i // bz_n, i % bz_n
            gl, gh = got_low[t * BE : (t + 1) * BE], got_high[t * BE : (t + 1) * BE]
            at_low.append(jnp.where(bz8 == 0, turn(gl, -a), 0.0))
            at_high.append(jnp.where(bz8 == bz_n - 1, turn(gh, bz_n - 1 - a), 0.0))
        return at_low, at_high

    def take_off(ref, xl, xh, zl, zh):
        at_low, at_high = spread_x(xl, xh)
        for h in range(2):
            a, b = h * half, cells - slab + h * half
            ref[a : a + half, :] = ref[a : a + half, :] - at_low[h]
            ref[b : b + half, :] = ref[b : b + half, :] - at_high[h]
        at_low, at_high = spread_z(zl, zh)
        for i in range(BE):
            a, b = i * slab, (i + 1) * slab - BE
            ref[a : a + BE, :] = ref[a : a + BE, :] - at_low[i]
            ref[b : b + BE, :] = ref[b : b + BE, :] - at_high[i]

    def ring_part(ring, at, xl, xh, zl, zh):
        low, high = spread_x(xl, xh)
        zlow, zhigh = spread_z(zl, zh)
        low, high = jnp.concatenate(low, axis=0), jnp.concatenate(high, axis=0)
        outer = []
        for rows, i in ((low, 0), (high, BE - 1)):
            outer += [rows[:BE] + zlow[i], rows[BE : slab - BE], rows[slab - BE :] + zhigh[i]]
        part = jnp.concatenate(outer + zlow[1:-1] + zhigh[1:-1], axis=0)
        hi = part.astype(BF16)
        low_at = ring.shape[1] // 2 + at
        ring[0:faces, at : at + lanes] = hi
        ring[0:faces, low_at : low_at + lanes] = (part - hi.astype(F32)).astype(BF16)

    for part in (own, ring):
        part[faces:, :] = jnp.zeros((wide - faces, part.shape[1]), BF16)

    def stencil(v_ref, out_ref):
        v0 = v_ref[0:slab, :]
        v7 = v_ref[cells - slab : cells, :]
        for i in range(BE):
            v = v_ref[i * slab : (i + 1) * slab, :]
            if i > 0:
                beside = v_ref[(i - 1) * slab : i * slab, :]
            else:
                beside = jnp.where(bx64 > 0, turn(v7, bz_n), 0.0)
            if i < BE - 1:
                beside = beside + v_ref[(i + 1) * slab : (i + 2) * slab, :]
            else:
                beside = beside + jnp.where(bx64 < bx_n - 1, turn(v0, -bz_n), 0.0)
            rows = []
            for k in range(BE):
                t = v[k * BE : (k + 1) * BE, :]
                if k > 0:
                    s = v[(k - 1) * BE : k * BE, :]
                else:
                    s = jnp.where(bz8 > 0, turn(v[slab - BE :, :], 1), 0.0)
                if k < BE - 1:
                    s = s + v[(k + 1) * BE : (k + 2) * BE, :]
                else:
                    s = s + jnp.where(bz8 < bz_n - 1, turn(v[:BE, :], -1), 0.0)
                down = pltpu.roll(t, 1, axis=0)
                edge = jnp.where(lane8 < group, 0.0, turn(down, group))
                s = s + jnp.where(sub8 == 0, edge, down)
                up = pltpu.roll(t, BE - 1, axis=0)
                edge = jnp.where(lane8 >= lanes - group, 0.0, turn(up, -group))
                s = s + jnp.where(sub8 == BE - 1, edge, up)
                rows.append(s)
            beside = beside + jnp.concatenate(rows, axis=0)
            out_ref[i * slab : (i + 1) * slab, :] = (
                diag[i * slab : (i + 1) * slab, :] * v - beside
            )

    def store(ref, f):
        for (a, b), c in zip(pieces, starts):
            if c < faces:
                ref[a:b, :] = f[c : c + b - a]

    starts = []
    for a, b in pieces:
        starts.append(starts[-1] + size if starts else 0)
        size = b - a

    def store_rest(ref, f):
        for (a, b), c in zip(pieces, starts):
            if c >= faces:
                ref[a:b, :] = f[c - faces : c - faces + b - a]

    ways = {
        "xl": (0, -1), "xh": (0, 1), "zl": (-1, 0), "zh": (1, 0),
        "xlzl": (-1, -1), "xhzl": (-1, 1), "xhzh": (1, 1), "xlzh": (1, -1),
    }
    zrows = tiles * BE
    span = half + zrows
    first_rows = {
        "xl": (0, half), "zl": (half, zrows), "xh": (span, half), "zh": (span + half, zrows),
    }
    order = ("xlzl", "xhzl", "xhzh", "xlzh", "xl", "xh", "zl", "zh")
    back = {"xl": "xh", "xh": "xl", "zl": "zh", "zh": "zl"}

    def opposite(key):
        return back[key[:2]] + back[key[2:]] if len(key) == 4 else back[key]

    def device(key):
        df, dc = ways[key]
        return lax.rem(mf + df + nf, nf), lax.min(lax.max(mc + dc, 0), nc - 1)

    groups = {"xl": ("xlzl", "xlzh", "xl"), "xh": ("xhzl", "xhzh", "xh"), "z": ("zl", "zh")}
    number = {key: n for n, keys in enumerate(groups.values()) for key in keys}

    def face_copy(e, key):
        if len(key) == 4:
            source = csend.at[e, order.index(key)]
            target = ydiag.at[e, order.index(opposite(key))]
        else:
            source = ysend.at[e, pl.ds(*first_rows[key])]
            target = (yz if key[0] == "z" else yx).at[e, int(key[1] == "l")]
        return pltpu.make_async_remote_copy(
            src_ref=source,
            dst_ref=target,
            send_sem=ysend_sem.at[e, number[key]],
            recv_sem=yrecv_sem.at[e, number[key]],
            device_id=device(key),
            device_id_type=MESH,
        )

    def second_copy(e, key):
        side = int(key[1] == "h")
        return pltpu.make_async_remote_copy(
            src_ref=(gsz if key[0] == "z" else gsx).at[e, side],
            dst_ref=(gz if key[0] == "z" else gx).at[e, 1 - side],
            send_sem=gsend_sem.at[e, number[key]],
            recv_sem=grecv_sem.at[e, number[key]],
            device_id=device(key),
            device_id_type=MESH,
        )

    def start_all(copies):
        for copy in copies:
            copy.start()

    def start_group(copy, e, x_only=False):
        for side in ("xl", "xh"):
            keys = [side] if x_only else groups[side]
            pl.when(has[side])(functools.partial(start_all, [copy(e, k) for k in keys]))
        start_all([copy(e, k) for k in groups["z"]])

    def wait_bytes(ref, sem):
        pltpu.make_async_copy(ref, ref, sem).wait()

    def wait_group(e, sems, x_bytes, z_bytes, received):
        for n, side in enumerate(("xl", "xh")):
            cond = has[back[side]] if received else has[side]
            pl.when(cond)(functools.partial(wait_bytes, x_bytes, sems.at[e, n]))
        wait_bytes(z_bytes, sems.at[e, 2])

    def keep(cond, value):
        return jnp.where(cond, value, 0.0)

    def corner_at(key):
        return (bz_n - 1) * (key[3] == "h"), (bx_n - 1) * (key[1] == "h")

    def corner_pack(xp, zp, bz, bx):
        px = pz = None
        for g in range(half // BE):
            piece = turn(xp[g * BE : (g + 1) * BE], g - bz)
            px = piece if g == 0 else jnp.where(bz8 == g, piece, px)
        for t in range(tiles):
            piece = turn(zp[t * BE : (t + 1) * BE], (t - bx) * bz_n)
            pz = piece if t == 0 else jnp.where(bx8 == t, piece, pz)
        return jnp.concatenate([px, pz], axis=0)

    def corner_open(p, bz, bx):
        px, pz = p[:BE], p[BE:]
        return (
            jnp.concatenate([turn(px, bz - g) for g in range(half // BE)], axis=0),
            jnp.concatenate([turn(pz, (bx - t) * bz_n) for t in range(tiles)], axis=0),
        )

    def twice(e, p_ref, first_ref, image_ref, second_ref, out_ref, during, ahead=None):
        load(p_ref[...])
        f = product(0, faces)
        xl, xh = pack_x(f)
        zl, zh = pack_z(f)
        for key, value in (("xl", xl), ("zl", zl), ("xh", xh), ("zh", zh)):
            a, size = first_rows[key]
            ysend[e, a : a + size, :] = value
        for n, key in enumerate(order[:4]):
            csend[e, n] = corner_pack(
                {"xl": xl, "xh": xh}[key[:2]], {"zl": zl, "zh": zh}[key[2:]], *corner_at(key)
            )
        start_group(face_copy, e)
        store(first_ref, f)
        store_rest(first_ref, product(faces, cells))
        stencil(first_ref, image_ref)
        load(image_ref[...])
        g = product(0, faces)
        packed_x, packed_z = pack_x(g), pack_z(g)
        for n in range(2):
            gsx[e, n] = packed_x[n]
            gsz[e, n] = packed_z[n]
        start_group(second_copy, e, True)
        store(second_ref, g)
        store_rest(second_ref, product(faces, cells))
        during()
        wait_group(e, yrecv_sem, csend.at[e], yz.at[e], True)
        first = (
            keep(has["xl"], yx[e, 0]), keep(has["xh"], yx[e, 1]),
            keep(has["zl"], yz[e, 0]), keep(has["zh"], yz[e, 1]),
        )
        ring_part(own, 0, *first)
        both = nn_dot(fh[...], own[...])
        change = (both[:, :lanes] + both[:, lanes:]) + nn_dot(fl[...], own[:, :lanes])
        for (a, b), c in zip(pieces, starts):
            second_ref[a:b, :] = second_ref[a:b, :] - change[c : c + b - a]

        def corner(key):
            return corner_open(ydiag[e, order.index(key)], *corner_at(opposite(key)))

        (llx, llz), (hlx, hlz), (hhx, hhz), (lhx, lhz) = (corner(k) for k in order[:4])
        bxz = jnp.concatenate([bx8] * tiles, axis=0)
        lowx, highx = has["xl"], has["xh"]

        def by_x(high, low):
            return jnp.where(bxz == 0, keep(highx, high), keep(lowx, low))

        def by_z(low, high):
            low = jnp.where(bz32 == 0, keep(has["zh"], high), 0.0) + jnp.where(
                bz32 == bz_n - 1, keep(has["zl"], low), 0.0
            )
            return low

        ring_part(
            ring, 0, ysend[e, span : span + half, :], ysend[e, 0:half, :],
            keep(has["zl"], by_x(hlz, llz)), keep(has["zh"], by_x(hhz, lhz)),
        )
        ring_part(
            ring, lanes, keep(lowx, by_z(llx, lhx)), keep(highx, by_z(hlx, hhx)),
            ysend[e, span + half : 2 * span, :], ysend[e, half : span, :],
        )
        count = ring.shape[1] // 2
        both = nn_dot(fh[0:faces, :], ring[...])
        full = (both[:, :count] + both[:, count:]) + nn_dot(fl[0:faces, :], ring[:, :count])
        cxl, cxh = pack_x(full[:, :lanes])
        czl, czh = pack_z(full[:, lanes:])
        stencil(second_ref, out_ref)
        take_off(image_ref, *first)
        if ahead is not None:
            ahead()
        wait_group(e, grecv_sem, gx.at[e, 0], gz.at[e], True)
        take_off(
            out_ref,
            keep(has["xl"], gx[e, 0] - cxh),
            keep(has["xh"], gx[e, 1] - cxl),
            keep(has["zl"], gz[e, 0] - czh),
            keep(has["zh"], gz[e, 1] - czl),
        )

    def gram(pairs):
        total = [None] * len(pairs)
        for i in range(BE):
            read = {}
            for p in pairs:
                for ref in p:
                    if id(ref) not in read:
                        read[id(ref)] = ref[i * slab : (i + 1) * slab, :]
            for n, (a, b) in enumerate(pairs):
                part = jnp.sum((read[id(a)] * read[id(b)]).reshape(BE, BE, lanes), axis=0)
                total[n] = part if i == 0 else total[n] + part
        return [jnp.sum(t, axis=0, keepdims=True) for t in total]

    def show_obstacle():
        for c in range(4):
            def write(x, plane, c=c):
                obf[c, x] = plane.astype(BF16)

            rows_to_field(
                lambda j, c=c: ob[c, pl.ds(j, slab, stride=BE), :], write, bx_n, bz_n, lane64
            )

    basis = (src, v1, w1, u1, x1)
    known = [(a, b) for a in range(3) for b in range(a, 3)]
    late = [(a, b) for b in (3, 4) for a in range(b + 1)]
    ready = []

    def ahead():
        ready.extend(sums_of(late[:4]))

    me = mf * nc + mc

    few = everyone <= 64 and nf & (nf - 1) == 0 and nc & (nc - 1) == 0

    def flips(me, count):
        out = []
        for mask in range(count if few else 0):
            to, bit = me, 1
            while bit <= mask:
                if mask & bit:
                    to = to + bit - 2 * bit * lax.rem(me // bit, 2)
                bit *= 2
            out.append(to)
        return out

    flip_fish, flip_curve = flips(mf, nf), flips(mc, nc)
    far_first = sorted(
        ((a, b) for a in range(len(flip_fish)) for b in range(len(flip_curve)) if a or b),
        key=lambda m: -(m[0] // 2 + m[1] % 2 + m[1] // 2),
    )

    def sums_of(pairs):
        return gram([(basis[a], basis[b]) for a, b in pairs])

    def tell(no, lines):
        number = -(-len(lines) // 8) * 8
        lines += [jnp.zeros((1, lanes), F32)] * (number - len(lines))
        tile = jnp.sum(jnp.concatenate(lines, axis=0), axis=1, keepdims=True)
        spot = lax.broadcasted_iota(jnp.int32, (number, lanes), 0) == lax.broadcasted_iota(
            jnp.int32, (number, lanes), 1
        )
        red[no, me] = jnp.sum(jnp.where(spot, tile, 0.0), axis=0, keepdims=True)

        def send(to_fish, to_curve):
            pltpu.make_async_remote_copy(
                src_ref=red.at[no, me],
                dst_ref=red.at[no, me],
                send_sem=rsend_sem.at[no],
                recv_sem=rrecv_sem.at[no],
                device_id=(to_fish, to_curve),
                device_id_type=MESH,
            ).start()

        if few:
            for a, b in far_first:
                send(flip_fish[a], flip_curve[b])
        else:

            def body(k, _):
                send(lax.rem(mf + k // nc, nf), lax.rem(mc + k, nc))
                return 0

            lax.fori_loop(1, everyone, body, 0)

    def hear(no, pairs):
        heard = red.at[no, pl.ds(0, everyone - 1)]
        pltpu.make_async_copy(heard, heard, rrecv_sem.at[no]).wait()
        row = jnp.sum(red[no], axis=0)
        return dict(zip(pairs, entries(row, len(pairs))))

    def show(ref, out):
        def write(x, plane):
            out[x] = plane

        rows_to_field(lambda j: ref[pl.ds(j, slab, stride=BE), :], write, bx_n, bz_n, lane64)

    twice(0, src, y1, v1, m1, w1, show_obstacle)
    twice(1, w1, n1, u1, q1, x1, lambda: tell(0, sums_of(known)), ahead)
    tell(1, ready + sums_of(late[4:]))
    sums = hear(0, known)
    scalars = first_scalars(sums)
    for ref, out in (
        (src, rfield), (v1, vfield), (w1, wfield), (u1, ufield), (x1, xfield),
        (y1, yfield), (m1, mfield), (n1, nfield), (q1, qfield),
    ):
        show(ref, out)
    wait_bytes(precv.at[pl.ds(0, nc - 1)], psend_sem)
    for e in range(2):
        wait_group(e, ysend_sem, csend.at[e], yz.at[e], False)
        wait_group(e, gsend_sem, gx.at[e, 0], gz.at[e], False)
    sums.update(hear(1, late))
    resid, press = coefficients(sums, scalars)
    for first, coefs in ((0, resid), (8, press)):
        for k, coef in enumerate(coefs):
            coef_ref[first + k : first + k + 1, :] = jnp.broadcast_to(coef, (1, lanes))
    for no in range(2):
        heard = red.at[no, pl.ds(0, everyone - 1)]
        pltpu.make_async_copy(heard, heard, rsend_sem.at[no]).wait()


def local(right_side, block_inverse, midline, entry_fish, entry_seg, entry_dest, entry_block):
    nf, nc = lax.axis_size("fish"), lax.axis_size("curve")
    count = entry_fish.shape[0]
    cap = max(2, 2 * count // nc)
    cx, cz, ny = right_side.shape
    lanes = (cx // BE) * (cz // BE) * (ny // BE)
    cells = BE**3
    slab = BE * BE
    half = slab // 2
    zrows = BE // (cz // BE) * BE
    span = half + zrows
    wide = 4 * slab
    rows, fishes, npts = midline.shape
    width = fishes * npts
    vmem = pl.BlockSpec(memory_space=pltpu.VMEM)
    big = pltpu.VMEM((cells, lanes), F32)
    dma = pltpu.SemaphoreType.DMA
    anywhere = pl.BlockSpec(memory_space=pl.ANY)
    field = jax.ShapeDtypeStruct((cx, cz, ny), F32)
    fields = jax.ShapeDtypeStruct((4, cx, cz, ny), BF16)
    solved = pl.pallas_call(
        functools.partial(kernel, nf, nc, cap, npts),
        out_shape=(
            (pltpu.VMEM((16, lanes), F32),)
            + (pltpu.VMEM((cx, cz, ny), F32),) * 9
            + (pltpu.VMEM((4, cx, cz, ny), BF16),)
        ),
        in_specs=[anywhere] * 7,
        out_specs=(vmem,) * 11,
        scratch_shapes=[big] * 9
        + [
            pltpu.VMEM((cx, cz, ny), F32),
            pltpu.VMEM((cells, cells), F32),
            pltpu.VMEM((rows, fishes, npts), F32),
            pltpu.VMEM((4, 1, count), jnp.int32),
            dma((4,)),
            pltpu.VMEM((cells, cells), BF16),
            pltpu.VMEM((cells, cells), BF16),
            pltpu.VMEM((cells, wide), BF16),
            pltpu.VMEM((cells, wide), BF16),
            pltpu.VMEM((cells, 2 * lanes), BF16),
            pltpu.VMEM((wide, 2 * lanes), BF16),
            pltpu.VMEM((wide, 4 * lanes), BF16),
            pltpu.VMEM((8, lanes), F32),
            pltpu.VMEM((8, width), F32),
            pltpu.VMEM((SEG * 8, width), F32),
            pltpu.VMEM((nc, cap, lanes), F32),
            pltpu.VMEM((nc, cap, lanes), F32),
            pltpu.VMEM((SEG * 8, lanes), F32),
            pltpu.VMEM((SEG, slab, lanes), F32),
            pltpu.VMEM((4, cells // 2, 2 * lanes), BF16),
            pltpu.VMEM((2 * lanes, 2 * lanes), BF16),
            pltpu.VMEM((4, cells, lanes), F32),
            big,
            pltpu.VMEM((2, 2 * span, lanes), F32),
            pltpu.VMEM((2, 4, 2 * BE, lanes), F32),
            pltpu.VMEM((2, 2, half, lanes), F32),
            pltpu.VMEM((2, 2, zrows, lanes), F32),
            pltpu.VMEM((2, 4, 2 * BE, lanes), F32),
            pltpu.VMEM((2, 2, half, lanes), F32),
            pltpu.VMEM((2, 2, zrows, lanes), F32),
            pltpu.VMEM((2, 2, half, lanes), F32),
            pltpu.VMEM((2, 2, zrows, lanes), F32),
            pltpu.VMEM((2, nf * nc, 1, lanes), F32),
            dma,
            dma((2,)),
            dma((2, 3)),
            dma((2, 3)),
            dma((2, 3)),
            dma((2, 3)),
            dma((2,)),
            dma((2,)),
        ],
        compiler_params=pltpu.CompilerParams(
            collective_id=0, has_side_effects=True, vmem_limit_bytes=VMEM_LIMIT
        ),
    )(
        *(
            pltpu.with_memory_space_constraint(a, pltpu.HBM)
            for a in (
                right_side,
                block_inverse,
                midline,
                *(e.reshape(1, count) for e in (entry_fish, entry_seg, entry_dest, entry_block)),
            )
        )
    )
    return pl.pallas_call(
        finish,
        out_shape=(field, field, fields),
        in_specs=[vmem] * 11,
        out_specs=(anywhere,) * 3,
        scratch_shapes=[
            pltpu.VMEM((cx, cz, ny), F32),
            pltpu.VMEM((cx, cz, ny), F32),
            dma,
            dma((2, 4)),
        ],
        compiler_params=pltpu.CompilerParams(vmem_limit_bytes=VMEM_LIMIT),
    )(*(pltpu.with_memory_space_constraint(a, pltpu.VMEM) for a in solved))


def solution(mesh):
    return jax.shard_map(
        local,
        mesh=mesh,
        in_specs=(
            P("curve", "fish", None),
            P(),
            P(None, "fish", None),
            P(("fish", "curve")),
            P(("fish", "curve")),
            P(("fish", "curve"), None),
            P(("fish", "curve")),
        ),
        out_specs=(
            P("curve", "fish", None),
            P("curve", "fish", None),
            P(None, "curve", "fish", None),
        ),
        check_vma=False,
    )
```

```python
import functools
import jax
import jax.numpy as jnp
from jax import lax
from jax.experimental import pallas as pl
from jax.experimental.pallas import tpu as pltpu
from jax.sharding import PartitionSpec as P

BE = 8
SEG = 16
PENALTY = 4.0
F32 = jnp.float32
BF16 = jnp.bfloat16
MESH = pl.DeviceIdType.MESH


def nt_dot(a, b):
    return lax.dot_general(a, b, (((1,), (1,)), ((), ())), preferred_element_type=F32)


def nn_dot(a, b):
    return lax.dot_general(a, b, (((1,), (0,)), ((), ())), preferred_element_type=F32)


def split3(x):
    hi = x.astype(BF16)
    rest = x - hi.astype(F32)
    mid = rest.astype(BF16)
    low = (rest - mid.astype(F32)).astype(BF16)
    return hi, mid, low


def swap_bits(arrays, lane):
    arrays = list(arrays)
    lanes = lane.shape[-1]
    for step in (4, 2, 1):
        clear = (lane & step) == 0
        for a in range(8):
            if a & step:
                continue
            low, high = arrays[a], arrays[a | step]
            arrays[a] = jnp.where(clear, low, pltpu.roll(high, step, axis=1))
            arrays[a | step] = jnp.where(clear, pltpu.roll(low, lanes - step, axis=1), high)
    return arrays


def rows_to_field(read_j, write, bx_n, bz_n, lane):
    parts = swap_bits([read_j(j) for j in range(BE)], lane)
    for bx in range(bx_n):
        for i in range(BE):
            plane = jnp.concatenate(
                [parts[bx * bz_n + bz][i * BE : (i + 1) * BE, :] for bz in range(bz_n)], axis=0
            )
            write(bx * BE + i, plane)


VMEM_LIMIT = 40 * 1024 * 1024


def finish(
    coef_ref, r_ref, v_ref, w_ref, u_ref, x_ref, y_ref, m_ref, n_ref, q_ref, oin_ref,
    press_ref, resid_ref, obst_ref, pf, rf, osem, sems,
):
    give = pltpu.make_async_copy(oin_ref, obst_ref, osem)
    give.start()
    chunks = sems.shape[1]
    size = rf.shape[0] // chunks
    outs = []
    for c in range(chunks):
        part = pl.ds(c * size, size)
        for n, (out, dst, basis, first) in enumerate(
            (
                (rf, resid_ref, (r_ref, v_ref, w_ref, u_ref, x_ref), 0),
                (pf, press_ref, (y_ref, m_ref, n_ref, q_ref), 8),
            )
        ):
            total = None
            for k, ref in enumerate(basis):
                term = ref[part]
                if first or k:
                    term = coef_ref[first + k : first + k + 1, :] * term
                total = term if total is None else total + term
            out[part] = total
            copy = pltpu.make_async_copy(out.at[part], dst.at[part], sems.at[n, c])
            copy.start()
            outs.append(copy)
    for copy in outs:
        copy.wait()
    give.wait()


def entries(row, count):
    lane = lax.broadcasted_iota(jnp.int32, row.shape, 1)
    return [
        jnp.sum(jnp.where(lane == k, row, 0.0), axis=1, keepdims=True) for k in range(count)
    ]


def first_scalars(gram):
    rr, rv, vv, vw, ww, rw = (gram[k] for k in ((0, 0), (0, 1), (1, 1), (1, 2), (2, 2), (0, 2)))
    alpha = rr / rv
    ts = (rv - alpha * vv) - alpha * (rw - alpha * vw)
    tt = (vv - alpha * vw) - alpha * (vw - alpha * ww)
    omega = ts / tt
    rho2 = (rr - alpha * rv) - omega * (rv - alpha * rw)
    beta = rho2 / rr * (alpha / omega)
    both, prod = alpha + omega, alpha * omega
    d0, d1, d2 = 1.0 + beta, -(both + beta * omega), prod
    return rho2, both, prod, d0, d1, d2, d0 * rv + d1 * rw


def coefficients(gram, scalars):
    rho2, both, prod, d0, d1, d2, known = scalars
    gram = {**gram, **{(b, a): g for (a, b), g in gram.items()}}
    alpha2 = rho2 / (known + d2 * gram[0, 3])
    s1, s2, s3 = -both - alpha2 * d0, prod - alpha2 * d1, -alpha2 * d2
    ts = tt = None
    for a, sa in ((1, None), (2, s1), (3, s2), (4, s3)):
        q = (gram[a, 0] + s1 * gram[a, 1]) + (s2 * gram[a, 2] + s3 * gram[a, 3])
        z = (gram[a, 1] + s1 * gram[a, 2]) + (s2 * gram[a, 3] + s3 * gram[a, 4])
        ts = q if sa is None else ts + sa * q
        tt = z if sa is None else tt + sa * z
    omega2 = ts / tt
    resid = (omega2, s1 - omega2, s2 - omega2 * s1, s3 - omega2 * s2, -omega2 * s3)
    press = (
        both + alpha2 * d0 + omega2,
        alpha2 * d1 - prod + omega2 * s1,
        alpha2 * d2 + omega2 * s2,
        omega2 * s3,
    )
    return resid, press


def kernel(
    nf, nc, cap, npts,
    rs_hbm, inv_hbm, mid_hbm, fish_hbm, seg_hbm, dest_hbm, block_hbm,
    coef_ref, rfield, vfield, wfield, ufield, xfield, yfield, mfield, nfield, qfield, obf,
    src, v1, w1, u1, x1, y1, m1, n1, q1, rs_ref, inv_ref, mid_ref, ent_ref, in_sem,
    mh, ml, fh, fl, rhs, own, ring, meta_ref, tab, shifted, psend, precv, pt, dyz, paid, spread, ob, diag,
    ysend, csend, yx, yz, ydiag, gsx, gsz, gx, gz, red,
    psend_sem, precv_sem, ysend_sem, yrecv_sem, gsend_sem, grecv_sem, rsend_sem, rrecv_sem,
):
    mf = lax.axis_index("fish")
    mc = lax.axis_index("curve")
    cells, lanes = src.shape
    slab = BE * BE
    half = slab // 2
    bx_n = rs_ref.shape[0] // BE
    bz_n = rs_ref.shape[1] // BE
    group = bx_n * bz_n
    everyone = nf * nc

    barrier = pltpu.get_barrier_semaphore()

    def greet_fish(k, _):
        pl.semaphore_signal(
            barrier, inc=1, device_id=(lax.rem(mf + k, nf), mc), device_id_type=MESH
        )
        return 0

    def greet_curve(k, _):
        pl.semaphore_signal(
            barrier, inc=1, device_id=(mf, lax.rem(mc + k, nc)), device_id_type=MESH
        )
        return 0

    lax.fori_loop(1, nc, greet_curve, 0)
    lax.fori_loop(1, nf, greet_fish, 0)

    takes = [
        pltpu.make_async_copy(a, b, in_sem.at[max(n - 3, 0)])
        for n, (a, b) in enumerate(
            [(a, ent_ref.at[k]) for k, a in enumerate((fish_hbm, seg_hbm, dest_hbm, block_hbm))]
            + [(mid_hbm, mid_ref), (inv_hbm, inv_ref), (rs_hbm, rs_ref)]
        )
    ]
    for copy in takes:
        copy.start()

    lane8 = lax.broadcasted_iota(jnp.int32, (BE, lanes), 1)
    lane64 = lax.broadcasted_iota(jnp.int32, (slab, lanes), 1)
    lane32 = lax.broadcasted_iota(jnp.int32, (half, lanes), 1)
    sub8 = lax.broadcasted_iota(jnp.int32, (BE, lanes), 0)
    col = lax.broadcasted_iota(jnp.int32, (lanes, lanes), 1)
    row = lax.broadcasted_iota(jnp.int32, (lanes, lanes), 0)
    colf, rowf = col.astype(F32), row.astype(F32)

    pltpu.make_async_copy(ent_ref, ent_ref, in_sem.at[0]).wait()
    takes[4].wait()
    nyb = rs_ref.shape[2] // BE
    count = ent_ref.shape[2]
    rows, fishes, _ = mid_ref.shape
    width = tab.shape[1]
    block = ent_ref[3]
    place_in = block % nyb * group + block // nyb + 1
    meta_ref[...] = jnp.full_like(meta_ref, -1.0)
    for r, column in enumerate((ent_ref[0], ent_ref[1], ent_ref[2], place_in)):
        meta_ref[r : r + 1, 0:count] = column.astype(F32)
    for f in range(fishes):
        tab[0:rows, f * npts : (f + 1) * npts] = mid_ref[:, f, :]
    tab[rows:8, :] = jnp.zeros((8 - rows, width), F32)
    table = tab[...]
    for m in range(SEG):
        turned = table if m == 0 else pltpu.roll(table, width - m, axis=1)
        shifted[m * 8 : m * 8 + 8, :] = turned
    meta = meta_ref[...]
    owner = lax.broadcasted_iota(jnp.int32, (nc, lanes), 0).astype(F32)
    mine = owner == meta[2:3, :]
    earlier = jnp.where(row < col, 1.0, 0.0).astype(BF16)
    rank = nn_dot(jnp.where(mine, 1.0, 0.0).astype(BF16), earlier)
    slot = jnp.sum(jnp.where(mine, owner * cap + rank + 1.0, 0.0), axis=0, keepdims=True) - 1.0
    hot = jnp.where(rowf == slot, 1.0, 0.0).astype(BF16)
    picked = nt_dot(hot, meta.astype(BF16))
    index = picked[:, 0:1] * npts + picked[:, 1:2]
    place = picked[:, 3:4] - 1.0
    point_hot = jnp.where(
        lax.broadcasted_iota(jnp.int32, (lanes, width), 1).astype(F32) == index, 1.0, 0.0
    ).astype(BF16)
    hi, mid, low = split3(shifted[...])
    points = (nt_dot(point_hot, hi) + nt_dot(point_hot, mid)) + nt_dot(point_hot, low)
    points = jnp.where(col == 7, place, points)
    for c in range(nc):
        psend[c] = points[c * cap : (c + 1) * cap, :]

    pl.semaphore_wait(barrier, nf - 1 + nc - 1)

    part = nc // 2
    near = mc // part * part
    bases = (near, part - near)

    def hand_start(far):
        def body(k, _):
            to = bases[far] + lax.rem(mc - near + k, part)
            pltpu.make_async_remote_copy(
                src_ref=psend.at[to],
                dst_ref=precv.at[mc],
                send_sem=psend_sem,
                recv_sem=precv_sem.at[far],
                device_id=(mf, to),
                device_id_type=MESH,
            ).start()
            return 0

        lax.fori_loop(1 - far, part, body, 0)

    hand_start(0)
    hand_start(1)
    precv[mc] = psend[mc]
    spread[...] = jnp.zeros_like(spread)

    takes[5].wait()
    whole = inv_ref[...]
    top = jnp.max(jnp.max(jnp.abs(whole), axis=0, keepdims=True), axis=1, keepdims=True)
    scale = 1.0 / (slab * top)
    inner_k = slab - 2 * BE
    pieces = [(0, slab), (cells - slab, cells)]
    pieces += [(i * slab, i * slab + BE) for i in range(1, BE - 1)]
    pieces += [((i + 1) * slab - BE, (i + 1) * slab) for i in range(1, BE - 1)]
    pieces += [(i * slab + BE, (i + 1) * slab - BE) for i in range(1, BE - 1)]
    faces = 2 * slab + 2 * BE * (BE - 2)
    arranged = jnp.concatenate([inv_ref[a:b, :] for a, b in pieces], axis=0) * scale
    hi = arranged.astype(BF16)
    mh[...] = hi
    ml[...] = (arranged - hi.astype(F32)).astype(BF16)
    wide = fh.shape[1]
    cell = lax.broadcasted_iota(jnp.int32, (cells, wide), 0)
    face = lax.broadcasted_iota(jnp.int32, (1, wide), 1)
    side = (face - 2 * slab) // (BE * (BE - 2))
    deep = (face - 2 * slab) % (BE * (BE - 2))
    where_z = (deep // BE + 1) * slab + side * (slab - BE) + deep % BE
    where_x = face // slab * (cells - slab) + face % slab
    at = jnp.where(face < 2 * slab, where_x, jnp.where(face < faces, where_z, -1))
    pick = jnp.where(cell == at, 1.0, 0.0).astype(BF16)
    for full, kept in ((mh, fh), (ml, fl)):
        kept[...] = nn_dot(full[...], pick).astype(BF16)

    def field_to_rows(read, out_ref):
        parts = []
        for g in range(group):
            bx, bz = g // bz_n, g % bz_n
            parts.append(read(bx, bz).reshape(slab, lanes))
        for j, rows in enumerate(swap_bits(parts, lane64)):
            out_ref[pl.ds(j, slab, stride=BE), :] = rows

    takes[6].wait()
    field_to_rows(
        lambda bx, bz: rs_ref[bx * BE : (bx + 1) * BE, bz * BE : (bz + 1) * BE, :], src
    )

    has = {"xl": mc > 0, "xh": mc < nc - 1, "zl": mf > 0, "zh": mf < nf - 1}
    cell = lax.broadcasted_iota(jnp.int32, (slab, lanes), 0)
    zc = (cell // BE).astype(F32) + 0.5
    yc = (cell % BE).astype(F32) + 0.5
    slots = part * cap
    deep = BE // 2
    xbase = jnp.where(lane8[0:1, :] < slots, 0.5, 0.5 + deep)

    for far in range(2):
        handed = precv.at[pl.ds(0, part - 1 + far)]
        pltpu.make_async_copy(handed, handed, precv_sem.at[far]).wait()
        for c in range(part):
            value = precv[bases[far] + c]
            for h in range(2):
                pt[h * slots + c * cap : h * slots + (c + 1) * cap, :] = value
        got = pt[...]
        hot = jnp.where(colf[0:slots, :] == got[0:slots, 7:8], 1.0, 0.0).astype(BF16)
        for h in range(2):
            a = (2 * far + h) * slots
            spread[a : a + slots, h * lanes : (h + 1) * lanes] = hot
        pt[...] = got.T
        for m in range(SEG):
            dy = yc - pt[m * 8 + 1 : m * 8 + 2, :]
            dz = zc - pt[m * 8 + 2 : m * 8 + 3, :]
            dyz[m] = (dy * dy + dz * dz) + 0.25

        def build(i, _):
            xc = i.astype(F32) + xbase
            for h in range(2):
                lo_row = h * half
                near = ws = vx = vy = vz = None
                for m in range(SEG):
                    dx = xc - pt[m * 8 : m * 8 + 1, :]
                    e = dyz[m, lo_row : lo_row + half, :] + dx * dx
                    signed = e * lax.rsqrt(e) - pt[m * 8 + 6 : m * 8 + 7, :]
                    a = pl.reciprocal(e + 0.75, approx=True)
                    ax = a * pt[m * 8 + 3 : m * 8 + 4, :]
                    ay = a * pt[m * 8 + 4 : m * 8 + 5, :]
                    az = a * pt[m * 8 + 5 : m * 8 + 6, :]
                    if m == 0:
                        near, ws, vx, vy, vz = signed, a, ax, ay, az
                    else:
                        near = jnp.minimum(near, signed)
                        ws, vx, vy, vz = ws + a, vx + ax, vy + ay, vz + az
                ind = 0.5 - 0.5 * jnp.tanh(near)
                scale = ind / ws
                base = pl.multiple_of(i * slab + lo_row, half)
                for c, value in enumerate((ind, vx * scale, vy * scale, vz * scale)):
                    paid[c, pl.ds(base, half), far * lanes : (far + 1) * lanes] = value.astype(BF16)
            return 0

        lax.fori_loop(0, deep, build, 0, unroll=True)

    for c in range(4):
        summed = nn_dot(paid[c], spread[...]).astype(BF16).astype(F32)
        ob[c, 0 : deep * slab, :] = summed[:, :lanes]
        ob[c, deep * slab :, :] = summed[:, lanes:]
    diag[...] = 6.0 + PENALTY * ob[0]
    src[...] = src[...] - ((ob[1] + ob[2]) + ob[3])

    bz8 = lane8 % bz_n
    bx8 = (lane8 // bz_n) % bx_n
    bx64 = (lane64 // bz_n) % bx_n
    bx32 = (lane32 // bz_n) % bx_n
    bz32 = lane32 % bz_n
    tiles = BE // bz_n

    def turn(x, shift):
        shift = shift % lanes
        return x if shift == 0 else pltpu.roll(x, shift, axis=1)

    def load(value):
        vh = value.astype(BF16)
        rhs[:, :lanes] = vh
        rhs[:, lanes:] = (value - vh.astype(F32)).astype(BF16)

    def product(a, b):
        both = nn_dot(mh[a:b, :], rhs[...])
        return (both[:, :lanes] + both[:, lanes:]) + nn_dot(ml[a:b, :], rhs[:, :lanes])

    def face_low(f, i):
        if i == 0:
            return f[0:BE]
        if i == BE - 1:
            return f[slab : slab + BE]
        a = 2 * slab + (i - 1) * BE
        return f[a : a + BE]

    def face_high(f, i):
        if i == 0:
            return f[slab - BE : slab]
        if i == BE - 1:
            return f[2 * slab - BE : 2 * slab]
        a = 2 * slab + BE * (BE - 2) + (i - 1) * BE
        return f[a : a + BE]

    def pack_x(f):
        f0, f7 = f[:slab], f[slab : 2 * slab]
        low = jnp.where(bx32 == 0, f0[:half], turn(f0[half:], bz_n))
        high = jnp.where(bx32 == 0, turn(f7[:half], -bz_n), f7[half:])
        return low, high

    def pack_z(f):
        lows, highs = [], []
        for t in range(tiles):
            lowp = highp = None
            for a in range(bz_n):
                lo = turn(face_low(f, t * bz_n + a), a)
                hg = turn(face_high(f, t * bz_n + a), a - (bz_n - 1))
                lowp = lo if a == 0 else jnp.where(bz8 == a, lo, lowp)
                highp = hg if a == 0 else jnp.where(bz8 == a, hg, highp)
            lows.append(lowp)
            highs.append(highp)
        return jnp.concatenate(lows, axis=0), jnp.concatenate(highs, axis=0)

    def spread_x(got_low, got_high):
        at_low = [jnp.where(bx32 == 0, p, 0.0) for p in (got_low, turn(got_low, -bz_n))]
        at_high = [
            jnp.where(bx32 == bx_n - 1, p, 0.0) for p in (turn(got_high, bz_n), got_high)
        ]
        return at_low, at_high

    def spread_z(got_low, got_high):
        at_low, at_high = [], []
        for i in range(BE):
            t, a = i // bz_n, i % bz_n
            gl, gh = got_low[t * BE : (t + 1) * BE], got_high[t * BE : (t + 1) * BE]
            at_low.append(jnp.where(bz8 == 0, turn(gl, -a), 0.0))
            at_high.append(jnp.where(bz8 == bz_n - 1, turn(gh, bz_n - 1 - a), 0.0))
        return at_low, at_high

    def take_off(ref, xl, xh, zl, zh):
        at_low, at_high = spread_x(xl, xh)
        for h in range(2):
            a, b = h * half, cells - slab + h * half
            ref[a : a + half, :] = ref[a : a + half, :] - at_low[h]
            ref[b : b + half, :] = ref[b : b + half, :] - at_high[h]
        at_low, at_high = spread_z(zl, zh)
        for i in range(BE):
            a, b = i * slab, (i + 1) * slab - BE
            ref[a : a + BE, :] = ref[a : a + BE, :] - at_low[i]
            ref[b : b + BE, :] = ref[b : b + BE, :] - at_high[i]

    def ring_part(ring, at, xl, xh, zl, zh):
        low, high = spread_x(xl, xh)
        zlow, zhigh = spread_z(zl, zh)
        low, high = jnp.concatenate(low, axis=0), jnp.concatenate(high, axis=0)
        outer = []
        for rows, i in ((low, 0), (high, BE - 1)):
            outer += [rows[:BE] + zlow[i], rows[BE : slab - BE], rows[slab - BE :] + zhigh[i]]
        part = jnp.concatenate(outer + zlow[1:-1] + zhigh[1:-1], axis=0)
        hi = part.astype(BF16)
        low_at = ring.shape[1] // 2 + at
        ring[0:faces, at : at + lanes] = hi
        ring[0:faces, low_at : low_at + lanes] = (part - hi.astype(F32)).astype(BF16)

    for part in (own, ring):
        part[faces:, :] = jnp.zeros((wide - faces, part.shape[1]), BF16)

    def stencil(v_ref, out_ref):
        v0 = v_ref[0:slab, :]
        v7 = v_ref[cells - slab : cells, :]
        for i in range(BE):
            v = v_ref[i * slab : (i + 1) * slab, :]
            if i > 0:
                beside = v_ref[(i - 1) * slab : i * slab, :]
            else:
                beside = jnp.where(bx64 > 0, turn(v7, bz_n), 0.0)
            if i < BE - 1:
                beside = beside + v_ref[(i + 1) * slab : (i + 2) * slab, :]
            else:
                beside = beside + jnp.where(bx64 < bx_n - 1, turn(v0, -bz_n), 0.0)
            rows = []
            for k in range(BE):
                t = v[k * BE : (k + 1) * BE, :]
                if k > 0:
                    s = v[(k - 1) * BE : k * BE, :]
                else:
                    s = jnp.where(bz8 > 0, turn(v[slab - BE :, :], 1), 0.0)
                if k < BE - 1:
                    s = s + v[(k + 1) * BE : (k + 2) * BE, :]
                else:
                    s = s + jnp.where(bz8 < bz_n - 1, turn(v[:BE, :], -1), 0.0)
                down = pltpu.roll(t, 1, axis=0)
                edge = jnp.where(lane8 < group, 0.0, turn(down, group))
                s = s + jnp.where(sub8 == 0, edge, down)
                up = pltpu.roll(t, BE - 1, axis=0)
                edge = jnp.where(lane8 >= lanes - group, 0.0, turn(up, -group))
                s = s + jnp.where(sub8 == BE - 1, edge, up)
                rows.append(s)
            beside = beside + jnp.concatenate(rows, axis=0)
            out_ref[i * slab : (i + 1) * slab, :] = (
                diag[i * slab : (i + 1) * slab, :] * v - beside
            )

    def store(ref, f):
        for (a, b), c in zip(pieces, starts):
            if c < faces:
                ref[a:b, :] = f[c : c + b - a]

    starts = []
    for a, b in pieces:
        starts.append(starts[-1] + size if starts else 0)
        size = b - a

    def store_rest(ref, f):
        for (a, b), c in zip(pieces, starts):
            if c >= faces:
                ref[a:b, :] = f[c - faces : c - faces + b - a]

    ways = {
        "xl": (0, -1), "xh": (0, 1), "zl": (-1, 0), "zh": (1, 0),
        "xlzl": (-1, -1), "xhzl": (-1, 1), "xhzh": (1, 1), "xlzh": (1, -1),
    }
    zrows = tiles * BE
    span = half + zrows
    first_rows = {
        "xl": (0, half), "zl": (half, zrows), "xh": (span, half), "zh": (span + half, zrows),
    }
    order = ("xlzl", "xhzl", "xhzh", "xlzh", "xl", "xh", "zl", "zh")
    back = {"xl": "xh", "xh": "xl", "zl": "zh", "zh": "zl"}

    def opposite(key):
        return back[key[:2]] + back[key[2:]] if len(key) == 4 else back[key]

    def device(key):
        df, dc = ways[key]
        return lax.rem(mf + df + nf, nf), lax.min(lax.max(mc + dc, 0), nc - 1)

    groups = {"xl": ("xlzl", "xlzh", "xl"), "xh": ("xhzl", "xhzh", "xh"), "z": ("zl", "zh")}
    number = {key: n for n, keys in enumerate(groups.values()) for key in keys}

    def face_copy(e, key):
        if len(key) == 4:
            source = csend.at[e, order.index(key)]
            target = ydiag.at[e, order.index(opposite(key))]
        else:
            source = ysend.at[e, pl.ds(*first_rows[key])]
            target = (yz if key[0] == "z" else yx).at[e, int(key[1] == "l")]
        return pltpu.make_async_remote_copy(
            src_ref=source,
            dst_ref=target,
            send_sem=ysend_sem.at[e, number[key]],
            recv_sem=yrecv_sem.at[e, number[key]],
            device_id=device(key),
            device_id_type=MESH,
        )

    def second_copy(e, key):
        side = int(key[1] == "h")
        return pltpu.make_async_remote_copy(
            src_ref=(gsz if key[0] == "z" else gsx).at[e, side],
            dst_ref=(gz if key[0] == "z" else gx).at[e, 1 - side],
            send_sem=gsend_sem.at[e, number[key]],
            recv_sem=grecv_sem.at[e, number[key]],
            device_id=device(key),
            device_id_type=MESH,
        )

    def start_all(copies):
        for copy in copies:
            copy.start()

    def start_group(copy, e, x_only=False):
        for side in ("xl", "xh"):
            keys = [side] if x_only else groups[side]
            pl.when(has[side])(functools.partial(start_all, [copy(e, k) for k in keys]))
        start_all([copy(e, k) for k in groups["z"]])

    def wait_bytes(ref, sem):
        pltpu.make_async_copy(ref, ref, sem).wait()

    def wait_group(e, sems, x_bytes, z_bytes, received):
        for n, side in enumerate(("xl", "xh")):
            cond = has[back[side]] if received else has[side]
            pl.when(cond)(functools.partial(wait_bytes, x_bytes, sems.at[e, n]))
        wait_bytes(z_bytes, sems.at[e, 2])

    def keep(cond, value):
        return jnp.where(cond, value, 0.0)

    def corner_at(key):
        return (bz_n - 1) * (key[3] == "h"), (bx_n - 1) * (key[1] == "h")

    def corner_pack(xp, zp, bz, bx):
        px = pz = None
        for g in range(half // BE):
            piece = turn(xp[g * BE : (g + 1) * BE], g - bz)
            px = piece if g == 0 else jnp.where(bz8 == g, piece, px)
        for t in range(tiles):
            piece = turn(zp[t * BE : (t + 1) * BE], (t - bx) * bz_n)
            pz = piece if t == 0 else jnp.where(bx8 == t, piece, pz)
        return jnp.concatenate([px, pz], axis=0)

    def corner_open(p, bz, bx):
        px, pz = p[:BE], p[BE:]
        return (
            jnp.concatenate([turn(px, bz - g) for g in range(half // BE)], axis=0),
            jnp.concatenate([turn(pz, (bx - t) * bz_n) for t in range(tiles)], axis=0),
        )

    def twice(e, p_ref, first_ref, image_ref, second_ref, out_ref, during, ahead=None):
        load(p_ref[...])
        f = product(0, faces)
        xl, xh = pack_x(f)
        zl, zh = pack_z(f)
        for key, value in (("xl", xl), ("zl", zl), ("xh", xh), ("zh", zh)):
            a, size = first_rows[key]
            ysend[e, a : a + size, :] = value
        for n, key in enumerate(order[:4]):
            csend[e, n] = corner_pack(
                {"xl": xl, "xh": xh}[key[:2]], {"zl": zl, "zh": zh}[key[2:]], *corner_at(key)
            )
        start_group(face_copy, e)
        store(first_ref, f)
        store_rest(first_ref, product(faces, cells))
        stencil(first_ref, image_ref)
        load(image_ref[...])
        g = product(0, faces)
        packed_x, packed_z = pack_x(g), pack_z(g)
        for n in range(2):
            gsx[e, n] = packed_x[n]
            gsz[e, n] = packed_z[n]
        start_group(second_copy, e, True)
        store(second_ref, g)
        store_rest(second_ref, product(faces, cells))
        during()
        wait_group(e, yrecv_sem, csend.at[e], yz.at[e], True)
        first = (
            keep(has["xl"], yx[e, 0]), keep(has["xh"], yx[e, 1]),
            keep(has["zl"], yz[e, 0]), keep(has["zh"], yz[e, 1]),
        )
        ring_part(own, 0, *first)
        both = nn_dot(fh[...], own[...])
        change = (both[:, :lanes] + both[:, lanes:]) + nn_dot(fl[...], own[:, :lanes])
        for (a, b), c in zip(pieces, starts):
            second_ref[a:b, :] = second_ref[a:b, :] - change[c : c + b - a]

        def corner(key):
            return corner_open(ydiag[e, order.index(key)], *corner_at(opposite(key)))

        (llx, llz), (hlx, hlz), (hhx, hhz), (lhx, lhz) = (corner(k) for k in order[:4])
        bxz = jnp.concatenate([bx8] * tiles, axis=0)
        lowx, highx = has["xl"], has["xh"]

        def by_x(high, low):
            return jnp.where(bxz == 0, keep(highx, high), keep(lowx, low))

        def by_z(low, high):
            low = jnp.where(bz32 == 0, keep(has["zh"], high), 0.0) + jnp.where(
                bz32 == bz_n - 1, keep(has["zl"], low), 0.0
            )
            return low

        ring_part(
            ring, 0, ysend[e, span : span + half, :], ysend[e, 0:half, :],
            keep(has["zl"], by_x(hlz, llz)), keep(has["zh"], by_x(hhz, lhz)),
        )
        ring_part(
            ring, lanes, keep(lowx, by_z(llx, lhx)), keep(highx, by_z(hlx, hhx)),
            ysend[e, span + half : 2 * span, :], ysend[e, half : span, :],
        )
        count = ring.shape[1] // 2
        both = nn_dot(fh[0:faces, :], ring[...])
        full = (both[:, :count] + both[:, count:]) + nn_dot(fl[0:faces, :], ring[:, :count])
        cxl, cxh = pack_x(full[:, :lanes])
        czl, czh = pack_z(full[:, lanes:])
        stencil(second_ref, out_ref)
        take_off(image_ref, *first)
        if ahead is not None:
            ahead()
        wait_group(e, grecv_sem, gx.at[e, 0], gz.at[e], True)
        take_off(
            out_ref,
            keep(has["xl"], gx[e, 0] - cxh),
            keep(has["xh"], gx[e, 1] - cxl),
            keep(has["zl"], gz[e, 0] - czh),
            keep(has["zh"], gz[e, 1] - czl),
        )

    def gram(pairs):
        total = [None] * len(pairs)
        for i in range(BE):
            read = {}
            for p in pairs:
                for ref in p:
                    if id(ref) not in read:
                        read[id(ref)] = ref[i * slab : (i + 1) * slab, :]
            for n, (a, b) in enumerate(pairs):
                part = jnp.sum((read[id(a)] * read[id(b)]).reshape(BE, BE, lanes), axis=0)
                total[n] = part if i == 0 else total[n] + part
        return [jnp.sum(t, axis=0, keepdims=True) for t in total]

    def show_obstacle():
        for c in range(4):
            def write(x, plane, c=c):
                obf[c, x] = plane.astype(BF16)

            rows_to_field(
                lambda j, c=c: ob[c, pl.ds(j, slab, stride=BE), :], write, bx_n, bz_n, lane64
            )

    basis = (src, v1, w1, u1, x1)
    known = [(a, b) for a in range(3) for b in range(a, 3)]
    late = [(a, b) for b in (3, 4) for a in range(b + 1)]
    ready = []

    def ahead():
        ready.extend(sums_of(late[:4]))

    me = mf * nc + mc

    few = everyone <= 64 and nf & (nf - 1) == 0 and nc & (nc - 1) == 0

    def flips(me, count):
        out = []
        for mask in range(count if few else 0):
            to, bit = me, 1
            while bit <= mask:
                if mask & bit:
                    to = to + bit - 2 * bit * lax.rem(me // bit, 2)
                bit *= 2
            out.append(to)
        return out

    flip_fish, flip_curve = flips(mf, nf), flips(mc, nc)
    far_first = sorted(
        ((a, b) for a in range(len(flip_fish)) for b in range(len(flip_curve)) if a or b),
        key=lambda m: -(m[0] // 2 + m[1] % 2 + m[1] // 2),
    )

    def sums_of(pairs):
        return gram([(basis[a], basis[b]) for a, b in pairs])

    def tell(no, lines):
        number = -(-len(lines) // 8) * 8
        lines += [jnp.zeros((1, lanes), F32)] * (number - len(lines))
        tile = jnp.sum(jnp.concatenate(lines, axis=0), axis=1, keepdims=True)
        spot = lax.broadcasted_iota(jnp.int32, (number, lanes), 0) == lax.broadcasted_iota(
            jnp.int32, (number, lanes), 1
        )
        red[no, me] = jnp.sum(jnp.where(spot, tile, 0.0), axis=0, keepdims=True)

        def send(to_fish, to_curve):
            pltpu.make_async_remote_copy(
                src_ref=red.at[no, me],
                dst_ref=red.at[no, me],
                send_sem=rsend_sem.at[no],
                recv_sem=rrecv_sem.at[no],
                device_id=(to_fish, to_curve),
                device_id_type=MESH,
            ).start()

        if few:
            for a, b in far_first:
                send(flip_fish[a], flip_curve[b])
        else:

            def body(k, _):
                send(lax.rem(mf + k // nc, nf), lax.rem(mc + k, nc))
                return 0

            lax.fori_loop(1, everyone, body, 0)

    def hear(no, pairs):
        heard = red.at[no, pl.ds(0, everyone - 1)]
        pltpu.make_async_copy(heard, heard, rrecv_sem.at[no]).wait()
        row = jnp.sum(red[no], axis=0)
        return dict(zip(pairs, entries(row, len(pairs))))

    def show(ref, out):
        def write(x, plane):
            out[x] = plane

        rows_to_field(lambda j: ref[pl.ds(j, slab, stride=BE), :], write, bx_n, bz_n, lane64)

    twice(0, src, y1, v1, m1, w1, show_obstacle)
    twice(1, w1, n1, u1, q1, x1, lambda: tell(0, sums_of(known)), ahead)
    tell(1, ready + sums_of(late[4:]))
    sums = hear(0, known)
    scalars = first_scalars(sums)
    for ref, out in (
        (src, rfield), (v1, vfield), (w1, wfield), (u1, ufield), (x1, xfield),
        (y1, yfield), (m1, mfield), (n1, nfield), (q1, qfield),
    ):
        show(ref, out)
    wait_bytes(precv.at[pl.ds(0, nc - 1)], psend_sem)
    for e in range(2):
        wait_group(e, ysend_sem, csend.at[e], yz.at[e], False)
        wait_group(e, gsend_sem, gx.at[e, 0], gz.at[e], False)
    sums.update(hear(1, late))
    resid, press = coefficients(sums, scalars)
    for first, coefs in ((0, resid), (8, press)):
        for k, coef in enumerate(coefs):
            coef_ref[first + k : first + k + 1, :] = jnp.broadcast_to(coef, (1, lanes))
    for no in range(2):
        heard = red.at[no, pl.ds(0, everyone - 1)]
        pltpu.make_async_copy(heard, heard, rsend_sem.at[no]).wait()


def local(right_side, block_inverse, midline, entry_fish, entry_seg, entry_dest, entry_block):
    nf, nc = lax.axis_size("fish"), lax.axis_size("curve")
    count = entry_fish.shape[0]
    cap = max(2, 2 * count // nc)
    cx, cz, ny = right_side.shape
    lanes = (cx // BE) * (cz // BE) * (ny // BE)
    cells = BE**3
    slab = BE * BE
    half = slab // 2
    zrows = BE // (cz // BE) * BE
    span = half + zrows
    wide = 4 * slab
    rows, fishes, npts = midline.shape
    width = fishes * npts
    vmem = pl.BlockSpec(memory_space=pltpu.VMEM)
    big = pltpu.VMEM((cells, lanes), F32)
    dma = pltpu.SemaphoreType.DMA
    anywhere = pl.BlockSpec(memory_space=pl.ANY)
    field = jax.ShapeDtypeStruct((cx, cz, ny), F32)
    fields = jax.ShapeDtypeStruct((4, cx, cz, ny), BF16)
    solved = pl.pallas_call(
        functools.partial(kernel, nf, nc, cap, npts),
        out_shape=(
            (pltpu.VMEM((16, lanes), F32),)
            + (pltpu.VMEM((cx, cz, ny), F32),) * 9
            + (pltpu.VMEM((4, cx, cz, ny), BF16),)
        ),
        in_specs=[anywhere] * 7,
        out_specs=(vmem,) * 11,
        scratch_shapes=[big] * 9
        + [
            pltpu.VMEM((cx, cz, ny), F32),
            pltpu.VMEM((cells, cells), F32),
            pltpu.VMEM((rows, fishes, npts), F32),
            pltpu.VMEM((4, 1, count), jnp.int32),
            dma((4,)),
            pltpu.VMEM((cells, cells), BF16),
            pltpu.VMEM((cells, cells), BF16),
            pltpu.VMEM((cells, wide), BF16),
            pltpu.VMEM((cells, wide), BF16),
            pltpu.VMEM((cells, 2 * lanes), BF16),
            pltpu.VMEM((wide, 2 * lanes), BF16),
            pltpu.VMEM((wide, 4 * lanes), BF16),
            pltpu.VMEM((8, lanes), F32),
            pltpu.VMEM((8, width), F32),
            pltpu.VMEM((SEG * 8, width), F32),
            pltpu.VMEM((nc, cap, lanes), F32),
            pltpu.VMEM((nc, cap, lanes), F32),
            pltpu.VMEM((SEG * 8, lanes), F32),
            pltpu.VMEM((SEG, slab, lanes), F32),
            pltpu.VMEM((4, cells // 2, 2 * lanes), BF16),
            pltpu.VMEM((2 * lanes, 2 * lanes), BF16),
            pltpu.VMEM((4, cells, lanes), F32),
            big,
            pltpu.VMEM((2, 2 * span, lanes), F32),
            pltpu.VMEM((2, 4, 2 * BE, lanes), F32),
            pltpu.VMEM((2, 2, half, lanes), F32),
            pltpu.VMEM((2, 2, zrows, lanes), F32),
            pltpu.VMEM((2, 4, 2 * BE, lanes), F32),
            pltpu.VMEM((2, 2, half, lanes), F32),
            pltpu.VMEM((2, 2, zrows, lanes), F32),
            pltpu.VMEM((2, 2, half, lanes), F32),
            pltpu.VMEM((2, 2, zrows, lanes), F32),
            pltpu.VMEM((2, nf * nc, 1, lanes), F32),
            dma,
            dma((2,)),
            dma((2, 3)),
            dma((2, 3)),
            dma((2, 3)),
            dma((2, 3)),
            dma((2,)),
            dma((2,)),
        ],
        compiler_params=pltpu.CompilerParams(
            collective_id=0, has_side_effects=True, vmem_limit_bytes=VMEM_LIMIT
        ),
    )(
        *(
            pltpu.with_memory_space_constraint(a, pltpu.HBM)
            for a in (
                right_side,
                block_inverse,
                midline,
                *(e.reshape(1, count) for e in (entry_fish, entry_seg, entry_dest, entry_block)),
            )
        )
    )
    return pl.pallas_call(
        finish,
        out_shape=(field, field, fields),
        in_specs=[vmem] * 11,
        out_specs=(anywhere,) * 3,
        scratch_shapes=[
            pltpu.VMEM((cx, cz, ny), F32),
            pltpu.VMEM((cx, cz, ny), F32),
            dma,
            dma((2, 4)),
        ],
        compiler_params=pltpu.CompilerParams(vmem_limit_bytes=VMEM_LIMIT),
    )(*(pltpu.with_memory_space_constraint(a, pltpu.VMEM) for a in solved))


def solution(mesh):
    return jax.shard_map(
        local,
        mesh=mesh,
        in_specs=(
            P("curve", "fish", None),
            P(),
            P(None, "fish", None),
            P(("fish", "curve")),
            P(("fish", "curve")),
            P(("fish", "curve"), None),
            P(("fish", "curve")),
        ),
        out_specs=(
            P("curve", "fish", None),
            P("curve", "fish", None),
            P(None, "curve", "fish", None),
        ),
        check_vma=False,
    )
```

```python
import functools
import jax
import jax.numpy as jnp
from jax import lax
from jax.experimental import pallas as pl
from jax.experimental.pallas import tpu as pltpu
from jax.sharding import PartitionSpec as P

BE = 8
SEG = 16
PENALTY = 4.0
F32 = jnp.float32
BF16 = jnp.bfloat16
MESH = pl.DeviceIdType.MESH


def nt_dot(a, b):
    return lax.dot_general(a, b, (((1,), (1,)), ((), ())), preferred_element_type=F32)


def nn_dot(a, b):
    return lax.dot_general(a, b, (((1,), (0,)), ((), ())), preferred_element_type=F32)


def split3(x):
    hi = x.astype(BF16)
    rest = x - hi.astype(F32)
    mid = rest.astype(BF16)
    low = (rest - mid.astype(F32)).astype(BF16)
    return hi, mid, low


def swap_bits(arrays, lane):
    arrays = list(arrays)
    lanes = lane.shape[-1]
    for step in (4, 2, 1):
        clear = (lane & step) == 0
        for a in range(8):
            if a & step:
                continue
            low, high = arrays[a], arrays[a | step]
            arrays[a] = jnp.where(clear, low, pltpu.roll(high, step, axis=1))
            arrays[a | step] = jnp.where(clear, pltpu.roll(low, lanes - step, axis=1), high)
    return arrays


def rows_to_field(read_j, write, bx_n, bz_n, lane):
    parts = swap_bits([read_j(j) for j in range(BE)], lane)
    for bx in range(bx_n):
        for i in range(BE):
            plane = jnp.concatenate(
                [parts[bx * bz_n + bz][i * BE : (i + 1) * BE, :] for bz in range(bz_n)], axis=0
            )
            write(bx * BE + i, plane)


VMEM_LIMIT = 40 * 1024 * 1024


def finish(
    coef_ref, r_ref, v_ref, w_ref, u_ref, x_ref, y_ref, m_ref, n_ref, q_ref, oin_ref,
    press_ref, resid_ref, obst_ref, pf, rf, osem, sems,
):
    give = pltpu.make_async_copy(oin_ref, obst_ref, osem)
    give.start()
    chunks = sems.shape[1]
    size = rf.shape[0] // chunks
    outs = []
    for c in range(chunks):
        part = pl.ds(c * size, size)
        for n, (out, dst, basis, first) in enumerate(
            (
                (rf, resid_ref, (r_ref, v_ref, w_ref, u_ref, x_ref), 0),
                (pf, press_ref, (y_ref, m_ref, n_ref, q_ref), 8),
            )
        ):
            total = None
            for k, ref in enumerate(basis):
                term = ref[part]
                if first or k:
                    term = coef_ref[first + k : first + k + 1, :] * term
                total = term if total is None else total + term
            out[part] = total
            copy = pltpu.make_async_copy(out.at[part], dst.at[part], sems.at[n, c])
            copy.start()
            outs.append(copy)
    for copy in outs:
        copy.wait()
    give.wait()


def entries(row, count):
    lane = lax.broadcasted_iota(jnp.int32, row.shape, 1)
    return [
        jnp.sum(jnp.where(lane == k, row, 0.0), axis=1, keepdims=True) for k in range(count)
    ]


def first_scalars(gram):
    rr, rv, vv, vw, ww, rw = (gram[k] for k in ((0, 0), (0, 1), (1, 1), (1, 2), (2, 2), (0, 2)))
    alpha = rr / rv
    ts = (rv - alpha * vv) - alpha * (rw - alpha * vw)
    tt = (vv - alpha * vw) - alpha * (vw - alpha * ww)
    omega = ts / tt
    rho2 = (rr - alpha * rv) - omega * (rv - alpha * rw)
    beta = rho2 / rr * (alpha / omega)
    both, prod = alpha + omega, alpha * omega
    d0, d1, d2 = 1.0 + beta, -(both + beta * omega), prod
    return rho2, both, prod, d0, d1, d2, d0 * rv + d1 * rw


def coefficients(gram, scalars):
    rho2, both, prod, d0, d1, d2, known = scalars
    gram = {**gram, **{(b, a): g for (a, b), g in gram.items()}}
    alpha2 = rho2 / (known + d2 * gram[0, 3])
    s1, s2, s3 = -both - alpha2 * d0, prod - alpha2 * d1, -alpha2 * d2
    ts = tt = None
    for a, sa in ((1, None), (2, s1), (3, s2), (4, s3)):
        q = (gram[a, 0] + s1 * gram[a, 1]) + (s2 * gram[a, 2] + s3 * gram[a, 3])
        z = (gram[a, 1] + s1 * gram[a, 2]) + (s2 * gram[a, 3] + s3 * gram[a, 4])
        ts = q if sa is None else ts + sa * q
        tt = z if sa is None else tt + sa * z
    omega2 = ts / tt
    resid = (omega2, s1 - omega2, s2 - omega2 * s1, s3 - omega2 * s2, -omega2 * s3)
    press = (
        both + alpha2 * d0 + omega2,
        alpha2 * d1 - prod + omega2 * s1,
        alpha2 * d2 + omega2 * s2,
        omega2 * s3,
    )
    return resid, press


def kernel(
    nf, nc, cap, npts,
    rs_hbm, inv_hbm, mid_hbm, fish_hbm, seg_hbm, dest_hbm, block_hbm,
    coef_ref, rfield, vfield, wfield, ufield, xfield, yfield, mfield, nfield, qfield, obf,
    src, v1, w1, u1, x1, y1, m1, n1, q1, rs_ref, inv_ref, mid_ref, ent_ref, in_sem,
    mh, ml, fh, fl, rhs, own, ring, meta_ref, tab, shifted, psend, precv, pt, dyz, paid, spread, ob, diag,
    ysend, csend, yx, yz, ydiag, gsx, gsz, gx, gz, red,
    psend_sem, precv_sem, ysend_sem, yrecv_sem, gsend_sem, grecv_sem, rsend_sem, rrecv_sem,
):
    mf = lax.axis_index("fish")
    mc = lax.axis_index("curve")
    cells, lanes = src.shape
    slab = BE * BE
    half = slab // 2
    bx_n = rs_ref.shape[0] // BE
    bz_n = rs_ref.shape[1] // BE
    group = bx_n * bz_n
    everyone = nf * nc

    barrier = pltpu.get_barrier_semaphore()

    def greet_fish(k, _):
        pl.semaphore_signal(
            barrier, inc=1, device_id=(lax.rem(mf + k, nf), mc), device_id_type=MESH
        )
        return 0

    def greet_curve(k, _):
        pl.semaphore_signal(
            barrier, inc=1, device_id=(mf, lax.rem(mc + k, nc)), device_id_type=MESH
        )
        return 0

    lax.fori_loop(1, nc, greet_curve, 0)
    lax.fori_loop(1, nf, greet_fish, 0)

    takes = [
        pltpu.make_async_copy(a, b, in_sem.at[max(n - 3, 0)])
        for n, (a, b) in enumerate(
            [(a, ent_ref.at[k]) for k, a in enumerate((fish_hbm, seg_hbm, dest_hbm, block_hbm))]
            + [(mid_hbm, mid_ref), (inv_hbm, inv_ref), (rs_hbm, rs_ref)]
        )
    ]
    for copy in takes:
        copy.start()

    lane8 = lax.broadcasted_iota(jnp.int32, (BE, lanes), 1)
    lane64 = lax.broadcasted_iota(jnp.int32, (slab, lanes), 1)
    lane32 = lax.broadcasted_iota(jnp.int32, (half, lanes), 1)
    sub8 = lax.broadcasted_iota(jnp.int32, (BE, lanes), 0)
    col = lax.broadcasted_iota(jnp.int32, (lanes, lanes), 1)
    row = lax.broadcasted_iota(jnp.int32, (lanes, lanes), 0)
    colf, rowf = col.astype(F32), row.astype(F32)

    pltpu.make_async_copy(ent_ref, ent_ref, in_sem.at[0]).wait()
    takes[4].wait()
    nyb = rs_ref.shape[2] // BE
    count = ent_ref.shape[2]
    rows, fishes, _ = mid_ref.shape
    width = tab.shape[1]
    block = ent_ref[3]
    place_in = block % nyb * group + block // nyb + 1
    meta_ref[...] = jnp.full_like(meta_ref, -1.0)
    for r, column in enumerate((ent_ref[0], ent_ref[1], ent_ref[2], place_in)):
        meta_ref[r : r + 1, 0:count] = column.astype(F32)
    for f in range(fishes):
        tab[0:rows, f * npts : (f + 1) * npts] = mid_ref[:, f, :]
    tab[rows:8, :] = jnp.zeros((8 - rows, width), F32)
    table = tab[...]
    for m in range(SEG):
        turned = table if m == 0 else pltpu.roll(table, width - m, axis=1)
        shifted[m * 8 : m * 8 + 8, :] = turned
    meta = meta_ref[...]
    owner = lax.broadcasted_iota(jnp.int32, (nc, lanes), 0).astype(F32)
    mine = owner == meta[2:3, :]
    earlier = jnp.where(row < col, 1.0, 0.0).astype(BF16)
    rank = nn_dot(jnp.where(mine, 1.0, 0.0).astype(BF16), earlier)
    slot = jnp.sum(jnp.where(mine, owner * cap + rank + 1.0, 0.0), axis=0, keepdims=True) - 1.0
    hot = jnp.where(rowf == slot, 1.0, 0.0).astype(BF16)
    picked = nt_dot(hot, meta.astype(BF16))
    index = picked[:, 0:1] * npts + picked[:, 1:2]
    place = picked[:, 3:4] - 1.0
    point_hot = jnp.where(
        lax.broadcasted_iota(jnp.int32, (lanes, width), 1).astype(F32) == index, 1.0, 0.0
    ).astype(BF16)
    hi, mid, low = split3(shifted[...])
    points = (nt_dot(point_hot, hi) + nt_dot(point_hot, mid)) + nt_dot(point_hot, low)
    points = jnp.where(col == 7, place, points)
    for c in range(nc):
        psend[c] = points[c * cap : (c + 1) * cap, :]

    pl.semaphore_wait(barrier, nf - 1 + nc - 1)

    part = nc // 2
    near = mc // part * part
    bases = (near, part - near)

    def hand_start(far):
        def body(k, _):
            to = bases[far] + lax.rem(mc - near + k, part)
            pltpu.make_async_remote_copy(
                src_ref=psend.at[to],
                dst_ref=precv.at[mc],
                send_sem=psend_sem,
                recv_sem=precv_sem.at[far],
                device_id=(mf, to),
                device_id_type=MESH,
            ).start()
            return 0

        lax.fori_loop(1 - far, part, body, 0)

    hand_start(0)
    hand_start(1)
    precv[mc] = psend[mc]
    spread[...] = jnp.zeros_like(spread)

    takes[5].wait()
    whole = inv_ref[...]
    top = jnp.max(jnp.max(jnp.abs(whole), axis=0, keepdims=True), axis=1, keepdims=True)
    scale = 1.0 / (slab * top)
    inner_k = slab - 2 * BE
    pieces = [(0, slab), (cells - slab, cells)]
    pieces += [(i * slab, i * slab + BE) for i in range(1, BE - 1)]
    pieces += [((i + 1) * slab - BE, (i + 1) * slab) for i in range(1, BE - 1)]
    pieces += [(i * slab + BE, (i + 1) * slab - BE) for i in range(1, BE - 1)]
    faces = 2 * slab + 2 * BE * (BE - 2)
    arranged = jnp.concatenate([inv_ref[a:b, :] for a, b in pieces], axis=0) * scale
    hi = arranged.astype(BF16)
    mh[...] = hi
    ml[...] = (arranged - hi.astype(F32)).astype(BF16)
    wide = fh.shape[1]
    cell = lax.broadcasted_iota(jnp.int32, (cells, wide), 0)
    face = lax.broadcasted_iota(jnp.int32, (1, wide), 1)
    side = (face - 2 * slab) // (BE * (BE - 2))
    deep = (face - 2 * slab) % (BE * (BE - 2))
    where_z = (deep // BE + 1) * slab + side * (slab - BE) + deep % BE
    where_x = face // slab * (cells - slab) + face % slab
    at = jnp.where(face < 2 * slab, where_x, jnp.where(face < faces, where_z, -1))
    pick = jnp.where(cell == at, 1.0, 0.0).astype(BF16)
    for full, kept in ((mh, fh), (ml, fl)):
        kept[...] = nn_dot(full[...], pick).astype(BF16)

    def field_to_rows(read, out_ref):
        parts = []
        for g in range(group):
            bx, bz = g // bz_n, g % bz_n
            parts.append(read(bx, bz).reshape(slab, lanes))
        for j, rows in enumerate(swap_bits(parts, lane64)):
            out_ref[pl.ds(j, slab, stride=BE), :] = rows

    takes[6].wait()
    field_to_rows(
        lambda bx, bz: rs_ref[bx * BE : (bx + 1) * BE, bz * BE : (bz + 1) * BE, :], src
    )

    has = {"xl": mc > 0, "xh": mc < nc - 1, "zl": mf > 0, "zh": mf < nf - 1}
    cell = lax.broadcasted_iota(jnp.int32, (slab, lanes), 0)
    zc = (cell // BE).astype(F32) + 0.5
    yc = (cell % BE).astype(F32) + 0.5
    slots = part * cap
    deep = BE // 2
    xbase = jnp.where(lane8[0:1, :] < slots, 0.5, 0.5 + deep)

    for far in range(2):
        handed = precv.at[pl.ds(0, part - 1 + far)]
        pltpu.make_async_copy(handed, handed, precv_sem.at[far]).wait()
        for c in range(part):
            value = precv[bases[far] + c]
            for h in range(2):
                pt[h * slots + c * cap : h * slots + (c + 1) * cap, :] = value
        got = pt[...]
        hot = jnp.where(colf[0:slots, :] == got[0:slots, 7:8], 1.0, 0.0).astype(BF16)
        for h in range(2):
            a = (2 * far + h) * slots
            spread[a : a + slots, h * lanes : (h + 1) * lanes] = hot
        pt[...] = got.T
        for m in range(SEG):
            dy = yc - pt[m * 8 + 1 : m * 8 + 2, :]
            dz = zc - pt[m * 8 + 2 : m * 8 + 3, :]
            dyz[m] = (dy * dy + dz * dz) + 0.25

        def build(i, _):
            xc = i.astype(F32) + xbase
            for h in range(2):
                lo_row = h * half
                near = ws = vx = vy = vz = None
                for m in range(SEG):
                    dx = xc - pt[m * 8 : m * 8 + 1, :]
                    e = dyz[m, lo_row : lo_row + half, :] + dx * dx
                    signed = e * lax.rsqrt(e) - pt[m * 8 + 6 : m * 8 + 7, :]
                    a = pl.reciprocal(e + 0.75, approx=True)
                    ax = a * pt[m * 8 + 3 : m * 8 + 4, :]
                    ay = a * pt[m * 8 + 4 : m * 8 + 5, :]
                    az = a * pt[m * 8 + 5 : m * 8 + 6, :]
                    if m == 0:
                        near, ws, vx, vy, vz = signed, a, ax, ay, az
                    else:
                        near = jnp.minimum(near, signed)
                        ws, vx, vy, vz = ws + a, vx + ax, vy + ay, vz + az
                ind = 0.5 - 0.5 * jnp.tanh(near)
                scale = ind / ws
                base = pl.multiple_of(i * slab + lo_row, half)
                for c, value in enumerate((ind, vx * scale, vy * scale, vz * scale)):
                    paid[c, pl.ds(base, half), far * lanes : (far + 1) * lanes] = value.astype(BF16)
            return 0

        lax.fori_loop(0, deep, build, 0, unroll=True)

    for c in range(4):
        summed = nn_dot(paid[c], spread[...]).astype(BF16).astype(F32)
        ob[c, 0 : deep * slab, :] = summed[:, :lanes]
        ob[c, deep * slab :, :] = summed[:, lanes:]
    diag[...] = 6.0 + PENALTY * ob[0]
    src[...] = src[...] - ((ob[1] + ob[2]) + ob[3])

    bz8 = lane8 % bz_n
    bx8 = (lane8 // bz_n) % bx_n
    bx64 = (lane64 // bz_n) % bx_n
    bx32 = (lane32 // bz_n) % bx_n
    bz32 = lane32 % bz_n
    tiles = BE // bz_n

    def turn(x, shift):
        shift = shift % lanes
        return x if shift == 0 else pltpu.roll(x, shift, axis=1)

    def load(value):
        vh = value.astype(BF16)
        rhs[:, :lanes] = vh
        rhs[:, lanes:] = (value - vh.astype(F32)).astype(BF16)

    def product(a, b):
        both = nn_dot(mh[a:b, :], rhs[...])
        return (both[:, :lanes] + both[:, lanes:]) + nn_dot(ml[a:b, :], rhs[:, :lanes])

    def face_low(f, i):
        if i == 0:
            return f[0:BE]
        if i == BE - 1:
            return f[slab : slab + BE]
        a = 2 * slab + (i - 1) * BE
        return f[a : a + BE]

    def face_high(f, i):
        if i == 0:
            return f[slab - BE : slab]
        if i == BE - 1:
            return f[2 * slab - BE : 2 * slab]
        a = 2 * slab + BE * (BE - 2) + (i - 1) * BE
        return f[a : a + BE]

    def pack_x(f):
        f0, f7 = f[:slab], f[slab : 2 * slab]
        low = jnp.where(bx32 == 0, f0[:half], turn(f0[half:], bz_n))
        high = jnp.where(bx32 == 0, turn(f7[:half], -bz_n), f7[half:])
        return low, high

    def pack_z(f):
        lows, highs = [], []
        for t in range(tiles):
            lowp = highp = None
            for a in range(bz_n):
                lo = turn(face_low(f, t * bz_n + a), a)
                hg = turn(face_high(f, t * bz_n + a), a - (bz_n - 1))
                lowp = lo if a == 0 else jnp.where(bz8 == a, lo, lowp)
                highp = hg if a == 0 else jnp.where(bz8 == a, hg, highp)
            lows.append(lowp)
            highs.append(highp)
        return jnp.concatenate(lows, axis=0), jnp.concatenate(highs, axis=0)

    def spread_x(got_low, got_high):
        at_low = [jnp.where(bx32 == 0, p, 0.0) for p in (got_low, turn(got_low, -bz_n))]
        at_high = [
            jnp.where(bx32 == bx_n - 1, p, 0.0) for p in (turn(got_high, bz_n), got_high)
        ]
        return at_low, at_high

    def spread_z(got_low, got_high):
        at_low, at_high = [], []
        for i in range(BE):
            t, a = i // bz_n, i % bz_n
            gl, gh = got_low[t * BE : (t + 1) * BE], got_high[t * BE : (t + 1) * BE]
            at_low.append(jnp.where(bz8 == 0, turn(gl, -a), 0.0))
            at_high.append(jnp.where(bz8 == bz_n - 1, turn(gh, bz_n - 1 - a), 0.0))
        return at_low, at_high

    def take_off(ref, xl, xh, zl, zh):
        at_low, at_high = spread_x(xl, xh)
        for h in range(2):
            a, b = h * half, cells - slab + h * half
            ref[a : a + half, :] = ref[a : a + half, :] - at_low[h]
            ref[b : b + half, :] = ref[b : b + half, :] - at_high[h]
        at_low, at_high = spread_z(zl, zh)
        for i in range(BE):
            a, b = i * slab, (i + 1) * slab - BE
            ref[a : a + BE, :] = ref[a : a + BE, :] - at_low[i]
            ref[b : b + BE, :] = ref[b : b + BE, :] - at_high[i]

    def ring_part(ring, at, xl, xh, zl, zh):
        low, high = spread_x(xl, xh)
        zlow, zhigh = spread_z(zl, zh)
        low, high = jnp.concatenate(low, axis=0), jnp.concatenate(high, axis=0)
        outer = []
        for rows, i in ((low, 0), (high, BE - 1)):
            outer += [rows[:BE] + zlow[i], rows[BE : slab - BE], rows[slab - BE :] + zhigh[i]]
        part = jnp.concatenate(outer + zlow[1:-1] + zhigh[1:-1], axis=0)
        hi = part.astype(BF16)
        low_at = ring.shape[1] // 2 + at
        ring[0:faces, at : at + lanes] = hi
        ring[0:faces, low_at : low_at + lanes] = (part - hi.astype(F32)).astype(BF16)

    for part in (own, ring):
        part[faces:, :] = jnp.zeros((wide - faces, part.shape[1]), BF16)

    def stencil(v_ref, out_ref):
        v0 = v_ref[0:slab, :]
        v7 = v_ref[cells - slab : cells, :]
        for i in range(BE):
            v = v_ref[i * slab : (i + 1) * slab, :]
            if i > 0:
                beside = v_ref[(i - 1) * slab : i * slab, :]
            else:
                beside = jnp.where(bx64 > 0, turn(v7, bz_n), 0.0)
            if i < BE - 1:
                beside = beside + v_ref[(i + 1) * slab : (i + 2) * slab, :]
            else:
                beside = beside + jnp.where(bx64 < bx_n - 1, turn(v0, -bz_n), 0.0)
            rows = []
            for k in range(BE):
                t = v[k * BE : (k + 1) * BE, :]
                if k > 0:
                    s = v[(k - 1) * BE : k * BE, :]
                else:
                    s = jnp.where(bz8 > 0, turn(v[slab - BE :, :], 1), 0.0)
                if k < BE - 1:
                    s = s + v[(k + 1) * BE : (k + 2) * BE, :]
                else:
                    s = s + jnp.where(bz8 < bz_n - 1, turn(v[:BE, :], -1), 0.0)
                down = pltpu.roll(t, 1, axis=0)
                edge = jnp.where(lane8 < group, 0.0, turn(down, group))
                s = s + jnp.where(sub8 == 0, edge, down)
                up = pltpu.roll(t, BE - 1, axis=0)
                edge = jnp.where(lane8 >= lanes - group, 0.0, turn(up, -group))
                s = s + jnp.where(sub8 == BE - 1, edge, up)
                rows.append(s)
            beside = beside + jnp.concatenate(rows, axis=0)
            out_ref[i * slab : (i + 1) * slab, :] = (
                diag[i * slab : (i + 1) * slab, :] * v - beside
            )

    def store(ref, f):
        for (a, b), c in zip(pieces, starts):
            if c < faces:
                ref[a:b, :] = f[c : c + b - a]

    starts = []
    for a, b in pieces:
        starts.append(starts[-1] + size if starts else 0)
        size = b - a

    def store_rest(ref, f):
        for (a, b), c in zip(pieces, starts):
            if c >= faces:
                ref[a:b, :] = f[c - faces : c - faces + b - a]

    ways = {
        "xl": (0, -1), "xh": (0, 1), "zl": (-1, 0), "zh": (1, 0),
        "xlzl": (-1, -1), "xhzl": (-1, 1), "xhzh": (1, 1), "xlzh": (1, -1),
    }
    zrows = tiles * BE
    span = half + zrows
    first_rows = {
        "xl": (0, half), "zl": (half, zrows), "xh": (span, half), "zh": (span + half, zrows),
    }
    order = ("xlzl", "xhzl", "xhzh", "xlzh", "xl", "xh", "zl", "zh")
    back = {"xl": "xh", "xh": "xl", "zl": "zh", "zh": "zl"}

    def opposite(key):
        return back[key[:2]] + back[key[2:]] if len(key) == 4 else back[key]

    def device(key):
        df, dc = ways[key]
        return lax.rem(mf + df + nf, nf), lax.min(lax.max(mc + dc, 0), nc - 1)

    groups = {"xl": ("xlzl", "xlzh", "xl"), "xh": ("xhzl", "xhzh", "xh"), "z": ("zl", "zh")}
    number = {key: n for n, keys in enumerate(groups.values()) for key in keys}

    def face_copy(e, key):
        if len(key) == 4:
            source = csend.at[e, order.index(key)]
            target = ydiag.at[e, order.index(opposite(key))]
        else:
            source = ysend.at[e, pl.ds(*first_rows[key])]
            target = (yz if key[0] == "z" else yx).at[e, int(key[1] == "l")]
        return pltpu.make_async_remote_copy(
            src_ref=source,
            dst_ref=target,
            send_sem=ysend_sem.at[e, number[key]],
            recv_sem=yrecv_sem.at[e, number[key]],
            device_id=device(key),
            device_id_type=MESH,
        )

    def second_copy(e, key):
        side = int(key[1] == "h")
        return pltpu.make_async_remote_copy(
            src_ref=(gsz if key[0] == "z" else gsx).at[e, side],
            dst_ref=(gz if key[0] == "z" else gx).at[e, 1 - side],
            send_sem=gsend_sem.at[e, number[key]],
            recv_sem=grecv_sem.at[e, number[key]],
            device_id=device(key),
            device_id_type=MESH,
        )

    def start_all(copies):
        for copy in copies:
            copy.start()

    def start_group(copy, e, x_only=False):
        for side in ("xl", "xh"):
            keys = [side] if x_only else groups[side]
            pl.when(has[side])(functools.partial(start_all, [copy(e, k) for k in keys]))
        start_all([copy(e, k) for k in groups["z"]])

    def wait_bytes(ref, sem):
        pltpu.make_async_copy(ref, ref, sem).wait()

    def wait_group(e, sems, x_bytes, z_bytes, received):
        for n, side in enumerate(("xl", "xh")):
            cond = has[back[side]] if received else has[side]
            pl.when(cond)(functools.partial(wait_bytes, x_bytes, sems.at[e, n]))
        wait_bytes(z_bytes, sems.at[e, 2])

    def keep(cond, value):
        return jnp.where(cond, value, 0.0)

    def corner_at(key):
        return (bz_n - 1) * (key[3] == "h"), (bx_n - 1) * (key[1] == "h")

    def corner_pack(xp, zp, bz, bx):
        px = pz = None
        for g in range(half // BE):
            piece = turn(xp[g * BE : (g + 1) * BE], g - bz)
            px = piece if g == 0 else jnp.where(bz8 == g, piece, px)
        for t in range(tiles):
            piece = turn(zp[t * BE : (t + 1) * BE], (t - bx) * bz_n)
            pz = piece if t == 0 else jnp.where(bx8 == t, piece, pz)
        return jnp.concatenate([px, pz], axis=0)

    def corner_open(p, bz, bx):
        px, pz = p[:BE], p[BE:]
        return (
            jnp.concatenate([turn(px, bz - g) for g in range(half // BE)], axis=0),
            jnp.concatenate([turn(pz, (bx - t) * bz_n) for t in range(tiles)], axis=0),
        )

    def twice(e, p_ref, first_ref, image_ref, second_ref, out_ref, during, ahead=None):
        load(p_ref[...])
        f = product(0, faces)
        xl, xh = pack_x(f)
        zl, zh = pack_z(f)
        for key, value in (("xl", xl), ("zl", zl), ("xh", xh), ("zh", zh)):
            a, size = first_rows[key]
            ysend[e, a : a + size, :] = value
        for n, key in enumerate(order[:4]):
            csend[e, n] = corner_pack(
                {"xl": xl, "xh": xh}[key[:2]], {"zl": zl, "zh": zh}[key[2:]], *corner_at(key)
            )
        start_group(face_copy, e)
        store(first_ref, f)
        store_rest(first_ref, product(faces, cells))
        stencil(first_ref, image_ref)
        load(image_ref[...])
        g = product(0, faces)
        packed_x, packed_z = pack_x(g), pack_z(g)
        for n in range(2):
            gsx[e, n] = packed_x[n]
            gsz[e, n] = packed_z[n]
        start_group(second_copy, e, True)
        store(second_ref, g)
        store_rest(second_ref, product(faces, cells))
        during()
        wait_group(e, yrecv_sem, csend.at[e], yz.at[e], True)
        first = (
            keep(has["xl"], yx[e, 0]), keep(has["xh"], yx[e, 1]),
            keep(has["zl"], yz[e, 0]), keep(has["zh"], yz[e, 1]),
        )
        ring_part(own, 0, *first)
        both = nn_dot(fh[...], own[...])
        change = (both[:, :lanes] + both[:, lanes:]) + nn_dot(fl[...], own[:, :lanes])
        for (a, b), c in zip(pieces, starts):
            second_ref[a:b, :] = second_ref[a:b, :] - change[c : c + b - a]

        def corner(key):
            return corner_open(ydiag[e, order.index(key)], *corner_at(opposite(key)))

        (llx, llz), (hlx, hlz), (hhx, hhz), (lhx, lhz) = (corner(k) for k in order[:4])
        bxz = jnp.concatenate([bx8] * tiles, axis=0)
        lowx, highx = has["xl"], has["xh"]

        def by_x(high, low):
            return jnp.where(bxz == 0, keep(highx, high), keep(lowx, low))

        def by_z(low, high):
            low = jnp.where(bz32 == 0, keep(has["zh"], high), 0.0) + jnp.where(
                bz32 == bz_n - 1, keep(has["zl"], low), 0.0
            )
            return low

        ring_part(
            ring, 0, ysend[e, span : span + half, :], ysend[e, 0:half, :],
            keep(has["zl"], by_x(hlz, llz)), keep(has["zh"], by_x(hhz, lhz)),
        )
        ring_part(
            ring, lanes, keep(lowx, by_z(llx, lhx)), keep(highx, by_z(hlx, hhx)),
            ysend[e, span + half : 2 * span, :], ysend[e, half : span, :],
        )
        count = ring.shape[1] // 2
        both = nn_dot(fh[0:faces, :], ring[...])
        full = (both[:, :count] + both[:, count:]) + nn_dot(fl[0:faces, :], ring[:, :count])
        cxl, cxh = pack_x(full[:, :lanes])
        czl, czh = pack_z(full[:, lanes:])
        stencil(second_ref, out_ref)
        take_off(image_ref, *first)
        if ahead is not None:
            ahead()
        wait_group(e, grecv_sem, gx.at[e, 0], gz.at[e], True)
        take_off(
            out_ref,
            keep(has["xl"], gx[e, 0] - cxh),
            keep(has["xh"], gx[e, 1] - cxl),
            keep(has["zl"], gz[e, 0] - czh),
            keep(has["zh"], gz[e, 1] - czl),
        )

    def gram(pairs):
        total = [None] * len(pairs)
        for i in range(BE):
            read = {}
            for p in pairs:
                for ref in p:
                    if id(ref) not in read:
                        read[id(ref)] = ref[i * slab : (i + 1) * slab, :]
            for n, (a, b) in enumerate(pairs):
                part = jnp.sum((read[id(a)] * read[id(b)]).reshape(BE, BE, lanes), axis=0)
                total[n] = part if i == 0 else total[n] + part
        return [jnp.sum(t, axis=0, keepdims=True) for t in total]

    def show_obstacle():
        for c in range(4):
            def write(x, plane, c=c):
                obf[c, x] = plane.astype(BF16)

            rows_to_field(
                lambda j, c=c: ob[c, pl.ds(j, slab, stride=BE), :], write, bx_n, bz_n, lane64
            )

    basis = (src, v1, w1, u1, x1)
    known = [(a, b) for a in range(3) for b in range(a, 3)]
    late = [(a, b) for b in (3, 4) for a in range(b + 1)]
    early, ready = [], []

    def ahead():
        ready.extend(sums_of(late[:4]))

    me = mf * nc + mc

    few = everyone <= 64 and nf & (nf - 1) == 0 and nc & (nc - 1) == 0

    def flips(me, count):
        out = []
        for mask in range(count if few else 0):
            to, bit = me, 1
            while bit <= mask:
                if mask & bit:
                    to = to + bit - 2 * bit * lax.rem(me // bit, 2)
                bit *= 2
            out.append(to)
        return out

    flip_fish, flip_curve = flips(mf, nf), flips(mc, nc)
    far_first = sorted(
        ((a, b) for a in range(len(flip_fish)) for b in range(len(flip_curve)) if a or b),
        key=lambda m: -(m[0] // 2 + m[1] % 2 + m[1] // 2),
    )

    def sums_of(pairs):
        return gram([(basis[a], basis[b]) for a, b in pairs])

    def tell(no, lines):
        number = -(-len(lines) // 8) * 8
        lines += [jnp.zeros((1, lanes), F32)] * (number - len(lines))
        tile = jnp.sum(jnp.concatenate(lines, axis=0), axis=1, keepdims=True)
        spot = lax.broadcasted_iota(jnp.int32, (number, lanes), 0) == lax.broadcasted_iota(
            jnp.int32, (number, lanes), 1
        )
        red[no, me] = jnp.sum(jnp.where(spot, tile, 0.0), axis=0, keepdims=True)

        def send(to_fish, to_curve):
            pltpu.make_async_remote_copy(
                src_ref=red.at[no, me],
                dst_ref=red.at[no, me],
                send_sem=rsend_sem.at[no],
                recv_sem=rrecv_sem.at[no],
                device_id=(to_fish, to_curve),
                device_id_type=MESH,
            ).start()

        if few:
            for a, b in far_first:
                send(flip_fish[a], flip_curve[b])
        else:

            def body(k, _):
                send(lax.rem(mf + k // nc, nf), lax.rem(mc + k, nc))
                return 0

            lax.fori_loop(1, everyone, body, 0)

    def hear(no, pairs):
        heard = red.at[no, pl.ds(0, everyone - 1)]
        pltpu.make_async_copy(heard, heard, rrecv_sem.at[no]).wait()
        row = jnp.sum(red[no], axis=0)
        return dict(zip(pairs, entries(row, len(pairs))))

    def show(ref, out):
        def write(x, plane):
            out[x] = plane

        rows_to_field(lambda j: ref[pl.ds(j, slab, stride=BE), :], write, bx_n, bz_n, lane64)

    twice(0, src, y1, v1, m1, w1, show_obstacle)
    twice(1, w1, n1, u1, q1, x1, lambda: early.extend(sums_of(known)), ahead)
    tell(0, early + ready + sums_of(late[4:]))
    for ref, out in (
        (src, rfield), (v1, vfield), (w1, wfield), (u1, ufield), (x1, xfield),
        (y1, yfield), (m1, mfield), (n1, nfield), (q1, qfield),
    ):
        show(ref, out)
    wait_bytes(precv.at[pl.ds(0, nc - 1)], psend_sem)
    for e in range(2):
        wait_group(e, ysend_sem, csend.at[e], yz.at[e], False)
        wait_group(e, gsend_sem, gx.at[e, 0], gz.at[e], False)
    sums = hear(0, known + late)
    scalars = first_scalars(sums)
    resid, press = coefficients(sums, scalars)
    for first, coefs in ((0, resid), (8, press)):
        for k, coef in enumerate(coefs):
            coef_ref[first + k : first + k + 1, :] = jnp.broadcast_to(coef, (1, lanes))
    heard = red.at[0, pl.ds(0, everyone - 1)]
    pltpu.make_async_copy(heard, heard, rsend_sem.at[0]).wait()


def local(right_side, block_inverse, midline, entry_fish, entry_seg, entry_dest, entry_block):
    nf, nc = lax.axis_size("fish"), lax.axis_size("curve")
    count = entry_fish.shape[0]
    cap = max(2, 2 * count // nc)
    cx, cz, ny = right_side.shape
    lanes = (cx // BE) * (cz // BE) * (ny // BE)
    cells = BE**3
    slab = BE * BE
    half = slab // 2
    zrows = BE // (cz // BE) * BE
    span = half + zrows
    wide = 4 * slab
    rows, fishes, npts = midline.shape
    width = fishes * npts
    vmem = pl.BlockSpec(memory_space=pltpu.VMEM)
    big = pltpu.VMEM((cells, lanes), F32)
    dma = pltpu.SemaphoreType.DMA
    anywhere = pl.BlockSpec(memory_space=pl.ANY)
    field = jax.ShapeDtypeStruct((cx, cz, ny), F32)
    fields = jax.ShapeDtypeStruct((4, cx, cz, ny), BF16)
    solved = pl.pallas_call(
        functools.partial(kernel, nf, nc, cap, npts),
        out_shape=(
            (pltpu.VMEM((16, lanes), F32),)
            + (pltpu.VMEM((cx, cz, ny), F32),) * 9
            + (pltpu.VMEM((4, cx, cz, ny), BF16),)
        ),
        in_specs=[anywhere] * 7,
        out_specs=(vmem,) * 11,
        scratch_shapes=[big] * 9
        + [
            pltpu.VMEM((cx, cz, ny), F32),
            pltpu.VMEM((cells, cells), F32),
            pltpu.VMEM((rows, fishes, npts), F32),
            pltpu.VMEM((4, 1, count), jnp.int32),
            dma((4,)),
            pltpu.VMEM((cells, cells), BF16),
            pltpu.VMEM((cells, cells), BF16),
            pltpu.VMEM((cells, wide), BF16),
            pltpu.VMEM((cells, wide), BF16),
            pltpu.VMEM((cells, 2 * lanes), BF16),
            pltpu.VMEM((wide, 2 * lanes), BF16),
            pltpu.VMEM((wide, 4 * lanes), BF16),
            pltpu.VMEM((8, lanes), F32),
            pltpu.VMEM((8, width), F32),
            pltpu.VMEM((SEG * 8, width), F32),
            pltpu.VMEM((nc, cap, lanes), F32),
            pltpu.VMEM((nc, cap, lanes), F32),
            pltpu.VMEM((SEG * 8, lanes), F32),
            pltpu.VMEM((SEG, slab, lanes), F32),
            pltpu.VMEM((4, cells // 2, 2 * lanes), BF16),
            pltpu.VMEM((2 * lanes, 2 * lanes), BF16),
            pltpu.VMEM((4, cells, lanes), F32),
            big,
            pltpu.VMEM((2, 2 * span, lanes), F32),
            pltpu.VMEM((2, 4, 2 * BE, lanes), F32),
            pltpu.VMEM((2, 2, half, lanes), F32),
            pltpu.VMEM((2, 2, zrows, lanes), F32),
            pltpu.VMEM((2, 4, 2 * BE, lanes), F32),
            pltpu.VMEM((2, 2, half, lanes), F32),
            pltpu.VMEM((2, 2, zrows, lanes), F32),
            pltpu.VMEM((2, 2, half, lanes), F32),
            pltpu.VMEM((2, 2, zrows, lanes), F32),
            pltpu.VMEM((1, nf * nc, 1, lanes), F32),
            dma,
            dma((2,)),
            dma((2, 3)),
            dma((2, 3)),
            dma((2, 3)),
            dma((2, 3)),
            dma((1,)),
            dma((1,)),
        ],
        compiler_params=pltpu.CompilerParams(
            collective_id=0, has_side_effects=True, vmem_limit_bytes=VMEM_LIMIT
        ),
    )(
        *(
            pltpu.with_memory_space_constraint(a, pltpu.HBM)
            for a in (
                right_side,
                block_inverse,
                midline,
                *(e.reshape(1, count) for e in (entry_fish, entry_seg, entry_dest, entry_block)),
            )
        )
    )
    return pl.pallas_call(
        finish,
        out_shape=(field, field, fields),
        in_specs=[vmem] * 11,
        out_specs=(anywhere,) * 3,
        scratch_shapes=[
            pltpu.VMEM((cx, cz, ny), F32),
            pltpu.VMEM((cx, cz, ny), F32),
            dma,
            dma((2, 4)),
        ],
        compiler_params=pltpu.CompilerParams(vmem_limit_bytes=VMEM_LIMIT),
    )(*(pltpu.with_memory_space_constraint(a, pltpu.VMEM) for a in solved))


def solution(mesh):
    return jax.shard_map(
        local,
        mesh=mesh,
        in_specs=(
            P("curve", "fish", None),
            P(),
            P(None, "fish", None),
            P(("fish", "curve")),
            P(("fish", "curve")),
            P(("fish", "curve"), None),
            P(("fish", "curve")),
        ),
        out_specs=(
            P("curve", "fish", None),
            P("curve", "fish", None),
            P(None, "curve", "fish", None),
        ),
        check_vma=False,
    )
```
